32 devices in a mesh: rep: 16 (over z, y, x), shard: 2 (over core).
Axes of the slice: x: 2, y: 2, z: 4, core: 2. Of those that a mesh axis runs over, the one named last changes fastest.
Arguments:
- hidden: bfloat16 [16, 1024, 768], P('rep', 'shard'), may hold values from -6 to 6
- latents: bfloat16 [16, 6, 768], P('rep'), may hold values from -6 to 6
- latent_pos: int32 [16, 6], P('rep'), may hold values from 0 to 1023, as said below
- prefix: int32 [16], P('rep'), may hold values from 102 to 512
- ln1_gain: bfloat16 [768], P('shard'), may hold values from 0.099609375 to 1.8984375
- ln1_bias: bfloat16 [768], P('shard'), may hold values from -1.75 to 1.75
- w_qkv: bfloat16 [768, 2304], P('shard'), may hold values from -0.21875 to 0.21875
- b_qv: bfloat16 [1536], P('shard'), may hold values from -1.75 to 1.75
- w_proj: bfloat16 [768, 768], P('shard'), may hold values from -6 to 6
- b_proj: bfloat16 [768], P('shard'), may hold values from -1.75 to 1.75
- ln2_gain: bfloat16 [768], P('shard'), may hold values from 0.099609375 to 1.8984375
- ln2_bias: bfloat16 [768], P('shard'), may hold values from -1.75 to 1.75
- w_fc: bfloat16 [768, 3072], P('shard'), may hold values from -0.21875 to 0.21875
- b_fc: bfloat16 [3072], P('shard'), may hold values from -1.75 to 1.75
- w_out: bfloat16 [3072, 768], P('shard'), may hold values from -0.109375 to 0.109375
- b_out: bfloat16 [768], P('shard'), may hold values from -1.75 to 1.75
- cotangent: bfloat16 [16, 1024, 768], P('rep', 'shard'), may hold values from -6 to 6
Outputs:
- block_out: bfloat16 [16, 1024, 768], P('rep', 'shard')
- grad_hidden: bfloat16 [16, 1024, 768], P('rep', 'shard')
- grad_latents: float32 [16, 6, 768], P('rep')
- grad_ln1_gain: float32 [768], P('shard')
- grad_ln1_bias: float32 [768], P('shard')
- grad_w_qkv: float32 [768, 2304], P('shard')
- grad_b_qv: float32 [1536], P('shard')
- grad_w_proj: float32 [768, 768], P('shard')
- grad_b_proj: float32 [768], P('shard')
- grad_ln2_gain: float32 [768], P('shard')
- grad_ln2_bias: float32 [768], P('shard')
- grad_w_fc: float32 [768, 3072], P('shard')
- grad_b_fc: float32 [3072], P('shard')
- grad_w_out: float32 [3072, 768], P('shard')
- grad_b_out: float32 [768], P('shard')
The draws below stay inside these ranges and needn't reach their ends.
Inputs may be any that keep to these rules, and one draw needn't show every extreme that they name: `latent_pos`: the 6 positions of one sequence are distinct.
All inputs are finite; a program needn't handle non-finite values.
Results may differ from the reference program's by a relative error of at most 0.018.
Values may be sent and summed in bfloat16 or wider, within the bound.
No kernel may reach another device: no remote copies, remote signals or barrier semaphores. Data moves between devices by JAX's collectives and lax.ppermute only.
A program may use at most 256 MiB of HBM per device.

```python
import math
import jax
import jax.numpy as jnp
from jax import lax

D = 768
HEADS = 12
FF = 3072
LENGTH = 1024
LATENTS = 6
BATCH = 16


def draw_latent_pos(key, part):
    key_rows = jax.random.fold_in(key, 11)
    key_first = jax.random.fold_in(key, 12)
    key_second = jax.random.fold_in(key, 13)
    row_keys = jax.random.split(key_rows, BATCH)
    picked = jax.vmap(lambda row_key: jax.random.permutation(row_key, LENGTH - 2)[:LATENTS] + 1)(row_keys)
    first_row = jax.random.randint(key_first, (), 0, BATCH)
    second_row = jax.random.randint(key_second, (), 0, BATCH)
    row_index = jnp.arange(BATCH, dtype=jnp.int32)[:, None]
    column_index = jnp.arange(LATENTS, dtype=jnp.int32)[None, :]
    picked = jnp.where((row_index == first_row) & (column_index == 0), 0, picked)
    picked = jnp.where((row_index == second_row) & (column_index == LATENTS - 1), LENGTH - 1, picked)
    return picked.astype(jnp.int32)


def plant(drawn, own_key, least, largest):
    dims = drawn.shape
    spot = [jax.random.randint(jax.random.fold_in(own_key, axis), (), 0, dims[axis]) for axis in range(len(dims))]
    drawn = drawn.at[tuple(spot)].set(least)
    longest = dims.index(max(dims))
    spot[longest] = (spot[longest] + 1) % dims[longest]
    return drawn.at[tuple(spot)].set(largest)


def block_levels(key, extent, cuts, low, largest):
    loudness = 1.0
    for position, shards_of in cuts:
        heights = jax.random.uniform(jax.random.fold_in(jax.random.fold_in(key, 6), position), (shards_of,), jnp.float32, low / len(cuts), largest / len(cuts))
        loudness = loudness * jnp.repeat(jnp.exp(heights), extent[position] // shards_of).reshape((-1,) + (1,) * (len(extent) - 1 - position))
    return loudness


def bell_draw(key, dims, scale, most, cuts=(), kind=jnp.bfloat16):
    gain = block_levels(key, dims, cuts, -0.22, 0.18) if cuts else 1.0
    entries = jax.random.normal(key, dims, jnp.float32) * scale * gain
    return jnp.minimum(jnp.maximum(entries, -most), most).astype(kind)


def setup_inputs(seed: int = 0) -> dict:
    keys = jax.random.split(jax.random.key(seed), 18)
    return {
        "hidden": bell_draw(keys[0], (BATCH, LENGTH, D), 1.0, 6.0, ((0, 16), (1, 2))),
        "latents": bell_draw(keys[1], (BATCH, LATENTS, D), 1.0, 6.0, ((0, 16),)),
        "latent_pos": draw_latent_pos(jax.random.fold_in(keys[17], 71), 0),
        "prefix": plant(jax.random.randint(keys[3], (BATCH,), LENGTH // 10, LENGTH // 2 + 1), jax.random.fold_in(keys[3], 1), LENGTH // 10, (LENGTH // 2 + 1) - 1).astype(jnp.int32),
        "ln1_gain": jnp.clip(1.0 + 0.18 * jax.random.normal(keys[4], (D,), jnp.float32), 0.099609375, 1.8984375).astype(jnp.bfloat16),
        "ln1_bias": bell_draw(keys[5], (D,), 0.3, 1.75, ((0, 2),)),
        "w_qkv": bell_draw(keys[6], (D, 3 * D), D ** -0.5, 0.21875, ((0, 2),)),
        "b_qv": bell_draw(keys[7], (2 * D,), 0.3, 1.75, ((0, 2),)),
        "w_proj": bell_draw(keys[8], (D, D), (max(1, 2 * D // LENGTH)) ** -0.5, 6.0, ((0, 2),)),
        "b_proj": bell_draw(keys[9], (D,), 0.3, 1.75, ((0, 2),)),
        "ln2_gain": jnp.clip(1.0 + 0.18 * jax.random.normal(keys[10], (D,), jnp.float32), 0.099609375, 1.8984375).astype(jnp.bfloat16),
        "ln2_bias": bell_draw(keys[11], (D,), 0.3, 1.75, ((0, 2),)),
        "w_fc": bell_draw(keys[12], (D, FF), D ** -0.5, 0.21875, ((0, 2),)),
        "b_fc": bell_draw(keys[13], (FF,), 0.3, 1.75, ((0, 2),)),
        "w_out": bell_draw(keys[14], (FF, D), FF ** -0.5, 0.109375, ((0, 2),)),
        "b_out": bell_draw(keys[15], (D,), 0.3, 1.75, ((0, 2),)),
        "cotangent": bell_draw(keys[16], (BATCH, LENGTH, D), 1.0, 6.0, ((0, 16), (1, 2))),
    }


norm_epsilon = 1e-05
gelu_root = 0.7978845608028654
gelu_cubic = 0.044715
masked_score = -1e+30

@jax.custom_vjp
def low(v):
    return lax.optimization_barrier(v.astype(jnp.bfloat16)).astype(jnp.float32)

@jax.custom_vjp
def low_back(v):
    return v

def low_keep(v):
    return (low(v), None)

def low_pass(kept, grad):
    return (grad,)

def back_keep(v):
    return (v, None)

def back_low(kept, grad):
    return (low(grad),)
low.defvjp(low_keep, low_pass)
low_back.defvjp(back_keep, back_low)

def layer_norm(values, norm_gain, norm_shift):
    average = lax.optimization_barrier(jnp.mean(values, axis=-1, keepdims=True))
    centered = values - average
    variance = lax.optimization_barrier(jnp.mean(centered * centered, axis=-1, keepdims=True))
    return centered * lax.rsqrt(variance + norm_epsilon) * norm_gain + norm_shift

def gelu_tanh(values):
    return 0.5 * values * (1.0 + jnp.tanh(gelu_root * (values + gelu_cubic * values * values * values)))

def forward(params, hidden, latents, latent_pos, prefix):
    ln1_gain, ln1_bias, w_qkv, b_qv, w_proj, b_proj, ln2_gain, ln2_bias, w_fc, b_fc, w_out, b_out = params
    group_size, length, model_width = hidden.shape
    head_dim = model_width // HEADS
    maximal_precision = lax.Precision.HIGHEST
    positions = jnp.arange(length, dtype=jnp.int32)
    latent_matches = positions[None, :, None] == latent_pos[:, None, :]
    positioned_rows = jnp.einsum('fqm,fma->fqa', latent_matches.astype(hidden.dtype), latents, precision=maximal_precision)
    replaced = jnp.any(latent_matches, axis=-1)[..., None]
    block_in = jnp.where(replaced, positioned_rows, hidden)
    normed = low(layer_norm(block_in, ln1_gain, ln1_bias))
    zero_bias = jnp.zeros((model_width,), b_qv.dtype)
    bias_full = jnp.concatenate([b_qv[:model_width], zero_bias, b_qv[model_width:]])
    projected = low_back(low(jnp.einsum('gld,de->gle', normed, w_qkv, precision=maximal_precision) + bias_full))
    query_heads = projected[..., :model_width].reshape(group_size, length, HEADS, head_dim)
    key_heads = projected[..., model_width:2 * model_width].reshape(group_size, length, HEADS, head_dim)
    value_heads = projected[..., 2 * model_width:].reshape(group_size, length, HEADS, head_dim)
    score_scale = head_dim ** (-0.5)
    scores = low_back(jnp.einsum('gqhe,gkhe->ghqk', query_heads, key_heads, precision=maximal_precision) * score_scale)
    causal = (positions[None, :] <= positions[:, None])[None, None]
    in_prefix = positions[None, None, None, :] < prefix[:, None, None, None]
    scores = jnp.where(causal | in_prefix, scores, masked_score)
    row_peak = lax.optimization_barrier(jnp.max(scores, axis=-1, keepdims=True))
    weights = jnp.exp(scores - row_peak)
    attn_probs = low(weights / lax.optimization_barrier(jnp.sum(weights, axis=-1, keepdims=True)))
    mixed = jnp.einsum('ghqk,gkhe->gqhe', attn_probs, value_heads, precision=maximal_precision)
    attended = low_back(low(mixed.reshape(group_size, length, model_width)))
    branch = low_back(jnp.einsum('gld,de->gle', attended, w_proj, precision=maximal_precision) + b_proj)
    middle = block_in + branch
    normed_two = low(layer_norm(middle, ln2_gain, ln2_bias))
    pre_act = low_back(jnp.einsum('gld,df->glf', normed_two, w_fc, precision=maximal_precision) + b_fc)
    activated = low(gelu_tanh(pre_act))
    return middle + jnp.einsum('glf,fd->gld', activated, w_out, precision=maximal_precision) + b_out

def reference(hidden, latents, latent_pos, prefix, ln1_gain, ln1_bias, w_qkv, b_qv, w_proj, b_proj, ln2_gain, ln2_bias, w_fc, b_fc, w_out, b_out, cotangent):
    params = (ln1_gain.astype(jnp.float32), ln1_bias.astype(jnp.float32), w_qkv.astype(jnp.float32), b_qv.astype(jnp.float32), w_proj.astype(jnp.float32), b_proj.astype(jnp.float32), ln2_gain.astype(jnp.float32), ln2_bias.astype(jnp.float32), w_fc.astype(jnp.float32), b_fc.astype(jnp.float32), w_out.astype(jnp.float32), b_out.astype(jnp.float32))
    group_size = math.gcd(BATCH, max(1, 4096 // LENGTH))
    group_count = BATCH // group_size

    def by_group(array):
        return array.reshape((group_count, group_size) + array.shape[1:])

    def one_group(totals, pieces):
        hidden_part, latent_part, position_part, prefix_part, cotangent_part = pieces

        def closed(param_in, hidden_in, latent_input):
            return forward(param_in, hidden_in, latent_input, position_part, prefix_part)
        result, back_fn = jax.vjp(closed, params, hidden_part.astype(jnp.float32), latent_part.astype(jnp.float32))
        grad_params, grad_hidden_part, grad_latent_part = back_fn(cotangent_part.astype(jnp.float32))
        totals = jax.tree.map(lambda first, second: first + second, totals, grad_params)
        return (totals, (result.astype(jnp.bfloat16), grad_hidden_part.astype(jnp.bfloat16), grad_latent_part))
    zero_totals = jax.tree.map(jnp.zeros_like, params)
    totals, stacked = lax.scan(one_group, zero_totals, (by_group(hidden), by_group(latents), by_group(latent_pos), by_group(prefix), by_group(cotangent)))
    block_out = stacked[0].reshape(hidden.shape)
    grad_hidden = stacked[1].reshape(hidden.shape)
    grad_latents = stacked[2].reshape(latents.shape)
    g_ln1_gain, g_ln1_bias, g_w_qkv, g_b_qv, g_w_proj, g_b_proj, g_ln2_gain, g_ln2_bias, g_w_fc, g_b_fc, g_w_out, g_b_out = totals
    return (block_out, grad_hidden, grad_latents, g_ln1_gain, g_ln1_bias, g_w_qkv, g_b_qv, g_w_proj, g_b_proj, g_ln2_gain, g_ln2_bias, g_w_fc, g_b_fc, g_w_out, g_b_out)
```

```python
import functools
import jax
import jax.numpy as jnp
from jax import lax
from jax.experimental import pallas as pl
from jax.experimental.pallas import tpu as pltpu
from jax.sharding import PartitionSpec as P

HEADS = 12
F32 = jnp.float32
BF = jnp.bfloat16

norm_epsilon = 1e-05
gelu_root = 0.7978845608028654
gelu_cubic = 0.044715
masked_score = -1e30
LOG2E = 1.4426950408889634


def dot_nt(a, b):
    return lax.dot_general(a, b, (((1,), (1,)), ((), ())), preferred_element_type=F32)


def dot_nn(a, b):
    return lax.dot_general(a, b, (((1,), (0,)), ((), ())), preferred_element_type=F32)


def dot_tn(a, b):
    return lax.dot_general(a, b, (((0,), (0,)), ((), ())), preferred_element_type=F32)


def params(semantics=None):
    return pltpu.CompilerParams(dimension_semantics=semantics, vmem_limit_bytes=60 * 1024 * 1024)


def cost(flops, nbytes, trans=0):
    return pl.CostEstimate(flops=int(flops), bytes_accessed=int(nbytes), transcendentals=int(trans))


def whole(shape):
    return pl.BlockSpec(shape, lambda *_: (0,) * len(shape), pipeline_mode=pl.Buffered(1))


def both(own, oth, shard, a, n):
    o = own[0:1, a : a + n].astype(F32)
    t = oth[0:1, a : a + n].astype(F32)
    first = jnp.where(shard == 0, o, t)
    second = jnp.where(shard == 0, t, o)
    return jnp.concatenate([first, second], axis=1)


def half(i, n):
    return pl.ds(pl.multiple_of(i * n, n), n)


def ln_kv_kernel(scal, hid, lat, pk_own, pk_oth, w_own, w_oth, kv, normed_keep, normed_send, xb, xs, ns, *, L, D):
    r = pl.program_id(0)
    RB = hid.shape[0]
    H = D // 2
    shard = scal[0]
    xs[...] = hid[...].astype(F32)
    row0 = shard * L + r * RB
    for c in range(6):
        rel = scal[2 + c] - row0

        @pl.when((rel >= 0) & (rel < RB))
        def _():
            xs[pl.ds(rel, 1), :] = lat[c : c + 1, :].astype(F32)

    x = xs[...]
    xb[...] = x.astype(BF)
    mean = jnp.mean(x, axis=1, keepdims=True)
    cen = x - mean
    var = jnp.mean(cen * cen, axis=1, keepdims=True)
    g = both(pk_own, pk_oth, shard, 0, H)
    b = both(pk_own, pk_oth, shard, H, H)
    ns[...] = (cen * lax.rsqrt(var + norm_epsilon) * g + b).astype(BF)
    no = ns[:, half(shard, H)]
    nt = ns[:, half(1 - shard, H)]
    normed_keep[...] = no
    normed_send[...] = nt
    vb = jnp.where(shard == 0, pk_oth[0:1, 2 * H : 2 * H + D], pk_own[0:1, 2 * H : 2 * H + D]).astype(F32)
    k = dot_nn(no, w_own[:, 0:D]) + dot_nn(nt, w_oth[:, 0:D])
    kv[:, 0:D] = k.astype(BF)
    v = dot_nn(no, w_own[:, D : 2 * D]) + dot_nn(nt, w_oth[:, D : 2 * D]) + vb
    kv[:, D : 2 * D] = v.astype(BF)


def query_kernel(scal, no, nt, pk_own, pk_oth, w_own, w_oth, q, *, D):
    H = D // 2
    shard = scal[0]
    qb = jnp.where(shard == 0, pk_own[0:1, 2 * H : 2 * H + D], pk_oth[0:1, 2 * H : 2 * H + D]).astype(F32)
    q[...] = (dot_nn(no[...], w_own[...]) + dot_nn(nt[...], w_oth[...]) + qb).astype(BF)


def ln_kv(scal, hid, lat, pk_own, pk_oth, w_own, w_oth):
    L, D = hid.shape
    H = D // 2
    RB = L // 2
    NP = pk_own.shape[1]
    rows = lambda n: pl.BlockSpec((RB, n), lambda r, s: (r, 0))
    wkv = pl.BlockSpec((H, 2 * D), lambda r, s: (0, 0), pipeline_mode=pl.Buffered(1))
    return pl.pallas_call(
        functools.partial(ln_kv_kernel, L=L, D=D),
        out_shape=(
            jax.ShapeDtypeStruct((L, 2 * D), BF),
            jax.ShapeDtypeStruct((L, H), BF),
            jax.ShapeDtypeStruct((L, H), BF),
            jax.ShapeDtypeStruct((L, D), BF),
        ),
        grid_spec=pltpu.PrefetchScalarGridSpec(
            num_scalar_prefetch=1,
            grid=(2,),
            in_specs=[rows(D), whole(lat.shape), whole((1, NP)), whole((1, NP)), wkv, wkv],
            out_specs=[rows(2 * D), rows(H), rows(H), rows(D)],
            scratch_shapes=[pltpu.VMEM((RB, D), F32), pltpu.VMEM((RB, D), BF)],
        ),
        compiler_params=params(("arbitrary",)),
        cost_estimate=cost(2 * L * D * 2 * D, 7e6),
        name="ln_kv",
    )(scal, hid, lat, pk_own, pk_oth, w_own, w_oth)


def query(scal, no, nt, pk_own, pk_oth, w_own, w_oth):
    L, H = no.shape
    D = 2 * H
    NP = pk_own.shape[1]
    RB = L // 2
    rows = lambda n: pl.BlockSpec((RB, n), lambda r, s: (r, 0))
    wq = pl.BlockSpec((H, D), lambda r, s: (0, 0), pipeline_mode=pl.Buffered(1))
    return pl.pallas_call(
        functools.partial(query_kernel, D=D),
        out_shape=jax.ShapeDtypeStruct((L, D), BF),
        grid_spec=pltpu.PrefetchScalarGridSpec(
            num_scalar_prefetch=1,
            grid=(2,),
            in_specs=[rows(H), rows(H), whole((1, NP)), whole((1, NP)), wq, wq],
            out_specs=rows(D),
        ),
        compiler_params=params(("arbitrary",)),
        cost_estimate=cost(2 * L * D * D, 3e6),
        name="query",
    )(scal, no, nt, pk_own, pk_oth, w_own, w_oth)


def attn_fwd_kernel(scal, q_ref, k_own, v_own, k_oth, v_oth, o_ref, lse_ref, stat, *, L, RB):
    p_id = pl.program_id(0)
    shard = scal[0]
    pfx = scal[1]
    lane = lax.broadcasted_iota(jnp.int32, (RB, 128), 1)
    c = 0.125 * LOG2E
    NB = L // RB

    def run(first):
        for r in range(NB):
            q = q_ref[r * RB : (r + 1) * RB, :]
            outs = []
            for hh in range(2):
                sel = (lane < 64) if hh == 0 else (lane >= 64)
                qm = jnp.where(sel, q, jnp.zeros_like(q))
                pieces = []
                if not first:
                    pieces.append((dot_nt(qm, k_oth[...]) * c, v_oth[...]))
                for kb in range(NB if first else r + 1):
                    s = dot_nt(qm, k_own[kb * RB : (kb + 1) * RB, :]) * c
                    if kb >= r:
                        col = lax.broadcasted_iota(jnp.int32, (RB, RB), 1) + kb * RB
                        row = lax.broadcasted_iota(jnp.int32, (RB, RB), 0) + r * RB
                        keep = (col <= row) | (col < pfx) if first else (col <= row)
                        s = jnp.where(keep, s, masked_score)
                    pieces.append((s, v_own[kb * RB : (kb + 1) * RB, :]))
                m = functools.reduce(jnp.maximum, [jnp.max(s, axis=1, keepdims=True) for s, _ in pieces])
                total = jnp.zeros((RB, 1), F32)
                o = jnp.zeros((RB, 128), F32)
                for s, v in pieces:
                    p = jnp.exp2(s - m)
                    total = total + jnp.sum(p, axis=1, keepdims=True)
                    o = o + dot_nn(p.astype(BF), v)
                outs.append(o * (1.0 / total))
                lse = m + jnp.log2(total)
                here = lane == p_id * 2 + hh
                stat[r * RB : (r + 1) * RB, :] = jnp.where(here, lse, stat[r * RB : (r + 1) * RB, :])
            o_ref[r * RB : (r + 1) * RB, :] = jnp.where(lane < 64, outs[0], outs[1]).astype(BF)

    @pl.when(shard == 0)
    def _():
        run(True)

    @pl.when(shard != 0)
    def _():
        run(False)

    @pl.when(p_id == pl.num_programs(0) - 1)
    def _():
        lse_ref[...] = stat[...].T[0:16, :]


def attn_fwd(scal, q, kv_own, kv_oth):
    L, D = q.shape
    NP = D // 128
    spec = lambda off: pl.BlockSpec((L, 128), lambda p, s: (0, p + off))
    return pl.pallas_call(
        functools.partial(attn_fwd_kernel, L=L, RB=256),
        out_shape=(jax.ShapeDtypeStruct((L, D), BF), jax.ShapeDtypeStruct((16, L), F32)),
        grid_spec=pltpu.PrefetchScalarGridSpec(
            num_scalar_prefetch=1,
            grid=(NP,),
            in_specs=[spec(0), spec(0), spec(NP), spec(0), spec(NP)],
            out_specs=[spec(0), pl.BlockSpec((16, L), lambda p, s: (0, 0))],
            scratch_shapes=[pltpu.VMEM((L, 128), F32)],
        ),
        compiler_params=params(("arbitrary",)),
        cost_estimate=cost(12e9, 6e6, 6e6),
        name="attn_fwd",
    )(scal, q, kv_own, kv_own, kv_oth, kv_oth)


def attn_bwd_kernel(
    scal, q_ref, k_own, v_own, k_oth, v_oth, do_ref, lse_ref, dl_ref,
    dq_ref, dk_own, dv_own, dk_oth, dv_oth, dqt, *, L, KB, p0,
):
    shard = scal[0]
    pfx = scal[1]
    lane = lax.broadcasted_iota(jnp.int32, (L, 128), 1)
    c = 0.125 * LOG2E
    NB = L // KB
    q = q_ref[...]
    do = do_ref[...]
    z = jnp.zeros_like(q)
    qm = [jnp.where(lane < 64, q, z), jnp.where(lane >= 64, q, z)]
    dm = [jnp.where(lane < 64, do, z), jnp.where(lane >= 64, do, z)]
    hb = (pl.program_id(0) + p0) * 2
    lse = [lse_ref[pl.ds(hb + hh, 1), :] for hh in range(2)]
    dl = [dl_ref[pl.ds(hb + hh, 1), :] for hh in range(2)]
    dqt[...] = jnp.zeros_like(dqt)

    def block(k, v, q0, mask):
        kt = k.T
        dk = None
        dv = None
        for hh in range(2):
            st = dot_nt(k, qm[hh][q0:, :]) * c
            if mask is not None:
                st = jnp.where(mask, st, masked_score)
            pt = jnp.exp2(st - lse[hh][:, q0:])
            dpt = dot_nt(v, dm[hh][q0:, :])
            dst = (pt * (dpt - dl[hh][:, q0:])).astype(BF)
            a = dot_nn(pt.astype(BF), dm[hh][q0:, :])
            b = dot_nn(dst, qm[hh][q0:, :])
            dv = a if dv is None else dv + a
            dk = b if dk is None else dk + b
            dqt[hh * 64 : (hh + 1) * 64, q0:] += dot_nn(kt[hh * 64 : (hh + 1) * 64, :], dst)
        return (dk * 0.125).astype(BF), dv.astype(BF)

    @pl.when(shard == 0)
    def _():
        for kb in range(NB):
            rows = slice(kb * KB, (kb + 1) * KB)
            key = lax.broadcasted_iota(jnp.int32, (KB, L), 0) + kb * KB
            qry = lax.broadcasted_iota(jnp.int32, (KB, L), 1)
            dk, dv = block(k_own[rows, :], v_own[rows, :], 0, (key <= qry) | (key < pfx))
            dk_own[rows, :] = dk
            dv_own[rows, :] = dv
        dk_oth[...] = jnp.zeros_like(dk_oth)
        dv_oth[...] = jnp.zeros_like(dv_oth)

    @pl.when(shard != 0)
    def _():
        for kb in range(NB):
            rows = slice(kb * KB, (kb + 1) * KB)
            dk, dv = block(k_oth[rows, :], v_oth[rows, :], 0, None)
            dk_oth[rows, :] = dk
            dv_oth[rows, :] = dv
        for kb in range(NB):
            q0 = kb * KB
            rows = slice(kb * KB, (kb + 1) * KB)
            key = lax.broadcasted_iota(jnp.int32, (KB, L - q0), 0)
            qry = lax.broadcasted_iota(jnp.int32, (KB, L - q0), 1)
            dk, dv = block(k_own[rows, :], v_own[rows, :], q0, key <= qry)
            dk_own[rows, :] = dk
            dv_own[rows, :] = dv

    dq_ref[...] = (dqt[...].T * 0.125).astype(BF)


def attn_bwd(scal, q, kv_own, kv_oth, do, lse, dl, p0, count):
    L, D = q.shape
    NP = D // 128
    ispec = lambda off: pl.BlockSpec((L, 128), lambda p, s: (0, p + off))
    full = pl.BlockSpec((16, L), lambda p, s: (0, 0))
    o = jax.ShapeDtypeStruct((L, count * 128), BF)
    share = count / NP
    return pl.pallas_call(
        functools.partial(attn_bwd_kernel, L=L, KB=256, p0=p0),
        out_shape=(o,) * 5,
        grid_spec=pltpu.PrefetchScalarGridSpec(
            num_scalar_prefetch=1,
            grid=(count,),
            in_specs=[ispec(p0), ispec(p0), ispec(NP + p0), ispec(p0), ispec(NP + p0), ispec(p0), full, full],
            out_specs=[ispec(0)] * 5,
            scratch_shapes=[pltpu.VMEM((128, L), F32)],
        ),
        compiler_params=params(("arbitrary",)),
        cost_estimate=cost(20e9 * share, 8e6 * share, 6e6 * share),
        name="attn_bwd",
    )(scal, q, kv_own, kv_own, kv_oth, kv_oth, do, lse, dl)


def mid_kernel(
    scal, att, xb, dz, pk_own, pk_oth, wp_own, wp_oth, wf_own, wf_oth, wo_own, wo_oth,
    mid, n2_keep, n2_send, act_keep, act_send, gp, as_, ns, *, T,
):
    shard = scal[0]
    D = xb.shape[1]
    H = D // 2
    FH = wo_own.shape[0]
    o_bp, o_g2, o_b2, o_bf = 2 * H + D, 3 * H + D, 4 * H + D, 5 * H + D
    as_[...] = att[...]
    m = dot_nn(as_[:, half(shard, H)], wp_own[...]) + dot_nn(as_[:, half(1 - shard, H)], wp_oth[...])
    m = m + xb[...].astype(F32) + both(pk_own, pk_oth, shard, o_bp, H)
    mid[...] = m
    mean = jnp.mean(m, axis=1, keepdims=True)
    cen = m - mean
    var = jnp.mean(cen * cen, axis=1, keepdims=True)
    g = both(pk_own, pk_oth, shard, o_g2, H)
    b = both(pk_own, pk_oth, shard, o_b2, H)
    ns[...] = (cen * lax.rsqrt(var + norm_epsilon) * g + b).astype(BF)
    no = ns[:, half(shard, H)]
    nt = ns[:, half(1 - shard, H)]
    n2_keep[...] = no
    n2_send[...] = nt
    d = dz[...]
    for side in range(2):
        owner = shard if side == 0 else 1 - shard
        wo = wo_own if side == 0 else wo_oth
        pk = pk_own if side == 0 else pk_oth
        act = act_keep if side == 0 else act_send
        for t in range(FH // T):
            cols = pl.ds(pl.multiple_of(owner * FH + t * T, T), T)
            u = dot_nn(no, wf_own[:, cols]) + dot_nn(nt, wf_oth[:, cols])
            u = u + pk[0:1, o_bf + t * T : o_bf + (t + 1) * T].astype(F32)
            ga = dot_nt(d, wo[t * T : (t + 1) * T, :])
            u2 = u * u
            th = jnp.tanh(u * (gelu_root + (gelu_root * gelu_cubic) * u2))
            hp = 0.5 + 0.5 * th
            act[:, t * T : (t + 1) * T] = (u * hp).astype(BF)
            slope = hp + (u * hp) * ((1.0 - th) * (gelu_root + (3.0 * gelu_root * gelu_cubic) * u2))
            gp[:, cols] = (ga * slope).astype(BF)


def mid_block(scal, att, xb, dz, pk_own, pk_oth, wp_own, wp_oth, wf_own, wf_oth, wo_own, wo_oth):
    L, D = xb.shape
    H = D // 2
    FH = wo_own.shape[0]
    RB = L // 2
    NP = pk_own.shape[1]
    rows = lambda n: pl.BlockSpec((RB, n), lambda r, s: (r, 0))
    sds = jax.ShapeDtypeStruct
    return pl.pallas_call(
        functools.partial(mid_kernel, T=512),
        out_shape=(sds((L, D), F32), sds((L, H), BF), sds((L, H), BF), sds((L, FH), BF), sds((L, FH), BF), sds((L, 2 * FH), BF)),
        grid_spec=pltpu.PrefetchScalarGridSpec(
            num_scalar_prefetch=1,
            grid=(L // RB,),
            in_specs=[rows(D), rows(D), rows(D), whole((1, NP)), whole((1, NP)), whole((H, D)), whole((H, D)),
                      whole((H, 2 * FH)), whole((H, 2 * FH)), whole((FH, D)), whole((FH, D))],
            out_specs=[rows(D), rows(H), rows(H), rows(FH), rows(FH), rows(2 * FH)],
            scratch_shapes=[pltpu.VMEM((RB, D), BF), pltpu.VMEM((RB, D), BF)],
        ),
        compiler_params=params(("arbitrary",)),
        cost_estimate=cost(2 * L * D * (D + 4 * FH), 24e6, 1.5e6),
        name="mid_block",
    )(scal, att, xb, dz, pk_own, pk_oth, wp_own, wp_oth, wf_own, wf_oth, wo_own, wo_oth)


def out_kernel(scal, mid, act_keep, act_send, pk_own, pk_oth, wo_own, wo_oth, out):
    shard = scal[0]
    D = mid.shape[1]
    H = D // 2
    FH = wo_own.shape[0]
    o_bo = 5 * H + D + FH
    y = dot_nn(act_keep[...], wo_own[...]) + dot_nn(act_send[...], wo_oth[...])
    out[...] = (y + mid[...] + both(pk_own, pk_oth, shard, o_bo, H)).astype(BF)


def out_block(scal, mid, act_keep, act_send, pk_own, pk_oth, wo_own, wo_oth):
    L, D = mid.shape
    FH = wo_own.shape[0]
    RB = L // 2
    NP = pk_own.shape[1]
    rows = lambda n: pl.BlockSpec((RB, n), lambda r, s: (r, 0))
    return pl.pallas_call(
        out_kernel,
        out_shape=jax.ShapeDtypeStruct((L, D), BF),
        grid_spec=pltpu.PrefetchScalarGridSpec(
            num_scalar_prefetch=1,
            grid=(L // RB,),
            in_specs=[rows(D), rows(FH), rows(FH), whole((1, NP)), whole((1, NP)), whole((FH, D)), whole((FH, D))],
            out_specs=rows(D),
        ),
        compiler_params=params(("arbitrary",)),
        cost_estimate=cost(4 * L * D * FH, 10e6),
        name="out_block",
    )(scal, mid, act_keep, act_send, pk_own, pk_oth, wo_own, wo_oth)


def back_kernel(
    scal, gp, mid, dz, att, pk_own, pk_oth, wf_own, wf_oth, wp_own, wp_oth,
    dmid, gb, ga, delta, sums, es, gs,
):
    r_id = pl.program_id(0)
    shard = scal[0]
    RB, D = mid.shape
    H = D // 2
    o_g2 = 3 * H + D
    gpv = gp[...]
    es[:, half(shard, H)] = dot_nt(gpv, wf_own[...])
    es[:, half(1 - shard, H)] = dot_nt(gpv, wf_oth[...])
    gn = es[...]
    m = mid[...]
    cen = m - jnp.mean(m, axis=1, keepdims=True)
    r = lax.rsqrt(jnp.mean(cen * cen, axis=1, keepdims=True) + norm_epsilon)
    n = cen * r
    e = gn * both(pk_own, pk_oth, shard, o_g2, H)
    dzv = dz[...].astype(F32)
    g = dzv + r * (e - jnp.mean(e, axis=1, keepdims=True) - n * jnp.mean(e * n, axis=1, keepdims=True))
    dmid[...] = g
    gbv = g.astype(BF)
    gb[...] = gbv
    gs[:, half(shard, H)] = dot_nt(gbv, wp_own[...]).astype(BF)
    gs[:, half(1 - shard, H)] = dot_nt(gbv, wp_oth[...]).astype(BF)
    gav = gs[...]
    ga[...] = gav
    prod = gav.astype(F32) * att[...].astype(F32)
    hi = prod.astype(BF)
    lo = (prod - hi.astype(F32)).astype(BF)
    head = lax.broadcasted_iota(jnp.int32, (16, D), 0)
    lane = lax.broadcasted_iota(jnp.int32, (16, D), 1)
    pick = jnp.where((lane >= head * 64) & (lane < head * 64 + 64), 1.0, 0.0).astype(BF)
    delta[...] = dot_nt(pick, hi) + dot_nt(pick, lo)

    @pl.when(r_id == 0)
    def _():
        sums[...] = jnp.zeros_like(sums)

    sums[0:1, :] += jnp.sum(gpv.astype(F32), axis=0, keepdims=True)
    sums[1:2, 0:D] += jnp.sum(gn * n, axis=0, keepdims=True)
    sums[2:3, 0:D] += jnp.sum(gn, axis=0, keepdims=True)
    sums[3:4, 0:D] += jnp.sum(gbv.astype(F32), axis=0, keepdims=True)
    sums[4:5, 0:D] += jnp.sum(dzv, axis=0, keepdims=True)


def back_block(scal, gp, mid, dz, att, pk_own, pk_oth, wf_own, wf_oth, wp_own, wp_oth):
    L, D = mid.shape
    H = D // 2
    FF = gp.shape[1]
    RB = L // 2
    NP = pk_own.shape[1]
    rows = lambda n: pl.BlockSpec((RB, n), lambda r, s: (r, 0))
    sds = jax.ShapeDtypeStruct
    return pl.pallas_call(
        back_kernel,
        out_shape=(sds((L, D), F32), sds((L, D), BF), sds((L, D), BF), sds((16, L), F32), sds((8, FF), F32)),
        grid_spec=pltpu.PrefetchScalarGridSpec(
            num_scalar_prefetch=1,
            grid=(L // RB,),
            in_specs=[rows(FF), rows(D), rows(D), rows(D), whole((1, NP)), whole((1, NP)),
                      whole((H, FF)), whole((H, FF)), whole((H, D)), whole((H, D))],
            out_specs=[rows(D), rows(D), rows(D), pl.BlockSpec((16, RB), lambda r, s: (0, r)), pl.BlockSpec((8, FF), lambda r, s: (0, 0))],
            scratch_shapes=[pltpu.VMEM((RB, D), F32), pltpu.VMEM((RB, D), BF)],
        ),
        compiler_params=params(("arbitrary",)),
        cost_estimate=cost(2 * L * D * (D + FF), 18e6),
        name="back_block",
    )(scal, gp, mid, dz, att, pk_own, pk_oth, wf_own, wf_oth, wp_own, wp_oth)


def put_piece(value, pos, rows, send, keep, cols):
    at = pl.ds(pl.multiple_of((pos & 3) * rows, 16), rows)

    @pl.when(pos >= 4)
    def _():
        send[at, cols] = value

    @pl.when(pos < 4)
    def _():
        keep[at, cols] = value


def grad_rows_kernel(scal, a_own, a_oth, b_own, b_oth, send, keep, acc, *, R):
    i = pl.program_id(0)
    code = scal[8]
    acc[...] = (dot_tn(a_own[...], b_own[...]) + dot_tn(a_oth[...], b_oth[...])).astype(BF)
    per = acc.shape[0] // R
    for u in range(per):
        put_piece(acc[u * R : (u + 1) * R, :], (i * per + u) ^ code, R, send, keep, slice(None))


def grad_rows(scal, a_own, a_oth, b_own, b_oth, T):
    K, M = a_own.shape
    N = b_own.shape[1]
    cols = pl.BlockSpec((K, T), lambda i, s: (0, i))
    o = jax.ShapeDtypeStruct((M // 2, N), BF)
    return pl.pallas_call(
        functools.partial(grad_rows_kernel, R=M // 8),
        out_shape=(o, o),
        grid_spec=pltpu.PrefetchScalarGridSpec(
            num_scalar_prefetch=1,
            grid=(M // T,),
            in_specs=[cols, cols, whole((K, N)), whole((K, N))],
            out_specs=[pl.BlockSpec((M // 2, N), lambda i, s: (0, 0))] * 2,
            scratch_shapes=[pltpu.VMEM((T, N), BF)],
        ),
        compiler_params=params(("arbitrary",)),
        cost_estimate=cost(4 * K * M * N, 4 * K * (M + N) + 2 * M * N),
        name="grad_rows",
    )(scal, a_own, a_oth, b_own, b_oth)


def grad_cols_kernel(scal, a_own, a_oth, b_own, b_oth, send, keep, acc, *, R):
    code = scal[8]
    acc[...] = (dot_tn(a_own[...], b_own[...]) + dot_tn(a_oth[...], b_oth[...])).astype(BF)
    for u in range(8):
        put_piece(acc[u * R : (u + 1) * R, :], u ^ code, R, send, keep, slice(None))


def grad_cols(scal, a_own, a_oth, b_own, b_oth, T):
    K, M = a_own.shape
    N = b_own.shape[1]
    cols = pl.BlockSpec((K, T), lambda i, s: (0, i))
    o = jax.ShapeDtypeStruct((M // 2, N), BF)
    return pl.pallas_call(
        functools.partial(grad_cols_kernel, R=M // 8),
        out_shape=(o, o),
        grid_spec=pltpu.PrefetchScalarGridSpec(
            num_scalar_prefetch=1,
            grid=(N // T,),
            in_specs=[whole((K, M)), whole((K, M)), cols, cols],
            out_specs=[pl.BlockSpec((M // 2, T), lambda i, s: (0, i))] * 2,
            scratch_shapes=[pltpu.VMEM((M, T), BF)],
        ),
        compiler_params=params(("arbitrary",)),
        cost_estimate=cost(4 * K * M * N, 4 * K * (M + N) + 2 * M * N),
        name="grad_cols",
    )(scal, a_own, a_oth, b_own, b_oth)


def grad_qkv_kernel(scal, a_own, a_oth, q_own, q_oth, k_own, k_oth, rk_own, rk_oth, v_own, v_oth, rv_own, rv_oth, send, keep, acc, *, R):
    code = scal[8]
    N = q_own.shape[1]
    ao = a_own[...]
    at = a_oth[...]

    def total(a, b):
        return (a[...].astype(F32) + b[...].astype(F32)).astype(BF)

    acc[:, 0:N] = (dot_tn(ao, q_own[...]) + dot_tn(at, q_oth[...])).astype(BF)
    acc[:, N : 2 * N] = (dot_tn(ao, total(k_own, rk_oth)) + dot_tn(at, total(rk_own, k_oth))).astype(BF)
    acc[:, 2 * N : 3 * N] = (dot_tn(ao, total(v_own, rv_oth)) + dot_tn(at, total(rv_own, v_oth))).astype(BF)
    for u in range(8):
        put_piece(acc[u * R : (u + 1) * R, :], u ^ code, R, send, keep, slice(None))


def grad_qkv(scal, a_own, a_oth, parts):
    K, M = a_own.shape
    N = parts[0].shape[1]
    o = jax.ShapeDtypeStruct((M // 2, 3 * N), BF)
    return pl.pallas_call(
        functools.partial(grad_qkv_kernel, R=M // 8),
        out_shape=(o, o),
        grid_spec=pltpu.PrefetchScalarGridSpec(
            num_scalar_prefetch=1,
            grid=(1,),
            in_specs=[whole((K, M))] * 2 + [whole((K, N))] * 10,
            out_specs=[whole((M // 2, 3 * N))] * 2,
            scratch_shapes=[pltpu.VMEM((M, 3 * N), BF)],
        ),
        compiler_params=params(("arbitrary",)),
        cost_estimate=cost(12 * K * M * N, 2 * K * (2 * M + 10 * N) + 6 * M * N),
        name="grad_qkv",
    )(scal, a_own, a_oth, *parts)


def last_kernel(
    scal, q1, q2, k1, k2, rk1, rk2, v1, v2, rv1, rv2, xb, dmid, pk_own, pk_oth, w_own, w_oth, sums,
    gh, glat, s_keep, s_send, gi, es, vec, *, L,
):
    r_id = pl.program_id(0)
    shard = scal[0]
    RB, D = xb.shape
    H = D // 2
    G = q1.shape[1]
    FF = sums.shape[1]

    def total(a, b):
        return (a[...].astype(F32) + b[...].astype(F32)).astype(BF)

    gp = [q1[...], q2[...], total(k1, rk1), total(k2, rk2), total(v1, rv1), total(v2, rv2)]
    for side in range(2):
        w = w_own if side == 0 else w_oth
        owner = shard if side == 0 else 1 - shard
        es[:, half(owner, H)] = functools.reduce(
            lambda a, b: a + b, [dot_nt(gp[j], w[:, j * G : (j + 1) * G]) for j in range(6)]
        )
    gn = es[...]
    x = xb[...].astype(F32)
    cen = x - jnp.mean(x, axis=1, keepdims=True)
    r = lax.rsqrt(jnp.mean(cen * cen, axis=1, keepdims=True) + norm_epsilon)
    n = cen * r
    e = gn * both(pk_own, pk_oth, shard, 0, H)
    gi[...] = dmid[...] + r * (e - jnp.mean(e, axis=1, keepdims=True) - n * jnp.mean(e * n, axis=1, keepdims=True))

    @pl.when(r_id == 0)
    def _():
        glat[...] = jnp.zeros_like(glat)
        vec[...] = jnp.zeros_like(vec)

    row0 = shard * L + r_id * RB
    for c in range(6):
        rel = scal[2 + c] - row0

        @pl.when((rel >= 0) & (rel < RB))
        def _():
            glat[c : c + 1, :] = gi[pl.ds(rel, 1), :]
            gi[pl.ds(rel, 1), :] = jnp.zeros((1, D), F32)

    gh[...] = gi[...].astype(BF)
    vec[0:1, 0:D] += jnp.sum(gn * n, axis=0, keepdims=True)
    vec[1:2, 0:D] += jnp.sum(gn, axis=0, keepdims=True)
    for j, src in enumerate((0, 1, 4, 5)):
        vec[2:3, j * G : (j + 1) * G] += jnp.sum(gp[src].astype(F32), axis=0, keepdims=True)

    @pl.when(r_id == pl.num_programs(0) - 1)
    def _():
        for side in range(2):
            owner = shard if side == 0 else 1 - shard
            out = s_keep if side == 0 else s_send
            one = half(owner, H)
            wide = vec[2:3, half(owner, D)]
            fc = sums[0:1, half(owner, FF // 2)]
            flat = jnp.concatenate(
                [vec[0:1, one], vec[1:2, one], wide, sums[3:4, one], sums[1:2, one], sums[2:3, one], fc, sums[4:5, one]], axis=1
            )
            W = out.shape[1]
            out[...] = jnp.zeros_like(out)
            for k in range(flat.shape[1] // W):
                out[k : k + 1, :] = flat[:, k * W : (k + 1) * W]


def last_block(scal, grads, xb, dmid, pk_own, pk_oth, w_own, w_oth, sums, width):
    L, D = xb.shape
    H = D // 2
    G = grads[0].shape[1]
    FF = sums.shape[1]
    RB = L // 2
    NP = pk_own.shape[1]
    rows = lambda n: pl.BlockSpec((RB, n), lambda r, s: (r, 0))
    const = lambda shape: pl.BlockSpec(shape, lambda r, s: (0, 0))
    sds = jax.ShapeDtypeStruct
    return pl.pallas_call(
        functools.partial(last_kernel, L=L),
        out_shape=(sds((L, D), BF), sds((8, D), F32), sds((16, width), F32), sds((16, width), F32)),
        grid_spec=pltpu.PrefetchScalarGridSpec(
            num_scalar_prefetch=1,
            grid=(L // RB,),
            in_specs=[rows(G)] * 10 + [rows(D), rows(D), whole((1, NP)), whole((1, NP)), whole((H, 3 * D)), whole((H, 3 * D)), whole(sums.shape)],
            out_specs=[rows(D), const((8, D)), const((16, width)), const((16, width))],
            scratch_shapes=[pltpu.VMEM((RB, D), F32), pltpu.VMEM((RB, D), F32), pltpu.VMEM((8, 2 * D), F32)],
        ),
        compiler_params=params(("arbitrary",)),
        cost_estimate=cost(6 * L * D * D, 12e6),
        name="last_block",
    )(scal, *grads, xb, dmid, pk_own, pk_oth, w_own, w_oth, sums)


def add_split_kernel(a, b, send, keep):
    n = keep.shape[0]
    keep[...] = (a[0:n, :].astype(F32) + b[0:n, :].astype(F32)).astype(BF)
    send[...] = (a[n : 2 * n, :].astype(F32) + b[n : 2 * n, :].astype(F32)).astype(BF)


def add_split(a, b):
    M, N = a.shape
    o = jax.ShapeDtypeStruct((M // 2, N), BF)
    return pl.pallas_call(
        add_split_kernel,
        out_shape=(o, o),
        compiler_params=params(),
        cost_estimate=cost(M * N, 6 * M * N),
        name="add_split",
    )(a, b)


def final_kernel(scal, g, r, out):
    p = pl.program_id(0)
    pos = p ^ scal[8]

    @pl.when(pos < 4)
    def _():
        out[...] = g[...].astype(F32)

    @pl.when(pos >= 4)
    def _():
        out[...] = r[...].astype(F32)


def final(scal, g, r):
    M, N = g.shape
    R = M // 4
    src = pl.BlockSpec((R, N), lambda p, s: ((p ^ s[8]) & 3, 0))
    return pl.pallas_call(
        final_kernel,
        out_shape=jax.ShapeDtypeStruct((2 * M, N), F32),
        grid_spec=pltpu.PrefetchScalarGridSpec(
            num_scalar_prefetch=1,
            grid=(8,),
            in_specs=[src, src],
            out_specs=pl.BlockSpec((R, N), lambda p, s: (p, 0)),
        ),
        compiler_params=params(("arbitrary",)),
        cost_estimate=cost(M * N, 12 * M * N),
        name="final",
    )(scal, g, r)


def swap(x):
    return lax.ppermute(x, "shard", [(0, 1), (1, 0)])


def hop(x, first, second):
    pairs = []
    for rep in range(16):
        pairs.append((2 * rep, 2 * (rep ^ first)))
        pairs.append((2 * rep + 1, 2 * (rep ^ second) + 1))
    return lax.ppermute(x, ("rep", "shard"), pairs)


def add16(a, b):
    return (a.astype(F32) + b.astype(F32)).astype(BF)


class Reduce:
    def __init__(self, send, keep):
        self.send = send
        self.keep = keep

    def hop1(self):
        self.recv = hop(self.send, 1, 2)

    def hop2(self):
        send, self.keep = add_split(self.keep, self.recv)
        self.recv = hop(send, 4, 4)

    def hop3(self):
        send, self.keep = add_split(self.keep, self.recv)
        self.recv = hop(send, 2, 1)

    def hop4(self):
        self.keep = add16(self.keep, self.recv)
        self.recv = hop(self.keep, 8, 8)

    def hop5(self):
        self.keep = add16(self.keep, self.recv)
        self.recv = hop(self.keep, 2, 1)

    def hop6(self):
        self.keep = jnp.concatenate([self.keep, self.recv], axis=0)
        self.recv = hop(self.keep, 4, 4)

    def hop7(self):
        self.keep = jnp.concatenate([self.keep, self.recv], axis=0)
        self.recv = hop(self.keep, 1, 2)

    def done(self, scal):
        return final(scal, self.keep, self.recv)


class ReduceWith(Reduce):
    def hop4(self, small):
        self.n = self.keep.shape[0]
        self.keep = jnp.concatenate([add16(self.keep, self.recv), small], axis=0)
        self.recv = hop(self.keep, 8, 8)

    def hop5(self):
        self.keep = add16(self.keep, self.recv)
        self.recv = hop(self.keep, 2, 1)

    def hop6(self):
        n = self.n
        small = add16(self.keep[n:], self.recv[n:])
        self.keep = jnp.concatenate([self.keep[:n], self.recv[:n], small], axis=0)
        self.recv = hop(self.keep, 4, 4)

    def hop7(self):
        n = 2 * self.n
        small = add16(self.keep[n:], self.recv[n:])
        self.keep = jnp.concatenate([self.keep[:n], self.recv[:n], small], axis=0)
        self.recv = hop(self.keep, 1, 2)

    def done(self, scal):
        n = 4 * self.n
        small = self.keep[n:].astype(F32) + self.recv[n:].astype(F32)
        return final(scal, self.keep[:n], self.recv[:n]), small


def pair_device(
    hidden, latents, latent_pos, prefix, ln1_gain, ln1_bias, w_qkv, b_qv, w_proj, b_proj,
    ln2_gain, ln2_bias, w_fc, b_fc, w_out, b_out, cotangent,
):
    _, L, D = hidden.shape
    H = D // 2
    shard = lax.axis_index("shard").astype(jnp.int32)
    rep = lax.axis_index("rep").astype(jnp.int32)
    bit0, bit1, bit2 = rep & 1, (rep >> 1) & 1, (rep >> 2) & 1
    high = jnp.where(shard == 0, bit0, bit1)
    low = jnp.where(shard == 0, bit1, bit0)
    code = high * 4 + bit2 * 2 + low
    lead = lax.broadcasted_iota(jnp.int32, (16,), 0)
    scal = jnp.where(lead == 0, shard, jnp.where(lead == 1, prefix[0] - 0, jnp.where(lead == 8, code, 0)))
    scal = lax.dynamic_update_slice(scal, latent_pos[0].astype(jnp.int32), (2,))

    pk_own = jnp.concatenate([ln1_gain, ln1_bias, b_qv, b_proj, ln2_gain, ln2_bias, b_fc, b_out])[None, :]
    pk_oth = swap(pk_own)
    qkv_oth = swap(w_qkv)
    proj_oth = swap(w_proj)
    fc_oth = swap(w_fc)
    out_oth = swap(w_out)
    hid = hidden[0]
    dz = cotangent[0]
    lat = latents[0]

    kvw_own = w_qkv[:, D:]
    kvw_oth = qkv_oth[:, D:]
    qw_own = w_qkv[:, :D]
    qw_oth = qkv_oth[:, :D]
    kv_own, nrm_keep, nrm_send, xb = ln_kv(scal, hid, lat, pk_own, pk_oth, kvw_own, kvw_oth)
    kv_oth = swap(kv_own)
    q = query(scal, nrm_keep, nrm_send, pk_own, pk_oth, qw_own, qw_oth)
    nrm_recv = swap(nrm_send)
    dz_oth = swap(dz)
    att, lse = attn_fwd(scal, q, kv_own, kv_oth)
    mid, n2_keep, n2_send, act_keep, act_send, gp = mid_block(
        scal, att, xb, dz, pk_own, pk_oth, w_proj, proj_oth, w_fc, fc_oth, w_out, out_oth
    )
    act_recv = swap(act_send)
    n2_recv = swap(n2_send)
    gp_oth = swap(gp)
    block_out = out_block(scal, mid, act_keep, act_send, pk_own, pk_oth, w_out, out_oth)
    r_out = Reduce(*grad_rows(scal, act_keep, act_recv, dz, dz_oth, 384))
    r_out.hop1()
    r_fc = Reduce(*grad_cols(scal, n2_keep, n2_recv, gp, gp_oth, 768))
    dmid, gb, ga, delta, sums = back_block(
        scal, gp, mid, dz, att, pk_own, pk_oth, w_fc, fc_oth, w_proj, proj_oth
    )
    own_half = lambda a: lax.dynamic_slice_in_dim(a, shard * H, H, axis=1)
    att_recv = swap(lax.dynamic_slice_in_dim(att, (1 - shard) * H, H, axis=1))
    gb_oth = swap(gb)
    r_out.hop2()
    r_fc.hop1()
    parts = []
    groups = []
    count = D // 128 // 2
    for g in range(2):
        dq, dko, dvo, dkt, dvt = attn_bwd(scal, q, kv_own, kv_oth, ga, lse, delta, g * count, count)
        rq, rko, rvo, rkt, rvt = swap(dq), swap(dko), swap(dvo), swap(dkt), swap(dvt)
        groups.append((dq, rq, dko, dkt, rko, rkt, dvo, dvt, rvo, rvt))
    r_proj = Reduce(*grad_cols(scal, own_half(att), att_recv, gb, gb_oth, D))
    r_g = []
    for parts in groups:
        send, keep = grad_qkv(scal, nrm_keep, nrm_recv, parts)
        r_g.append((send, keep))
    r_a = Reduce(*r_g[0])
    r_b = ReduceWith(*r_g[1])
    a, b = groups
    gh, glat, s_keep, s_send = last_block(
        scal, (a[0], b[0], a[2], b[2], a[5], b[5], a[6], b[6], a[9], b[9]),
        xb, dmid, pk_own, pk_oth, w_qkv, qkv_oth, sums, r_b.keep.shape[1],
    )
    small = (s_keep + swap(s_send)).astype(BF)
    glat = glat + swap(glat)
    r_out.hop3()
    r_fc.hop2()
    r_proj.hop1()
    r_out.hop4()
    r_fc.hop3()
    r_a.hop1()
    r_out.hop5()
    r_fc.hop4()
    r_proj.hop2()
    r_a.hop2()
    r_b.hop1()
    r_out.hop6()
    r_fc.hop5()
    r_proj.hop3()
    r_a.hop3()
    r_b.hop2()
    r_out.hop7()
    r_fc.hop6()
    r_proj.hop4()
    r_a.hop4()
    r_b.hop3()
    r_fc.hop7()
    r_proj.hop5()
    r_a.hop5()
    r_b.hop4(small)
    r_proj.hop6()
    r_a.hop6()
    r_b.hop5()
    r_proj.hop7()
    r_a.hop7()
    r_b.hop6()
    r_b.hop7()
    g_out = r_out.done(scal)
    g_fc = r_fc.done(scal)
    g_proj = r_proj.done(scal)
    g_a = r_a.done(scal)
    g_b, small = r_b.done(scal)
    N = g_a.shape[1] // 3
    g_qkv = jnp.concatenate([g_a[:, :N], g_b[:, :N], g_a[:, N : 2 * N], g_b[:, N : 2 * N], g_a[:, 2 * N :], g_b[:, 2 * N :]], axis=1)
    flat = small[:4].reshape(-1)
    cuts = [0]
    for v in (ln1_gain, ln1_bias, b_qv, b_proj, ln2_gain, ln2_bias, b_fc, b_out):
        cuts.append(cuts[-1] + v.shape[0])
    vecs = [flat[cuts[i] : cuts[i + 1]] for i in range(8)]
    return (
        block_out[None], gh[None], glat[None, :6], vecs[0], vecs[1], g_qkv, vecs[2], g_proj, vecs[3],
        vecs[4], vecs[5], g_fc, vecs[6], g_out, vecs[7],
    )


def layer_norm(values, norm_gain, norm_shift):
    average = jnp.mean(values, axis=-1, keepdims=True)
    centered = values - average
    variance = jnp.mean(centered * centered, axis=-1, keepdims=True)
    return centered * lax.rsqrt(variance + norm_epsilon) * norm_gain + norm_shift


def gelu_tanh(values):
    return (
        0.5
        * values
        * (1.0 + jnp.tanh(gelu_root * (values + gelu_cubic * values * values * values)))
    )


def head_scores(query_one, key_one, query_pos, key_pos, prefix_one, score_scale):
    scores = (
        jnp.einsum("qhe,khe->hqk", query_one, key_one, preferred_element_type=jnp.float32)
        * score_scale
    )
    causal = (key_pos[None, :] <= query_pos[:, None])[None]
    in_prefix = (key_pos < prefix_one)[None, None, :]
    return jnp.where(causal | in_prefix, scores, masked_score)


def per_device(
    hidden,
    latents,
    latent_pos,
    prefix,
    ln1_gain,
    ln1_bias,
    w_qkv,
    b_qv,
    w_proj,
    b_proj,
    ln2_gain,
    ln2_bias,
    w_fc,
    b_fc,
    w_out,
    b_out,
    cotangent,
):
    seq_count, local_len, model_width = hidden.shape
    head_dim = model_width // HEADS
    score_scale = head_dim ** (-0.5)
    row_start = lax.axis_index("shard") * local_len
    gathered = (
        lax.all_gather(ln1_gain, "shard", axis=0, tiled=True),
        lax.all_gather(ln1_bias, "shard", axis=0, tiled=True),
        lax.all_gather(w_qkv, "shard", axis=0, tiled=True),
        lax.all_gather(b_qv, "shard", axis=0, tiled=True),
        lax.all_gather(w_proj, "shard", axis=0, tiled=True),
        lax.all_gather(b_proj, "shard", axis=0, tiled=True),
        lax.all_gather(ln2_gain, "shard", axis=0, tiled=True),
        lax.all_gather(ln2_bias, "shard", axis=0, tiled=True),
        lax.all_gather(w_fc, "shard", axis=0, tiled=True),
        lax.all_gather(b_fc, "shard", axis=0, tiled=True),
        lax.all_gather(w_out, "shard", axis=0, tiled=True),
        lax.all_gather(b_out, "shard", axis=0, tiled=True),
    )
    (
        full_ln1_gain,
        full_ln1_bias,
        full_qkv,
        full_b_qv,
        full_proj,
        full_b_proj,
        full_ln2_gain,
        full_ln2_bias,
        full_fc,
        full_b_fc,
        complete_output,
        full_b_out,
    ) = gathered
    row_ids = row_start + jnp.arange(local_len, dtype=jnp.int32)
    latent_matches = row_ids[None, :, None] == latent_pos[:, None, :]
    positioned_rows = jnp.einsum(
        "ety,eyw->etw",
        latent_matches.astype(jnp.bfloat16),
        latents,
        preferred_element_type=jnp.float32,
    )
    replaced = jnp.any(latent_matches, axis=-1)[..., None]
    block_in = jnp.where(replaced, positioned_rows, hidden.astype(jnp.float32)).reshape(
        -1, model_width
    )
    normed, back_norm_one = jax.vjp(
        layer_norm, block_in, full_ln1_gain.astype(jnp.float32), full_ln1_bias.astype(jnp.float32)
    )
    normed_low = normed.astype(jnp.bfloat16)
    bias_full = jnp.concatenate(
        [
            full_b_qv[:model_width].astype(jnp.float32),
            jnp.zeros((model_width,), jnp.float32),
            full_b_qv[model_width:].astype(jnp.float32),
        ]
    )
    projected = (
        jnp.dot(normed_low, full_qkv, preferred_element_type=jnp.float32) + bias_full
    ).astype(jnp.bfloat16)
    query_heads = projected[:, :model_width].reshape(seq_count, local_len, HEADS, head_dim)
    key_local = projected[:, model_width : 2 * model_width].reshape(
        seq_count, local_len, model_width
    )
    value_local = projected[:, 2 * model_width :].reshape(seq_count, local_len, model_width)
    key_full, value_full = (
        lax.all_gather(key_local, "shard", axis=1, tiled=True),
        lax.all_gather(value_local, "shard", axis=1, tiled=True),
    )
    full_len = key_full.shape[1]
    key_heads = key_full.reshape(seq_count, full_len, HEADS, head_dim)
    value_heads = value_full.reshape(seq_count, full_len, HEADS, head_dim)
    key_pos_all = jnp.arange(full_len, dtype=jnp.int32)

    def forward_seq(items):
        query_one, key_one, value_one, prefix_one = items
        scores = head_scores(query_one, key_one, row_ids, key_pos_all, prefix_one, score_scale)
        row_peak = jnp.max(scores, axis=-1, keepdims=True)
        single_logsumexp = row_peak + jnp.log(
            jnp.sum(jnp.exp(scores - row_peak), axis=-1, keepdims=True)
        )
        probs_low = jnp.exp(scores - single_logsumexp).astype(jnp.bfloat16)
        mixed = jnp.einsum("hqk,khe->qhe", probs_low, value_one, preferred_element_type=jnp.float32)
        return (mixed.astype(jnp.bfloat16), single_logsumexp)

    attended_heads, log_total = lax.map(forward_seq, (query_heads, key_heads, value_heads, prefix))
    attended = attended_heads.reshape(-1, model_width)
    middle = (
        block_in
        + jnp.dot(attended, full_proj, preferred_element_type=jnp.float32)
        + full_b_proj.astype(jnp.float32)
    )
    normed_two, back_norm_two = jax.vjp(
        layer_norm, middle, full_ln2_gain.astype(jnp.float32), full_ln2_bias.astype(jnp.float32)
    )
    normed_two_low = normed_two.astype(jnp.bfloat16)
    pre_act = jnp.dot(
        normed_two_low, full_fc, preferred_element_type=jnp.float32
    ) + full_b_fc.astype(jnp.float32)
    activated, back_gelu = jax.vjp(gelu_tanh, pre_act)
    activated_low = activated.astype(jnp.bfloat16)
    block_out = (
        middle
        + jnp.dot(activated_low, complete_output, preferred_element_type=jnp.float32)
        + full_b_out.astype(jnp.float32)
    )
    block_out = block_out.reshape(seq_count, local_len, model_width).astype(jnp.bfloat16)
    back_qkv, back_proj, back_fc, back_out = (
        lax.all_gather(w_qkv, "shard", axis=0, tiled=True),
        lax.all_gather(w_proj, "shard", axis=0, tiled=True),
        lax.all_gather(w_fc, "shard", axis=0, tiled=True),
        lax.all_gather(w_out, "shard", axis=0, tiled=True),
    )
    grad_top = cotangent.reshape(-1, model_width)
    grad_w_out = jnp.einsum(
        "nf,nd->fd", activated_low, grad_top, preferred_element_type=jnp.float32
    )
    grad_b_out = jnp.sum(grad_top.astype(jnp.float32), axis=0)
    grad_act = jnp.einsum("nd,fd->nf", grad_top, back_out, preferred_element_type=jnp.float32)
    (grad_pre,) = back_gelu(grad_act)
    grad_pre_low = grad_pre.astype(jnp.bfloat16)
    grad_w_fc = jnp.einsum(
        "nd,nf->df", normed_two_low, grad_pre_low, preferred_element_type=jnp.float32
    )
    grad_b_fc = jnp.sum(grad_pre_low.astype(jnp.float32), axis=0)
    grad_normed_two = jnp.einsum(
        "nf,df->nd", grad_pre_low, back_fc, preferred_element_type=jnp.float32
    )
    grad_mid_norm, grad_ln2_gain, grad_ln2_bias = back_norm_two(grad_normed_two)
    grad_mid = grad_top.astype(jnp.float32) + grad_mid_norm
    grad_branch_low = grad_mid.astype(jnp.bfloat16)
    grad_w_proj = jnp.einsum(
        "nd,ne->de", attended, grad_branch_low, preferred_element_type=jnp.float32
    )
    grad_b_proj = jnp.sum(grad_branch_low.astype(jnp.float32), axis=0)
    grad_att = jnp.einsum(
        "ne,de->nd", grad_branch_low, back_proj, preferred_element_type=jnp.float32
    )
    grad_att_low = grad_att.astype(jnp.bfloat16).reshape(seq_count, local_len, HEADS, head_dim)

    def backward_sequence(items):
        query_one, key_one, value_one, prefix_one, single_logsumexp, upstream = items
        scores = head_scores(query_one, key_one, row_ids, key_pos_all, prefix_one, score_scale)
        attn_probs = jnp.exp(scores - single_logsumexp)
        grad_value_one = jnp.einsum(
            "hqk,qhe->khe",
            attn_probs.astype(jnp.bfloat16),
            upstream,
            preferred_element_type=jnp.float32,
        )
        grad_probs = jnp.einsum(
            "qhe,khe->hqk", upstream, value_one, preferred_element_type=jnp.float32
        )
        delta_one = jnp.sum(grad_probs * attn_probs, axis=-1, keepdims=True)
        grad_scores = (attn_probs * (grad_probs - delta_one)).astype(jnp.bfloat16)
        grad_query_one = (
            jnp.einsum("hqk,khe->qhe", grad_scores, key_one, preferred_element_type=jnp.float32)
            * score_scale
        )
        grad_key_one = (
            jnp.einsum("hqk,qhe->khe", grad_scores, query_one, preferred_element_type=jnp.float32)
            * score_scale
        )
        return (
            grad_query_one,
            grad_key_one.reshape(full_len, model_width),
            grad_value_one.reshape(full_len, model_width),
        )

    grad_query, grad_key_all, grad_value_all = lax.map(
        backward_sequence, (query_heads, key_heads, value_heads, prefix, log_total, grad_att_low)
    )
    grad_key_own, grad_value_own = (
        lax.psum_scatter(
            grad_key_all.astype(jnp.bfloat16), "shard", scatter_dimension=1, tiled=True
        ).astype(jnp.float32),
        lax.psum_scatter(
            grad_value_all.astype(jnp.bfloat16), "shard", scatter_dimension=1, tiled=True
        ).astype(jnp.float32),
    )
    grad_query_low = grad_query.reshape(-1, model_width).astype(jnp.bfloat16)
    grad_key_low = grad_key_own.reshape(-1, model_width).astype(jnp.bfloat16)
    grad_value_low = grad_value_own.reshape(-1, model_width).astype(jnp.bfloat16)
    grad_projected = jnp.concatenate([grad_query_low, grad_key_low, grad_value_low], axis=1)
    grad_b_qv = jnp.concatenate(
        [
            jnp.sum(grad_query_low.astype(jnp.float32), axis=0),
            jnp.sum(grad_value_low.astype(jnp.float32), axis=0),
        ]
    )
    grad_w_qkv = jnp.einsum(
        "nd,ne->de", normed_low, grad_projected, preferred_element_type=jnp.float32
    )
    grad_normed = jnp.einsum(
        "ne,de->nd", grad_projected, back_qkv, preferred_element_type=jnp.float32
    )
    grad_in_norm, grad_ln1_gain, grad_ln1_bias = back_norm_one(grad_normed)
    block_gradient = (grad_mid + grad_in_norm).reshape(seq_count, local_len, model_width)
    latent_terms = jnp.einsum(
        "inv,inz->ivz",
        latent_matches.astype(jnp.float32),
        block_gradient,
        precision=lax.Precision.HIGHEST,
    )
    grad_latents = lax.psum(latent_terms, "shard")
    grad_hidden = jnp.where(replaced, 0.0, block_gradient).astype(jnp.bfloat16)
    shares = (
        lax.psum_scatter(
            grad_ln1_gain.astype(jnp.bfloat16), "shard", scatter_dimension=0, tiled=True
        ).astype(jnp.float32),
        lax.psum_scatter(
            grad_ln1_bias.astype(jnp.bfloat16), "shard", scatter_dimension=0, tiled=True
        ).astype(jnp.float32),
        lax.psum_scatter(
            grad_w_qkv.astype(jnp.bfloat16), "shard", scatter_dimension=0, tiled=True
        ).astype(jnp.float32),
        lax.psum_scatter(
            grad_b_qv.astype(jnp.bfloat16), "shard", scatter_dimension=0, tiled=True
        ).astype(jnp.float32),
        lax.psum_scatter(
            grad_w_proj.astype(jnp.bfloat16), "shard", scatter_dimension=0, tiled=True
        ).astype(jnp.float32),
        lax.psum_scatter(
            grad_b_proj.astype(jnp.bfloat16), "shard", scatter_dimension=0, tiled=True
        ).astype(jnp.float32),
        lax.psum_scatter(
            grad_ln2_gain.astype(jnp.bfloat16), "shard", scatter_dimension=0, tiled=True
        ).astype(jnp.float32),
        lax.psum_scatter(
            grad_ln2_bias.astype(jnp.bfloat16), "shard", scatter_dimension=0, tiled=True
        ).astype(jnp.float32),
        lax.psum_scatter(
            grad_w_fc.astype(jnp.bfloat16), "shard", scatter_dimension=0, tiled=True
        ).astype(jnp.float32),
        lax.psum_scatter(
            grad_b_fc.astype(jnp.bfloat16), "shard", scatter_dimension=0, tiled=True
        ).astype(jnp.float32),
        lax.psum_scatter(
            grad_w_out.astype(jnp.bfloat16), "shard", scatter_dimension=0, tiled=True
        ).astype(jnp.float32),
        lax.psum_scatter(
            grad_b_out.astype(jnp.bfloat16), "shard", scatter_dimension=0, tiled=True
        ).astype(jnp.float32),
    )
    summed = (
        lax.psum(shares[0].astype(jnp.bfloat16), "rep").astype(jnp.float32),
        lax.psum(shares[1].astype(jnp.bfloat16), "rep").astype(jnp.float32),
        lax.psum(shares[2].astype(jnp.bfloat16), "rep").astype(jnp.float32),
        lax.psum(shares[3].astype(jnp.bfloat16), "rep").astype(jnp.float32),
        lax.psum(shares[4].astype(jnp.bfloat16), "rep").astype(jnp.float32),
        lax.psum(shares[5].astype(jnp.bfloat16), "rep").astype(jnp.float32),
        lax.psum(shares[6].astype(jnp.bfloat16), "rep").astype(jnp.float32),
        lax.psum(shares[7].astype(jnp.bfloat16), "rep").astype(jnp.float32),
        lax.psum(shares[8].astype(jnp.bfloat16), "rep").astype(jnp.float32),
        lax.psum(shares[9].astype(jnp.bfloat16), "rep").astype(jnp.float32),
        lax.psum(shares[10].astype(jnp.bfloat16), "rep").astype(jnp.float32),
        lax.psum(shares[11].astype(jnp.bfloat16), "rep").astype(jnp.float32),
    )
    (
        total_ln1_gain,
        total_ln1_bias,
        total_w_qkv,
        total_b_qv,
        total_w_proj,
        total_b_proj,
        total_ln2_gain,
        total_ln2_bias,
        total_w_fc,
        total_b_fc,
        total_w_out,
        total_b_out,
    ) = summed
    return (
        block_out,
        grad_hidden,
        grad_latents,
        total_ln1_gain,
        total_ln1_bias,
        total_w_qkv,
        total_b_qv,
        total_w_proj,
        total_b_proj,
        total_ln2_gain,
        total_ln2_bias,
        total_w_fc,
        total_b_fc,
        total_w_out,
        total_b_out,
    )


def solution(mesh):
    sizes = dict(mesh.shape)
    paired = sizes["rep"] == 16 and sizes["shard"] == 2
    body = pair_device if paired else per_device
    in_specs = (
        P("rep", "shard", None),
        P("rep", None, None),
        P("rep", None),
        P("rep"),
        P("shard"),
        P("shard"),
        P("shard", None),
        P("shard"),
        P("shard", None),
        P("shard"),
        P("shard"),
        P("shard"),
        P("shard", None),
        P("shard"),
        P("shard", None),
        P("shard"),
        P("rep", "shard", None),
    )
    out_specs = (
        P("rep", "shard", None),
        P("rep", "shard", None),
        P("rep", None, None),
        P("shard"),
        P("shard"),
        P("shard", None),
        P("shard"),
        P("shard", None),
        P("shard"),
        P("shard"),
        P("shard"),
        P("shard", None),
        P("shard"),
        P("shard", None),
        P("shard"),
    )
    return jax.shard_map(
        body, mesh=mesh, in_specs=in_specs, out_specs=out_specs, check_vma=False
    )
```

```python
import functools
import jax
import jax.numpy as jnp
from jax import lax
from jax.experimental import pallas as pl
from jax.experimental.pallas import tpu as pltpu
from jax.sharding import PartitionSpec as P

HEADS = 12
F32 = jnp.float32
BF = jnp.bfloat16

norm_epsilon = 1e-05
gelu_root = 0.7978845608028654
gelu_cubic = 0.044715
masked_score = -1e30
LOG2E = 1.4426950408889634


def dot_nt(a, b):
    return lax.dot_general(a, b, (((1,), (1,)), ((), ())), preferred_element_type=F32)


def dot_nn(a, b):
    return lax.dot_general(a, b, (((1,), (0,)), ((), ())), preferred_element_type=F32)


def dot_tn(a, b):
    return lax.dot_general(a, b, (((0,), (0,)), ((), ())), preferred_element_type=F32)


def params(semantics=None, mb=16):
    return pltpu.CompilerParams(dimension_semantics=semantics, vmem_limit_bytes=mb * 1024 * 1024)


def cost(flops, nbytes, trans=0):
    return pl.CostEstimate(flops=int(flops), bytes_accessed=int(nbytes), transcendentals=int(trans))


def whole(shape):
    return pl.BlockSpec(shape, lambda *_: (0,) * len(shape), pipeline_mode=pl.Buffered(1))


def both(own, oth, shard, a, n):
    o = own[0:1, a : a + n].astype(F32)
    t = oth[0:1, a : a + n].astype(F32)
    first = jnp.where(shard == 0, o, t)
    second = jnp.where(shard == 0, t, o)
    return jnp.concatenate([first, second], axis=1)


def half(i, n):
    return pl.ds(pl.multiple_of(i * n, n), n)


def call(kernel, name, grid, in_specs, out_specs, out_shape, scratch, est, args, mb=16):
    return pl.pallas_call(
        kernel,
        out_shape=out_shape,
        grid_spec=pltpu.PrefetchScalarGridSpec(
            num_scalar_prefetch=1, grid=grid, in_specs=in_specs, out_specs=out_specs, scratch_shapes=scratch
        ),
        compiler_params=params(("arbitrary",), mb),
        cost_estimate=est,
        name=name,
    )(*args)


sds = jax.ShapeDtypeStruct


def pack_kernel(*refs):
    out = refs[-1]
    at = 0
    for ref in refs[:-1]:
        n = ref.shape[1]
        out[0:1, at : at + n] = ref[...]
        at += n


def pack(vecs):
    total = sum(v.shape[0] for v in vecs)
    return pl.pallas_call(
        pack_kernel,
        out_shape=sds((1, total), BF),
        compiler_params=params(),
        cost_estimate=cost(total, 4 * total),
        name="pack",
    )(*[v[None, :] for v in vecs])


def qv_bias(pk_own, pk_oth, shard, which, heads):
    H = pk_own.shape[1] // 12
    a = pk_own[0:1, 2 * H : 4 * H].astype(F32)
    b = pk_oth[0:1, 2 * H : 4 * H].astype(F32)
    src = jnp.where(shard == which, a, b)
    return jnp.where(heads == 0, src[:, :H], src[:, H:])


def project(n, ws, pk_own, pk_oth, shard, heads, out):
    H = ws.shape[0] // 2
    for j in range(3):
        y = dot_nn(n, ws[:, j * H : (j + 1) * H])
        if j != 1:
            y = y + qv_bias(pk_own, pk_oth, shard, j // 2, heads)
        out[:, j * H : (j + 1) * H] = y.astype(BF)


def ln_send_kernel(
    scal, hid, lat, pk_own, pk_oth, qo, ko, vo, qt, kt, vt, send, normed, nrm_send, xb, xs, ns, ws, *, L
):
    r = pl.program_id(0)
    RB, D = hid.shape
    H = D // 2
    shard = scal[0]

    @pl.when(r == 0)
    def _():
        for j, (o, t) in enumerate(((qo, qt), (ko, kt), (vo, vt))):
            ws[half(shard, H), j * H : (j + 1) * H] = o[...]
            ws[half(1 - shard, H), j * H : (j + 1) * H] = t[...]

    xs[...] = hid[...].astype(F32)
    row0 = shard * L + r * RB
    for c in range(6):
        rel = scal[2 + c] - row0

        @pl.when((rel >= 0) & (rel < RB))
        def _():
            xs[pl.ds(rel, 1), :] = lat[c : c + 1, :].astype(F32)

    g = both(pk_own, pk_oth, shard, 0, H)
    b = both(pk_own, pk_oth, shard, H, H)
    x = xs[...]
    xb[...] = x.astype(BF)
    cen = x - jnp.mean(x, axis=1, keepdims=True)
    var = jnp.mean(cen * cen, axis=1, keepdims=True)
    n = (cen * lax.rsqrt(var + norm_epsilon) * g + b).astype(BF)
    ns[...] = n
    normed[...] = n
    nrm_send[...] = ns[:, half(1 - shard, H)]
    project(n, ws, pk_own, pk_oth, shard, 1 - shard, send)


def ln_send(scal, hid, lat, pk_own, pk_oth, w_own, w_oth):
    L, D = hid.shape
    H = D // 2
    RB = L // 2
    NP = pk_own.shape[1]
    rows = lambda n: pl.BlockSpec((RB, n), lambda r, s: (r, 0))
    w = [
        pl.BlockSpec((H, H), lambda r, s, j=j: (0, 2 * j + 1 - s[0]), pipeline_mode=pl.Buffered(1)) for j in range(3)
    ]
    return call(
        functools.partial(ln_send_kernel, L=L), "ln_send", (2,),
        [rows(D), whole(lat.shape), whole((1, NP)), whole((1, NP))] + w + w,
        [rows(3 * H), rows(D), rows(H), rows(D)],
        (sds((L, 3 * H), BF), sds((L, D), BF), sds((L, H), BF), sds((L, D), BF)),
        [pltpu.VMEM((RB, D), F32), pltpu.VMEM((RB, D), BF), pltpu.VMEM((D, 3 * H), BF)],
        cost(6 * L * D * H, 6e6),
        (scal, hid, lat, pk_own, pk_oth, w_own, w_own, w_own, w_oth, w_oth, w_oth),
    )


def own_kernel(scal, normed, pk_own, pk_oth, qo, ko, vo, qt, kt, vt, keep, ws):
    H = qo.shape[0]
    shard = scal[0]

    @pl.when(pl.program_id(0) == 0)
    def _():
        for j, (o, t) in enumerate(((qo, qt), (ko, kt), (vo, vt))):
            ws[half(shard, H), j * H : (j + 1) * H] = o[...]
            ws[half(1 - shard, H), j * H : (j + 1) * H] = t[...]

    project(normed[...], ws, pk_own, pk_oth, shard, shard, keep)


def own_heads(scal, normed, pk_own, pk_oth, w_own, w_oth):
    L, D = normed.shape
    H = D // 2
    RB = L // 2
    NP = pk_own.shape[1]
    rows = lambda n: pl.BlockSpec((RB, n), lambda r, s: (r, 0))
    w = [pl.BlockSpec((H, H), lambda r, s, j=j: (0, 2 * j + s[0]), pipeline_mode=pl.Buffered(1)) for j in range(3)]
    return call(
        own_kernel, "own_heads", (2,),
        [rows(D), whole((1, NP)), whole((1, NP))] + w + w, rows(3 * H), sds((L, 3 * H), BF),
        [pltpu.VMEM((D, 3 * H), BF)],
        cost(6 * L * D * H, 4e6),
        (scal, normed, pk_own, pk_oth, w_own, w_own, w_own, w_oth, w_oth, w_oth),
    )


def join(dst, own, oth, shard):
    L = own.shape[0]
    dst[half(shard, L), :] = own[...]
    dst[half(1 - shard, L), :] = oth[...]


def attn_fwd_kernel(scal, qa, ka, va, qb, kb_, vb, o_keep, o_send, lse_ref, qs, ks, vs, os_, stat, *, L, RB):
    p_id = pl.program_id(0)
    shard = scal[0]
    pfx = scal[1]
    join(qs, qa, qb, shard)
    join(ks, ka, kb_, shard)
    join(vs, va, vb, shard)
    lane = lax.broadcasted_iota(jnp.int32, (RB, 128), 1)
    c = 0.125 * LOG2E
    HB = L // RB

    for r in range(2 * HB):
        q = qs[r * RB : (r + 1) * RB, :]
        outs = []
        for hh in range(2):
            sel = (lane < 64) if hh == 0 else (lane >= 64)
            qm = jnp.where(sel, q, jnp.zeros_like(q))
            pieces = []
            if r >= HB:
                pieces.append((dot_nt(qm, ks[0:L, :]) * c, vs[0:L, :]))
            for kb in range(HB) if r < HB else range(HB, r + 1):
                s = dot_nt(qm, ks[kb * RB : (kb + 1) * RB, :]) * c
                if kb >= r:
                    col = lax.broadcasted_iota(jnp.int32, (RB, RB), 1) + kb * RB
                    row = lax.broadcasted_iota(jnp.int32, (RB, RB), 0) + r * RB
                    keep = (col <= row) | (col < pfx) if r < HB else (col <= row)
                    s = jnp.where(keep, s, masked_score)
                pieces.append((s, vs[kb * RB : (kb + 1) * RB, :]))
            m = functools.reduce(jnp.maximum, [jnp.max(s, axis=1, keepdims=True) for s, _ in pieces])
            total = jnp.zeros((RB, 1), F32)
            o = jnp.zeros((RB, 128), F32)
            for s, v in pieces:
                p = jnp.exp2(s - m)
                total = total + jnp.sum(p, axis=1, keepdims=True)
                o = o + dot_nn(p.astype(BF), v)
            outs.append(o * (1.0 / total))
            lse = m + jnp.log2(total)
            here = lane == p_id * 2 + hh
            stat[r * RB : (r + 1) * RB, :] = jnp.where(here, lse, stat[r * RB : (r + 1) * RB, :])
        os_[r * RB : (r + 1) * RB, :] = jnp.where(lane < 64, outs[0], outs[1]).astype(BF)

    o_keep[...] = os_[half(shard, L), :]
    o_send[...] = os_[half(1 - shard, L), :]

    @pl.when(p_id == pl.num_programs(0) - 1)
    def _():
        lse_ref[...] = stat[...].T[0:8, :]


def attn_fwd(scal, keep, recv):
    L, W = keep.shape
    H = W // 3
    NP = H // 128
    spec = lambda off: pl.BlockSpec((L, 128), lambda p, s: (0, p + off))
    seq = pltpu.VMEM((2 * L, 128), BF)
    o = sds((L, H), BF)
    return call(
        functools.partial(attn_fwd_kernel, L=L, RB=256), "attn_fwd", (NP,),
        [spec(0), spec(NP), spec(2 * NP)] * 2,
        [spec(0), spec(0), pl.BlockSpec((8, 2 * L), lambda p, s: (0, 0))],
        (o, o, sds((8, 2 * L), F32)),
        [seq, seq, seq, seq, pltpu.VMEM((2 * L, 128), F32)],
        cost(12e9, 4e6, 6e6),
        (scal, keep, keep, keep, recv, recv, recv),
    )


def attn_bwd_kernel(
    scal, qa, ka, va, qb, kb_, vb, ga, gb, aa, ab, lse_ref, d_own, d_oth, qs, ks, vs, gs, as_, dks, dvs, dqt, *, L, KB, p0
):
    shard = scal[0]
    pfx = scal[1]
    join(qs, qa, qb, shard)
    join(ks, ka, kb_, shard)
    join(vs, va, vb, shard)
    join(gs, ga, gb, shard)
    join(as_, aa, ab, shard)
    S = 2 * L
    c = 0.125 * LOG2E
    lane = lax.broadcasted_iota(jnp.int32, (S, 128), 1)
    q = qs[...]
    do = gs[...]
    z = jnp.zeros_like(q)
    qm = [jnp.where(lane < 64, q, z), jnp.where(lane >= 64, q, z)]
    dm = [jnp.where(lane < 64, do, z), jnp.where(lane >= 64, do, z)]
    prod = do.astype(F32) * as_[...].astype(F32)
    hi = prod.astype(BF)
    lo = (prod - hi.astype(F32)).astype(BF)
    head = lax.broadcasted_iota(jnp.int32, (16, 128), 0)
    plane = lax.broadcasted_iota(jnp.int32, (16, 128), 1)
    pick = jnp.where((plane >= head * 64) & (plane < head * 64 + 64), 1.0, 0.0).astype(BF)
    delta = dot_nt(pick, hi) + dot_nt(pick, lo)
    hb = (pl.program_id(0) + p0) * 2
    lse = [lse_ref[pl.ds(hb + hh, 1), :] for hh in range(2)]
    dl = [delta[hh : hh + 1, :] for hh in range(2)]
    dqt[...] = jnp.zeros_like(dqt)

    for kb in range(S // KB):
        rows = slice(kb * KB, (kb + 1) * KB)
        k = ks[rows, :]
        v = vs[rows, :]
        kt = k.T
        dk = None
        dv = None
        spans = [(0, L), (L, S)] if kb * KB < L else [(kb * KB, S)]
        for q0, q1 in spans:
            mask = None
            if q0 <= kb * KB:
                key = lax.broadcasted_iota(jnp.int32, (KB, q1 - q0), 0) + kb * KB
                qry = lax.broadcasted_iota(jnp.int32, (KB, q1 - q0), 1) + q0
                mask = (key <= qry) | (key < pfx) if q1 <= L else key <= qry
            for hh in range(2):
                st = dot_nt(k, qm[hh][q0:q1, :]) * c
                if mask is not None:
                    st = jnp.where(mask, st, masked_score)
                pt = jnp.exp2(st - lse[hh][:, q0:q1])
                dpt = dot_nt(v, dm[hh][q0:q1, :])
                dst = (pt * (dpt - dl[hh][:, q0:q1])).astype(BF)
                a = dot_nn(pt.astype(BF), dm[hh][q0:q1, :])
                b = dot_nn(dst, qm[hh][q0:q1, :])
                dv = a if dv is None else dv + a
                dk = b if dk is None else dk + b
                dqt[hh * 64 : (hh + 1) * 64, q0:q1] += dot_nn(kt[hh * 64 : (hh + 1) * 64, :], dst)
        dks[rows, :] = (dk * 0.125).astype(BF)
        dvs[rows, :] = dv.astype(BF)

    gs[...] = (dqt[...].T * 0.125).astype(BF)
    for j, src in enumerate((gs, dks, dvs)):
        d_own[j] = src[half(shard, L), :]
        d_oth[j] = src[half(1 - shard, L), :]


def attn_bwd(scal, keep, recv, ga_keep, ga_recv, att_keep, att_send, lse, p0, count):
    L, W = keep.shape
    H = W // 3
    NP = H // 128
    spec = lambda off: pl.BlockSpec((L, 128), lambda p, s: (0, p + off))
    seq = pltpu.VMEM((2 * L, 128), BF)
    o = sds((3, L, count * 128), BF)
    ospec = pl.BlockSpec((3, L, 128), lambda p, s: (0, 0, p))
    share = count / NP
    return call(
        functools.partial(attn_bwd_kernel, L=L, KB=256, p0=p0), "attn_bwd", (count,),
        [spec(p0), spec(NP + p0), spec(2 * NP + p0)] * 2 + [spec(p0)] * 4 + [pl.BlockSpec((8, 2 * L), lambda p, s: (0, 0))],
        [ospec, ospec], (o, o),
        [seq] * 7 + [pltpu.VMEM((128, 2 * L), F32)],
        cost(24e9 * share, 8e6 * share, 6e6 * share),
        (scal, keep, keep, keep, recv, recv, recv, ga_keep, ga_recv, att_keep, att_send, lse),
    )


def ffn_kernel(
    scal, ak, ar, xb, dz, pk_own, pk_oth, wp_own, wp_oth, wf_own, wf_oth, wo_own, wo_oth,
    act_keep, act_send, gp, n2_keep, n2_send, out, dmid, gb, ga_keep, ga_send, sfc, sums,
    ns, mid, yacc, gacc, wfs, wos, *, T,
):
    t = pl.program_id(0)
    last = pl.num_programs(0) - 1
    NH = pl.num_programs(0) // 2
    shard = scal[0]
    L, D = xb.shape
    H = D // 2
    FH = wo_own.shape[0] * NH
    o_bp, o_g2, o_b2, o_bf = 4 * H, 5 * H, 6 * H, 7 * H
    o_bo = 11 * H
    RB = L // 4

    @pl.when(t == 0)
    def _():
        g = both(pk_own, pk_oth, shard, o_g2, H)
        b = both(pk_own, pk_oth, shard, o_b2, H)
        bp = both(pk_own, pk_oth, shard, o_bp, H)
        for i in range(4):
            rows = slice(i * RB, (i + 1) * RB)
            m = dot_nn(ak[rows, :], wp_own[...]) + dot_nn(ar[rows, :], wp_oth[...])
            m = m + xb[rows, :].astype(F32) + bp
            mid[rows, :] = m
            cen = m - jnp.mean(m, axis=1, keepdims=True)
            var = jnp.mean(cen * cen, axis=1, keepdims=True)
            ns[rows, :] = (cen * lax.rsqrt(var + norm_epsilon) * g + b).astype(BF)
        n2_keep[...] = ns[:, half(shard, H)]
        n2_send[...] = ns[:, half(1 - shard, H)]
        yacc[...] = jnp.zeros_like(yacc)
        gacc[...] = jnp.zeros_like(gacc)

    wfs[half(shard, H), :] = wf_own[...]
    wfs[half(1 - shard, H), :] = wf_oth[...]

    @pl.when(t < NH)
    def _():
        wos[...] = wo_own[...]

    @pl.when(t >= NH)
    def _():
        wos[...] = wo_oth[...]

    at = pl.ds(pl.multiple_of(o_bf + lax.rem(t, NH) * T, 128), T)
    bias = jnp.where(t < NH, pk_own[0:1, at].astype(F32), pk_oth[0:1, at].astype(F32))
    total = jnp.zeros((1, T), F32)
    CB = L // 2
    for i in range(2):
        rows = slice(i * CB, (i + 1) * CB)
        u = dot_nn(ns[rows, :], wfs[...]) + bias
        ga = dot_nt(dz[rows, :], wos[...])
        u2 = u * u
        th = jnp.tanh(u * (gelu_root + (gelu_root * gelu_cubic) * u2))
        hp = 0.5 + 0.5 * th
        av = u * hp
        slope = hp + av * ((1.0 - th) * (gelu_root + (3.0 * gelu_root * gelu_cubic) * u2))
        a = av.astype(BF)
        g = (ga * slope).astype(BF)
        gp[rows, :] = g

        @pl.when(t < NH)
        def _():
            act_keep[rows, :] = a

        @pl.when(t >= NH)
        def _():
            act_send[rows, :] = a

        total = total + jnp.sum(g.astype(F32), axis=0, keepdims=True)
        yacc[rows, :] += dot_nn(a, wos[...])
        gacc[rows, :] += dot_nt(g, wfs[...])
    sfc[...] = jnp.broadcast_to(total, sfc.shape)

    @pl.when(t == last)
    def _():
        g2 = both(pk_own, pk_oth, shard, o_g2, H)
        bo = both(pk_own, pk_oth, shard, o_bo, H)
        sums[...] = jnp.zeros_like(sums)
        for i in range(4):
            rows = slice(i * RB, (i + 1) * RB)
            m = mid[rows, :]
            out[rows, :] = (yacc[rows, :] + m + bo).astype(BF)
            gn = gacc[rows, :]
            cen = m - jnp.mean(m, axis=1, keepdims=True)
            r = lax.rsqrt(jnp.mean(cen * cen, axis=1, keepdims=True) + norm_epsilon)
            n = cen * r
            e = gn * g2
            dzv = dz[rows, :].astype(F32)
            g = dzv + r * (e - jnp.mean(e, axis=1, keepdims=True) - n * jnp.mean(e * n, axis=1, keepdims=True))
            dmid[rows, :] = g
            gbv = g.astype(BF)
            gb[rows, :] = gbv
            ga_keep[rows, :] = dot_nt(gbv, wp_own[...]).astype(BF)
            ga_send[rows, :] = dot_nt(gbv, wp_oth[...]).astype(BF)
            sums[0:1, :] += jnp.sum(gbv.astype(F32), axis=0, keepdims=True)
            sums[1:2, :] += jnp.sum(gn * n, axis=0, keepdims=True)
            sums[2:3, :] += jnp.sum(gn, axis=0, keepdims=True)
            sums[3:4, :] += jnp.sum(dzv, axis=0, keepdims=True)


def ffn(scal, ak, ar, xb, dz, pk_own, pk_oth, wp_own, wp_oth, wf_own, wf_oth, wo_own, wo_oth):
    L, D = xb.shape
    H = D // 2
    FH = wo_own.shape[0]
    T = 512
    NH = FH // T
    NP = pk_own.shape[1]
    tile = lambda t, s: jnp.where(t < NH, s[0] * NH + t, (1 - s[0]) * NH + t - NH)
    first = lambda t: jnp.minimum(t, NH - 1)
    second = lambda t: jnp.maximum(t - NH, 0)
    const = lambda *shape: pl.BlockSpec(shape, lambda t, s: (0,) * len(shape))
    wf = pl.BlockSpec((H, T), lambda t, s: (0, tile(t, s)))
    return call(
        functools.partial(ffn_kernel, T=T), "ffn", (2 * NH,),
        [whole((L, H)), whole((L, H)), whole((L, D)), whole((L, D)), whole((1, NP)), whole((1, NP)), whole((H, D)), whole((H, D)),
         wf, wf, pl.BlockSpec((T, D), lambda t, s: (first(t), 0)), pl.BlockSpec((T, D), lambda t, s: (second(t), 0))],
        [pl.BlockSpec((L, T), lambda t, s: (0, first(t))), pl.BlockSpec((L, T), lambda t, s: (0, second(t))),
         pl.BlockSpec((L, T), lambda t, s: (0, tile(t, s))), const(L, H), const(L, H), const(L, D), const(L, D), const(L, D),
         const(L, H), const(L, H), pl.BlockSpec((8, T), lambda t, s: (0, tile(t, s))), const(8, D)],
        (sds((L, FH), BF), sds((L, FH), BF), sds((L, 2 * FH), BF), sds((L, H), BF), sds((L, H), BF), sds((L, D), BF),
         sds((L, D), F32), sds((L, D), BF), sds((L, H), BF), sds((L, H), BF), sds((8, 2 * FH), F32), sds((8, D), F32)),
        [pltpu.VMEM((L, D), BF), pltpu.VMEM((L, D), F32), pltpu.VMEM((L, D), F32), pltpu.VMEM((L, D), F32),
         pltpu.VMEM((D, T), BF), pltpu.VMEM((T, D), BF)],
        cost(2 * L * D * (2 * D + 8 * FH), 24e6, 1.5e6),
        (scal, ak, ar, xb, dz, pk_own, pk_oth, wp_own, wp_oth, wf_own, wf_oth, wo_own, wo_oth),
    )


def pair_of(i, s):
    return ((i + 2) & 3) ^ (s[8] >> 1)


def put_pair(scal, left, right, send, keep):
    H = left.shape[0]
    i = pl.program_id(0)
    flip = scal[8] & 1
    for out, here in ((send, i < 2), (keep, i >= 2)):

        @pl.when(here)
        def _():
            out[half(flip, H), :] = left
            out[half(1 - flip, H), :] = right


def pair_specs(H):
    shape = (sds((4 * H, H), BF),) * 2
    specs = [
        pl.BlockSpec((2 * H, H), lambda i, s: (jnp.minimum(i, 1), 0)),
        pl.BlockSpec((2 * H, H), lambda i, s: (jnp.maximum(i - 2, 0), 0)),
    ]
    return specs, shape


def grad_pair_kernel(scal, a_own, a_oth, b_own, b_oth, send, keep):
    H = a_own.shape[1]
    val = (dot_tn(a_own[...], b_own[...]) + dot_tn(a_oth[...], b_oth[...])).astype(BF)
    put_pair(scal, val[:, :H], val[:, H:], send, keep)


def grad_rows(scal, a_own, a_oth, b_own, b_oth):
    K, M = a_own.shape
    N = b_own.shape[1]
    H = N // 2
    a = pl.BlockSpec((K, H), lambda i, s: (0, pair_of(i, s)))
    specs, shape = pair_specs(H)
    return call(
        grad_pair_kernel, "grad_rows", (4,), [a, a, whole((K, N)), whole((K, N))], specs, shape, [],
        cost(4 * K * M * N, 4 * K * (M + N) + 2 * M * N), (scal, a_own, a_oth, b_own, b_oth),
    )


def grad_cols(scal, a_own, a_oth, b_own, b_oth):
    K, M = a_own.shape
    N = b_own.shape[1]
    b = pl.BlockSpec((K, 2 * M), lambda i, s: (0, pair_of(i, s)))
    specs, shape = pair_specs(M)
    return call(
        grad_pair_kernel, "grad_cols", (4,), [whole((K, M)), whole((K, M)), b, b], specs, shape, [],
        cost(4 * K * M * N, 4 * K * (M + N) + 2 * M * N), (scal, a_own, a_oth, b_own, b_oth),
    )


def grad_attn_kernel(scal, n_own, n_oth, a_own, a_oth, gb_own, gb_oth, l_own, l_oth, r_own, r_oth, send, keep):
    H = n_own.shape[1]
    shard = scal[0]
    w = pair_of(pl.program_id(0), scal)
    flip = scal[8] & 1

    def put(rows, value):
        i = pl.program_id(0)
        for out, here in ((send, i < 2), (keep, i >= 2)):

            @pl.when(here)
            def _():
                out[half(rows, H), :] = value

    @pl.when(w < 3)
    def _():
        mine = dot_tn(n_own[...], l_own[0]) + dot_tn(n_oth[...], l_oth[0])
        put(shard ^ flip, mine.astype(BF))
        theirs = dot_tn(n_own[...], r_own[0]) + dot_tn(n_oth[...], r_oth[0])
        put(1 - (shard ^ flip), theirs.astype(BF))

    @pl.when(w == 3)
    def _():
        val = (dot_tn(a_own[...], gb_own[...]) + dot_tn(a_oth[...], gb_oth[...])).astype(BF)
        put(flip, val[:, :H])
        put(1 - flip, val[:, H:])


def grad_attn(scal, normed, n_oth, a_own, a_oth, gb_own, gb_oth, l_own, l_oth, r_own, r_oth):
    K, H = n_oth.shape
    D = 2 * H
    d = pl.BlockSpec((1, K, H), lambda i, s: (jnp.minimum(pair_of(i, s), 2), 0, 0))
    n = pl.BlockSpec((K, H), lambda i, s: (0, s[0]), pipeline_mode=pl.Buffered(1))
    w = whole((K, H))
    specs, shape = pair_specs(H)
    return call(
        grad_attn_kernel, "grad_attn", (4,), [n, w, w, w, whole((K, D)), whole((K, D)), d, d, d, d], specs, shape, [],
        cost(32 * K * H * H, 16e6), (scal, normed, n_oth, a_own, a_oth, gb_own, gb_oth, l_own, l_oth, r_own, r_oth),
    )


def last_kernel(
    scal, d_own, d_oth, xb, dmid, pk_own, pk_oth, w_own, w_oth, sfc, sums,
    gh, glat, s_keep, s_send, gi, es, ds_, vec, *, L,
):
    r_id = pl.program_id(0)
    shard = scal[0]
    RB, D = xb.shape
    H = D // 2
    FF = sfc.shape[1]
    for j in range(3):
        ds_[:, half(2 * j + shard, H)] = d_own[j]
        ds_[:, half(2 * j + 1 - shard, H)] = d_oth[j]
    d = ds_[...]
    es[:, half(shard, H)] = dot_nt(d, w_own[...])
    es[:, half(1 - shard, H)] = dot_nt(d, w_oth[...])
    gn = es[...]
    x = xb[...].astype(F32)
    cen = x - jnp.mean(x, axis=1, keepdims=True)
    r = lax.rsqrt(jnp.mean(cen * cen, axis=1, keepdims=True) + norm_epsilon)
    n = cen * r
    e = gn * both(pk_own, pk_oth, shard, 0, H)
    gi[...] = dmid[...] + r * (e - jnp.mean(e, axis=1, keepdims=True) - n * jnp.mean(e * n, axis=1, keepdims=True))

    @pl.when(r_id == 0)
    def _():
        glat[...] = jnp.zeros_like(glat)
        vec[...] = jnp.zeros_like(vec)

    row0 = shard * L + r_id * RB
    for c in range(6):
        rel = scal[2 + c] - row0

        @pl.when((rel >= 0) & (rel < RB))
        def _():
            glat[c : c + 1, :] = gi[pl.ds(rel, 1), :]
            gi[pl.ds(rel, 1), :] = jnp.zeros((1, D), F32)

    gh[...] = gi[...].astype(BF)
    vec[0:1, 0:D] += jnp.sum(gn * n, axis=0, keepdims=True)
    vec[1:2, 0:D] += jnp.sum(gn, axis=0, keepdims=True)
    vec[2:3, 0:D] += jnp.sum(ds_[:, 0:D].astype(F32), axis=0, keepdims=True)
    vec[2:3, D : 2 * D] += jnp.sum(ds_[:, 2 * D : 3 * D].astype(F32), axis=0, keepdims=True)

    @pl.when(r_id == pl.num_programs(0) - 1)
    def _():
        for side in range(2):
            owner = shard if side == 0 else 1 - shard
            out = s_keep if side == 0 else s_send
            one = half(owner, H)
            wide = vec[2:3, half(owner, D)]
            fc = sfc[0:1, half(owner, FF // 2)]
            flat = jnp.concatenate(
                [vec[0:1, one], vec[1:2, one], wide, sums[0:1, one], sums[1:2, one], sums[2:3, one], fc, sums[3:4, one]], axis=1
            )
            out[...] = jnp.zeros_like(out)
            for k in range(flat.shape[1] // (2 * D)):
                out[k : k + 1, :] = flat[:, k * 2 * D : (k + 1) * 2 * D]


def last_block(scal, d_own, d_oth, xb, dmid, pk_own, pk_oth, w_own, w_oth, sfc, sums):
    L, D = xb.shape
    H = D // 2
    RB = L // 2
    NP = pk_own.shape[1]
    rows = lambda n: pl.BlockSpec((RB, n), lambda r, s: (r, 0))
    const = lambda *shape: pl.BlockSpec(shape, lambda r, s: (0, 0))
    d = pl.BlockSpec((3, RB, H), lambda r, s: (0, r, 0))
    return call(
        functools.partial(last_kernel, L=L), "last_block", (2,),
        [d, d, rows(D), rows(D), whole((1, NP)), whole((1, NP)), whole((H, 3 * D)), whole((H, 3 * D)), whole(sfc.shape), whole(sums.shape)],
        [rows(D), const(8, D), const(8, 2 * D), const(8, 2 * D)],
        (sds((L, D), BF), sds((8, D), F32), sds((8, 2 * D), F32), sds((8, 2 * D), F32)),
        [pltpu.VMEM((RB, D), F32), pltpu.VMEM((RB, D), F32), pltpu.VMEM((RB, 3 * D), BF), pltpu.VMEM((8, 2 * D), F32)],
        cost(6 * L * D * D, 12e6),
        (scal, d_own, d_oth, xb, dmid, pk_own, pk_oth, w_own, w_oth, sfc, sums),
    )


def final_kernel(scal, *refs, wide):
    pos = refs[:8]
    outs = refs[8:]
    H = pos[0].shape[1]
    w = pl.program_id(0)
    k = w ^ (scal[8] >> 1)
    flip = scal[8] & 1
    for j in range(4):
        for f in range(2):
            for o, here in enumerate((w < wide, w >= wide) if len(outs) == 2 else (True,)):

                @pl.when((k == j) & (flip == f) & here)
                def _():
                    outs[o][:, :H] = pos[2 * j + f][...].astype(F32)
                    outs[o][:, H:] = pos[2 * j + 1 - f][...].astype(F32)


def final(scal, pos, out_specs, out_shape, wide=4):
    H = pos[0].shape[1]
    return call(
        functools.partial(final_kernel, wide=wide), "final", (4,), [whole((H, H))] * 8, out_specs, out_shape, [],
        cost(8 * H * H, 48 * H * H), (scal, *pos),
    )


def swap(x):
    return lax.ppermute(x, "shard", [(0, 1), (1, 0)])


def hop(x, first, second):
    pairs = []
    for rep in range(16):
        pairs.append((2 * rep, 2 * (rep ^ first)))
        pairs.append((2 * rep + 1, 2 * (rep ^ second) + 1))
    return lax.ppermute(x, ("rep", "shard"), pairs)


def gate(x, *deps):
    return lax.optimization_barrier((x, *deps))[0]


def gated(xs, *deps):
    return list(lax.optimization_barrier((*xs, *deps))[: len(xs)])


def total(*xs):
    return functools.reduce(lambda a, b: a + b, [x.astype(F32) for x in xs]).astype(BF)


class Reduce:
    def __init__(self, send, keep):
        self.H = keep.shape[1]
        self.keep = keep
        self.r1 = hop(send, 1, 2)

    def rows(self, x, a, b):
        return x[a * self.H : b * self.H]

    def hop2(self, *deps):
        self.r1 = gate(self.r1, *deps)
        send = total(self.rows(self.keep, 2, 4), self.rows(self.r1, 2, 4))
        self.r2 = hop(send, 4, 4)
        return send

    def hop3(self, *deps):
        self.r2 = gate(self.r2, *deps)
        send = total(self.rows(self.keep, 1, 2), self.rows(self.r1, 1, 2), self.rows(self.r2, 1, 2))
        self.r3 = hop(send, 2, 1)
        return send

    def hop4(self, *deps):
        self.x = total(self.rows(self.keep, 0, 1), self.rows(self.r1, 0, 1), self.rows(self.r2, 0, 1), gate(self.r3, *deps))
        self.r4 = hop(self.x, 8, 8)
        return self.x

    def hop5(self, *deps):
        p0 = total(self.x, gate(self.r4, *deps))
        self.pos = [p0] + [None] * 7
        self.pos[1] = hop(p0, 2, 1)
        self.pos[2] = hop(p0, 4, 4)
        self.pos[4] = hop(p0, 1, 2)
        return p0

    def hop6(self, *deps):
        self.pos[1] = gate(self.pos[1], *deps)
        self.pos[3] = hop(self.pos[1], 4, 4)
        self.pos[5] = hop(self.pos[1], 1, 2)

    def hop7(self, *deps):
        self.pos[2] = gate(self.pos[2], *deps)
        self.pos[6] = hop(self.pos[2], 1, 2)
        self.pos[7] = hop(self.pos[3], 1, 2)


def pair_device(
    hidden, latents, latent_pos, prefix, ln1_gain, ln1_bias, w_qkv, b_qv, w_proj, b_proj,
    ln2_gain, ln2_bias, w_fc, b_fc, w_out, b_out, cotangent,
):
    _, L, D = hidden.shape
    H = D // 2
    shard = lax.axis_index("shard").astype(jnp.int32)
    rep = lax.axis_index("rep").astype(jnp.int32)
    bit0, bit1, bit2 = rep & 1, (rep >> 1) & 1, (rep >> 2) & 1
    high = jnp.where(shard == 0, bit0, bit1)
    low = jnp.where(shard == 0, bit1, bit0)
    code = high * 4 + bit2 * 2 + low
    lead = lax.broadcasted_iota(jnp.int32, (16,), 0)
    scal = jnp.where(lead == 0, shard, jnp.where(lead == 1, prefix[0], jnp.where(lead == 8, code, 0)))
    scal = lax.dynamic_update_slice(scal, latent_pos[0].astype(jnp.int32), (2,))

    pk_own = pack([ln1_gain, ln1_bias, b_qv, b_proj, ln2_gain, ln2_bias, b_fc, b_out])
    qkv_oth = swap(w_qkv)
    pk_oth = swap(pk_own)
    hid = hidden[0]
    dz = cotangent[0]
    lat = latents[0]

    send, normed, nrm_send, xb = ln_send(scal, hid, lat, pk_own, pk_oth, w_qkv, qkv_oth)
    recv = swap(send)
    keep = own_heads(scal, normed, pk_own, pk_oth, w_qkv, qkv_oth)
    proj_oth = swap(gate(w_proj, xb))
    fc_oth = swap(gate(w_fc, xb))
    out_oth = swap(gate(w_out, xb))
    nrm_recv = swap(nrm_send)
    dz_oth = swap(gate(dz, keep))
    att_keep, att_send, lse = attn_fwd(scal, keep, recv)
    att_recv = swap(att_send)
    act_keep, act_send, gp, n2_keep, n2_send, block_out, dmid, gb, ga_keep, ga_send, sfc, sums = ffn(
        scal, att_keep, att_recv, xb, dz, pk_own, pk_oth, w_proj, proj_oth, w_fc, fc_oth, w_out, out_oth
    )
    act_recv = swap(act_send)
    ga_recv = swap(ga_send)
    gp_oth = swap(gate(gp, act_recv))
    n2_recv = swap(gate(n2_send, act_recv))
    gb_oth = swap(gate(gb, act_recv))
    s_out, k_out = grad_rows(scal, act_keep, act_recv, dz, dz_oth)
    r_out = Reduce(s_out, k_out)
    tok = k_out
    d_own = []
    d_oth = []
    for p in range(H // 128):
        a, b = attn_bwd(scal, keep, recv, ga_keep, gate(ga_recv, tok), att_keep, att_send, lse, p, 1)
        d_own.append(a)
        d_oth.append(b)
        tok = a
        if p == 0:
            s_fc, k_fc = grad_cols(scal, n2_keep, gate(n2_recv, tok), gp, gp_oth)
            r_fc = Reduce(s_fc, k_fc)
            tok = k_fc
        if p == 1:
            tok = r_out.hop2(a)
    d_own = jnp.concatenate(d_own, axis=2)
    d_oth = jnp.concatenate(d_oth, axis=2)
    e_own = swap(d_oth)
    e_oth = swap(d_own)
    tok = r_fc.hop2(d_own)
    s_c, k_c = grad_attn(scal, normed, nrm_recv, att_keep, att_send, gb, gb_oth, d_own, d_oth, gate(e_own, tok), e_oth)
    r_c = Reduce(s_c, k_c)
    tok = r_out.hop3(k_c)
    gh, glat, s_keep, s_send = last_block(scal, d_own, gate(e_own, tok), xb, dmid, pk_own, pk_oth, w_qkv, qkv_oth, sfc, sums)
    small = s_keep + swap(s_send)
    glat = glat + swap(glat)
    tok = r_out.hop4(gh)
    tok = r_fc.hop3(tok)
    tok = r_c.hop2(tok)
    small = small + hop(small, 1, 2)
    tok = r_fc.hop4(tok)
    tok = r_out.hop5(tok)
    small = small + hop(small, 2, 1)
    tok = r_c.hop3(tok)
    r_out.hop6()
    small = small + hop(small, 4, 4)
    tok = r_fc.hop5(tok)
    tok = r_c.hop4(tok)
    r_out.hop7()
    small = small + hop(small, 8, 8)
    r_fc.hop6()
    tok = r_c.hop5(tok)
    r_fc.hop7()
    g_out = final(scal, gated(r_out.pos, tok), pl.BlockSpec((H, D), lambda w, s: (w, 0)), sds((4 * H, D), F32))
    r_c.hop6(g_out)
    g_fc = final(scal, gated(r_fc.pos, g_out), pl.BlockSpec((H, D), lambda w, s: (0, w)), sds((H, 4 * D), F32))
    r_c.hop7(g_fc)
    g_qkv, g_proj = final(
        scal, r_c.pos, [pl.BlockSpec((H, D), lambda w, s: (0, jnp.minimum(w, 2))), pl.BlockSpec((H, D), lambda w, s: (0, 0))],
        (sds((H, 3 * D), F32), sds((H, D), F32)), 3,
    )
    flat = small[:3].reshape(-1)
    cuts = [0]
    for v in (ln1_gain, ln1_bias, b_qv, b_proj, ln2_gain, ln2_bias, b_fc, b_out):
        cuts.append(cuts[-1] + v.shape[0])
    vecs = [flat[cuts[i] : cuts[i + 1]] for i in range(8)]
    return (
        block_out[None], gh[None], glat[None, :6], vecs[0], vecs[1], g_qkv, vecs[2], g_proj, vecs[3],
        vecs[4], vecs[5], g_fc, vecs[6], g_out, vecs[7],
    )


def layer_norm(values, norm_gain, norm_shift):
    average = jnp.mean(values, axis=-1, keepdims=True)
    centered = values - average
    variance = jnp.mean(centered * centered, axis=-1, keepdims=True)
    return centered * lax.rsqrt(variance + norm_epsilon) * norm_gain + norm_shift


def gelu_tanh(values):
    return (
        0.5
        * values
        * (1.0 + jnp.tanh(gelu_root * (values + gelu_cubic * values * values * values)))
    )


def head_scores(query_one, key_one, query_pos, key_pos, prefix_one, score_scale):
    scores = (
        jnp.einsum("qhe,khe->hqk", query_one, key_one, preferred_element_type=jnp.float32)
        * score_scale
    )
    causal = (key_pos[None, :] <= query_pos[:, None])[None]
    in_prefix = (key_pos < prefix_one)[None, None, :]
    return jnp.where(causal | in_prefix, scores, masked_score)


def per_device(
    hidden,
    latents,
    latent_pos,
    prefix,
    ln1_gain,
    ln1_bias,
    w_qkv,
    b_qv,
    w_proj,
    b_proj,
    ln2_gain,
    ln2_bias,
    w_fc,
    b_fc,
    w_out,
    b_out,
    cotangent,
):
    seq_count, local_len, model_width = hidden.shape
    head_dim = model_width // HEADS
    score_scale = head_dim ** (-0.5)
    row_start = lax.axis_index("shard") * local_len
    gathered = (
        lax.all_gather(ln1_gain, "shard", axis=0, tiled=True),
        lax.all_gather(ln1_bias, "shard", axis=0, tiled=True),
        lax.all_gather(w_qkv, "shard", axis=0, tiled=True),
        lax.all_gather(b_qv, "shard", axis=0, tiled=True),
        lax.all_gather(w_proj, "shard", axis=0, tiled=True),
        lax.all_gather(b_proj, "shard", axis=0, tiled=True),
        lax.all_gather(ln2_gain, "shard", axis=0, tiled=True),
        lax.all_gather(ln2_bias, "shard", axis=0, tiled=True),
        lax.all_gather(w_fc, "shard", axis=0, tiled=True),
        lax.all_gather(b_fc, "shard", axis=0, tiled=True),
        lax.all_gather(w_out, "shard", axis=0, tiled=True),
        lax.all_gather(b_out, "shard", axis=0, tiled=True),
    )
    (
        full_ln1_gain,
        full_ln1_bias,
        full_qkv,
        full_b_qv,
        full_proj,
        full_b_proj,
        full_ln2_gain,
        full_ln2_bias,
        full_fc,
        full_b_fc,
        complete_output,
        full_b_out,
    ) = gathered
    row_ids = row_start + jnp.arange(local_len, dtype=jnp.int32)
    latent_matches = row_ids[None, :, None] == latent_pos[:, None, :]
    positioned_rows = jnp.einsum(
        "ety,eyw->etw",
        latent_matches.astype(jnp.bfloat16),
        latents,
        preferred_element_type=jnp.float32,
    )
    replaced = jnp.any(latent_matches, axis=-1)[..., None]
    block_in = jnp.where(replaced, positioned_rows, hidden.astype(jnp.float32)).reshape(
        -1, model_width
    )
    normed, back_norm_one = jax.vjp(
        layer_norm, block_in, full_ln1_gain.astype(jnp.float32), full_ln1_bias.astype(jnp.float32)
    )
    normed_low = normed.astype(jnp.bfloat16)
    bias_full = jnp.concatenate(
        [
            full_b_qv[:model_width].astype(jnp.float32),
            jnp.zeros((model_width,), jnp.float32),
            full_b_qv[model_width:].astype(jnp.float32),
        ]
    )
    projected = (
        jnp.dot(normed_low, full_qkv, preferred_element_type=jnp.float32) + bias_full
    ).astype(jnp.bfloat16)
    query_heads = projected[:, :model_width].reshape(seq_count, local_len, HEADS, head_dim)
    key_local = projected[:, model_width : 2 * model_width].reshape(
        seq_count, local_len, model_width
    )
    value_local = projected[:, 2 * model_width :].reshape(seq_count, local_len, model_width)
    key_full, value_full = (
        lax.all_gather(key_local, "shard", axis=1, tiled=True),
        lax.all_gather(value_local, "shard", axis=1, tiled=True),
    )
    full_len = key_full.shape[1]
    key_heads = key_full.reshape(seq_count, full_len, HEADS, head_dim)
    value_heads = value_full.reshape(seq_count, full_len, HEADS, head_dim)
    key_pos_all = jnp.arange(full_len, dtype=jnp.int32)

    def forward_seq(items):
        query_one, key_one, value_one, prefix_one = items
        scores = head_scores(query_one, key_one, row_ids, key_pos_all, prefix_one, score_scale)
        row_peak = jnp.max(scores, axis=-1, keepdims=True)
        single_logsumexp = row_peak + jnp.log(
            jnp.sum(jnp.exp(scores - row_peak), axis=-1, keepdims=True)
        )
        probs_low = jnp.exp(scores - single_logsumexp).astype(jnp.bfloat16)
        mixed = jnp.einsum("hqk,khe->qhe", probs_low, value_one, preferred_element_type=jnp.float32)
        return (mixed.astype(jnp.bfloat16), single_logsumexp)

    attended_heads, log_total = lax.map(forward_seq, (query_heads, key_heads, value_heads, prefix))
    attended = attended_heads.reshape(-1, model_width)
    middle = (
        block_in
        + jnp.dot(attended, full_proj, preferred_element_type=jnp.float32)
        + full_b_proj.astype(jnp.float32)
    )
    normed_two, back_norm_two = jax.vjp(
        layer_norm, middle, full_ln2_gain.astype(jnp.float32), full_ln2_bias.astype(jnp.float32)
    )
    normed_two_low = normed_two.astype(jnp.bfloat16)
    pre_act = jnp.dot(
        normed_two_low, full_fc, preferred_element_type=jnp.float32
    ) + full_b_fc.astype(jnp.float32)
    activated, back_gelu = jax.vjp(gelu_tanh, pre_act)
    activated_low = activated.astype(jnp.bfloat16)
    block_out = (
        middle
        + jnp.dot(activated_low, complete_output, preferred_element_type=jnp.float32)
        + full_b_out.astype(jnp.float32)
    )
    block_out = block_out.reshape(seq_count, local_len, model_width).astype(jnp.bfloat16)
    back_qkv, back_proj, back_fc, back_out = (
        lax.all_gather(w_qkv, "shard", axis=0, tiled=True),
        lax.all_gather(w_proj, "shard", axis=0, tiled=True),
        lax.all_gather(w_fc, "shard", axis=0, tiled=True),
        lax.all_gather(w_out, "shard", axis=0, tiled=True),
    )
    grad_top = cotangent.reshape(-1, model_width)
    grad_w_out = jnp.einsum(
        "nf,nd->fd", activated_low, grad_top, preferred_element_type=jnp.float32
    )
    grad_b_out = jnp.sum(grad_top.astype(jnp.float32), axis=0)
    grad_act = jnp.einsum("nd,fd->nf", grad_top, back_out, preferred_element_type=jnp.float32)
    (grad_pre,) = back_gelu(grad_act)
    grad_pre_low = grad_pre.astype(jnp.bfloat16)
    grad_w_fc = jnp.einsum(
        "nd,nf->df", normed_two_low, grad_pre_low, preferred_element_type=jnp.float32
    )
    grad_b_fc = jnp.sum(grad_pre_low.astype(jnp.float32), axis=0)
    grad_normed_two = jnp.einsum(
        "nf,df->nd", grad_pre_low, back_fc, preferred_element_type=jnp.float32
    )
    grad_mid_norm, grad_ln2_gain, grad_ln2_bias = back_norm_two(grad_normed_two)
    grad_mid = grad_top.astype(jnp.float32) + grad_mid_norm
    grad_branch_low = grad_mid.astype(jnp.bfloat16)
    grad_w_proj = jnp.einsum(
        "nd,ne->de", attended, grad_branch_low, preferred_element_type=jnp.float32
    )
    grad_b_proj = jnp.sum(grad_branch_low.astype(jnp.float32), axis=0)
    grad_att = jnp.einsum(
        "ne,de->nd", grad_branch_low, back_proj, preferred_element_type=jnp.float32
    )
    grad_att_low = grad_att.astype(jnp.bfloat16).reshape(seq_count, local_len, HEADS, head_dim)

    def backward_sequence(items):
        query_one, key_one, value_one, prefix_one, single_logsumexp, upstream = items
        scores = head_scores(query_one, key_one, row_ids, key_pos_all, prefix_one, score_scale)
        attn_probs = jnp.exp(scores - single_logsumexp)
        grad_value_one = jnp.einsum(
            "hqk,qhe->khe",
            attn_probs.astype(jnp.bfloat16),
            upstream,
            preferred_element_type=jnp.float32,
        )
        grad_probs = jnp.einsum(
            "qhe,khe->hqk", upstream, value_one, preferred_element_type=jnp.float32
        )
        delta_one = jnp.sum(grad_probs * attn_probs, axis=-1, keepdims=True)
        grad_scores = (attn_probs * (grad_probs - delta_one)).astype(jnp.bfloat16)
        grad_query_one = (
            jnp.einsum("hqk,khe->qhe", grad_scores, key_one, preferred_element_type=jnp.float32)
            * score_scale
        )
        grad_key_one = (
            jnp.einsum("hqk,qhe->khe", grad_scores, query_one, preferred_element_type=jnp.float32)
            * score_scale
        )
        return (
            grad_query_one,
            grad_key_one.reshape(full_len, model_width),
            grad_value_one.reshape(full_len, model_width),
        )

    grad_query, grad_key_all, grad_value_all = lax.map(
        backward_sequence, (query_heads, key_heads, value_heads, prefix, log_total, grad_att_low)
    )
    grad_key_own, grad_value_own = (
        lax.psum_scatter(
            grad_key_all.astype(jnp.bfloat16), "shard", scatter_dimension=1, tiled=True
        ).astype(jnp.float32),
        lax.psum_scatter(
            grad_value_all.astype(jnp.bfloat16), "shard", scatter_dimension=1, tiled=True
        ).astype(jnp.float32),
    )
    grad_query_low = grad_query.reshape(-1, model_width).astype(jnp.bfloat16)
    grad_key_low = grad_key_own.reshape(-1, model_width).astype(jnp.bfloat16)
    grad_value_low = grad_value_own.reshape(-1, model_width).astype(jnp.bfloat16)
    grad_projected = jnp.concatenate([grad_query_low, grad_key_low, grad_value_low], axis=1)
    grad_b_qv = jnp.concatenate(
        [
            jnp.sum(grad_query_low.astype(jnp.float32), axis=0),
            jnp.sum(grad_value_low.astype(jnp.float32), axis=0),
        ]
    )
    grad_w_qkv = jnp.einsum(
        "nd,ne->de", normed_low, grad_projected, preferred_element_type=jnp.float32
    )
    grad_normed = jnp.einsum(
        "ne,de->nd", grad_projected, back_qkv, preferred_element_type=jnp.float32
    )
    grad_in_norm, grad_ln1_gain, grad_ln1_bias = back_norm_one(grad_normed)
    block_gradient = (grad_mid + grad_in_norm).reshape(seq_count, local_len, model_width)
    latent_terms = jnp.einsum(
        "inv,inz->ivz",
        latent_matches.astype(jnp.float32),
        block_gradient,
        precision=lax.Precision.HIGHEST,
    )
    grad_latents = lax.psum(latent_terms, "shard")
    grad_hidden = jnp.where(replaced, 0.0, block_gradient).astype(jnp.bfloat16)
    shares = (
        lax.psum_scatter(
            grad_ln1_gain.astype(jnp.bfloat16), "shard", scatter_dimension=0, tiled=True
        ).astype(jnp.float32),
        lax.psum_scatter(
            grad_ln1_bias.astype(jnp.bfloat16), "shard", scatter_dimension=0, tiled=True
        ).astype(jnp.float32),
        lax.psum_scatter(
            grad_w_qkv.astype(jnp.bfloat16), "shard", scatter_dimension=0, tiled=True
        ).astype(jnp.float32),
        lax.psum_scatter(
            grad_b_qv.astype(jnp.bfloat16), "shard", scatter_dimension=0, tiled=True
        ).astype(jnp.float32),
        lax.psum_scatter(
            grad_w_proj.astype(jnp.bfloat16), "shard", scatter_dimension=0, tiled=True
        ).astype(jnp.float32),
        lax.psum_scatter(
            grad_b_proj.astype(jnp.bfloat16), "shard", scatter_dimension=0, tiled=True
        ).astype(jnp.float32),
        lax.psum_scatter(
            grad_ln2_gain.astype(jnp.bfloat16), "shard", scatter_dimension=0, tiled=True
        ).astype(jnp.float32),
        lax.psum_scatter(
            grad_ln2_bias.astype(jnp.bfloat16), "shard", scatter_dimension=0, tiled=True
        ).astype(jnp.float32),
        lax.psum_scatter(
            grad_w_fc.astype(jnp.bfloat16), "shard", scatter_dimension=0, tiled=True
        ).astype(jnp.float32),
        lax.psum_scatter(
            grad_b_fc.astype(jnp.bfloat16), "shard", scatter_dimension=0, tiled=True
        ).astype(jnp.float32),
        lax.psum_scatter(
            grad_w_out.astype(jnp.bfloat16), "shard", scatter_dimension=0, tiled=True
        ).astype(jnp.float32),
        lax.psum_scatter(
            grad_b_out.astype(jnp.bfloat16), "shard", scatter_dimension=0, tiled=True
        ).astype(jnp.float32),
    )
    summed = (
        lax.psum(shares[0].astype(jnp.bfloat16), "rep").astype(jnp.float32),
        lax.psum(shares[1].astype(jnp.bfloat16), "rep").astype(jnp.float32),
        lax.psum(shares[2].astype(jnp.bfloat16), "rep").astype(jnp.float32),
        lax.psum(shares[3].astype(jnp.bfloat16), "rep").astype(jnp.float32),
        lax.psum(shares[4].astype(jnp.bfloat16), "rep").astype(jnp.float32),
        lax.psum(shares[5].astype(jnp.bfloat16), "rep").astype(jnp.float32),
        lax.psum(shares[6].astype(jnp.bfloat16), "rep").astype(jnp.float32),
        lax.psum(shares[7].astype(jnp.bfloat16), "rep").astype(jnp.float32),
        lax.psum(shares[8].astype(jnp.bfloat16), "rep").astype(jnp.float32),
        lax.psum(shares[9].astype(jnp.bfloat16), "rep").astype(jnp.float32),
        lax.psum(shares[10].astype(jnp.bfloat16), "rep").astype(jnp.float32),
        lax.psum(shares[11].astype(jnp.bfloat16), "rep").astype(jnp.float32),
    )
    (
        total_ln1_gain,
        total_ln1_bias,
        total_w_qkv,
        total_b_qv,
        total_w_proj,
        total_b_proj,
        total_ln2_gain,
        total_ln2_bias,
        total_w_fc,
        total_b_fc,
        total_w_out,
        total_b_out,
    ) = summed
    return (
        block_out,
        grad_hidden,
        grad_latents,
        total_ln1_gain,
        total_ln1_bias,
        total_w_qkv,
        total_b_qv,
        total_w_proj,
        total_b_proj,
        total_ln2_gain,
        total_ln2_bias,
        total_w_fc,
        total_b_fc,
        total_w_out,
        total_b_out,
    )


def solution(mesh):
    sizes = dict(mesh.shape)
    paired = sizes["rep"] == 16 and sizes["shard"] == 2
    body = pair_device if paired else per_device
    in_specs = (
        P("rep", "shard", None),
        P("rep", None, None),
        P("rep", None),
        P("rep"),
        P("shard"),
        P("shard"),
        P("shard", None),
        P("shard"),
        P("shard", None),
        P("shard"),
        P("shard"),
        P("shard"),
        P("shard", None),
        P("shard"),
        P("shard", None),
        P("shard"),
        P("rep", "shard", None),
    )
    out_specs = (
        P("rep", "shard", None),
        P("rep", "shard", None),
        P("rep", None, None),
        P("shard"),
        P("shard"),
        P("shard", None),
        P("shard"),
        P("shard", None),
        P("shard"),
        P("shard"),
        P("shard"),
        P("shard", None),
        P("shard"),
        P("shard", None),
        P("shard"),
    )
    return jax.shard_map(
        body, mesh=mesh, in_specs=in_specs, out_specs=out_specs, check_vma=False
    )
```

```python
import functools
import jax
import jax.numpy as jnp
from jax import lax
from jax.experimental import pallas as pl
from jax.experimental.pallas import tpu as pltpu
from jax.sharding import PartitionSpec as P

HEADS = 12
F32 = jnp.float32
BF = jnp.bfloat16

norm_epsilon = 1e-05
gelu_root = 0.7978845608028654
gelu_cubic = 0.044715
masked_score = -1e30
LOG2E = 1.4426950408889634


def dot_nt(a, b):
    return lax.dot_general(a, b, (((1,), (1,)), ((), ())), preferred_element_type=F32)


def dot_nn(a, b):
    return lax.dot_general(a, b, (((1,), (0,)), ((), ())), preferred_element_type=F32)


def dot_tn(a, b):
    return lax.dot_general(a, b, (((0,), (0,)), ((), ())), preferred_element_type=F32)


def params(semantics=None, mb=16):
    return pltpu.CompilerParams(dimension_semantics=semantics, vmem_limit_bytes=mb * 1024 * 1024)


def cost(flops, nbytes, trans=0):
    return pl.CostEstimate(flops=1, bytes_accessed=1, transcendentals=0)


def whole(shape):
    return pl.BlockSpec(shape, lambda *_: (0,) * len(shape), pipeline_mode=pl.Buffered(1))


def both(own, oth, shard, a, n):
    o = own[0:1, a : a + n].astype(F32)
    t = oth[0:1, a : a + n].astype(F32)
    first = jnp.where(shard == 0, o, t)
    second = jnp.where(shard == 0, t, o)
    return jnp.concatenate([first, second], axis=1)


def half(i, n):
    return pl.ds(pl.multiple_of(i * n, n), n)


def call(kernel, name, grid, in_specs, out_specs, out_shape, scratch, est, args, mb=16):
    return pl.pallas_call(
        kernel,
        out_shape=out_shape,
        grid_spec=pltpu.PrefetchScalarGridSpec(
            num_scalar_prefetch=1, grid=grid, in_specs=in_specs, out_specs=out_specs, scratch_shapes=scratch
        ),
        compiler_params=params(("arbitrary",), mb),
        cost_estimate=est,
        name=name,
    )(*args)


sds = jax.ShapeDtypeStruct


def pack(vecs):
    n = sum(v.shape[0] for v in vecs)
    at = 0
    out = []
    for v in vecs:
        out.append(jnp.pad(v, (at, n - at - v.shape[0])))
        at += v.shape[0]
    return functools.reduce(jnp.add, out)[None, :]


def qv_bias(pk_own, pk_oth, shard, which, heads):
    H = pk_own.shape[1] // 12
    a = pk_own[0:1, 2 * H : 4 * H].astype(F32)
    b = pk_oth[0:1, 2 * H : 4 * H].astype(F32)
    src = jnp.where(shard == which, a, b)
    return jnp.where(heads == 0, src[:, :H], src[:, H:])


def project(n, ws, pk_own, pk_oth, shard, heads, out):
    H = ws.shape[0] // 2
    for j in range(3):
        y = dot_nn(n, ws[:, j * H : (j + 1) * H])
        if j != 1:
            y = y + qv_bias(pk_own, pk_oth, shard, j // 2, heads)
        out[:, j * H : (j + 1) * H] = y.astype(BF)


def ln_send_kernel(
    scal, hid, lat, pk_own, pk_oth, qo, ko, vo, qt, kt, vt, send, normed, nrm_send, xb, xs, ns, ws, *, L
):
    r = pl.program_id(0)
    RB, D = hid.shape
    H = D // 2
    shard = scal[0]

    @pl.when(r == 0)
    def _():
        for j, (o, t) in enumerate(((qo, qt), (ko, kt), (vo, vt))):
            ws[half(shard, H), j * H : (j + 1) * H] = o[...]
            ws[half(1 - shard, H), j * H : (j + 1) * H] = t[...]

    xs[...] = hid[...].astype(F32)
    row0 = shard * L + r * RB
    for c in range(6):
        rel = scal[2 + c] - row0

        @pl.when((rel >= 0) & (rel < RB))
        def _():
            xs[pl.ds(rel, 1), :] = lat[c : c + 1, :].astype(F32)

    g = both(pk_own, pk_oth, shard, 0, H)
    b = both(pk_own, pk_oth, shard, H, H)
    x = xs[...]
    xb[...] = x.astype(BF)
    cen = x - jnp.mean(x, axis=1, keepdims=True)
    var = jnp.mean(cen * cen, axis=1, keepdims=True)
    n = (cen * lax.rsqrt(var + norm_epsilon) * g + b).astype(BF)
    ns[...] = n
    normed[...] = n
    nrm_send[...] = ns[:, half(1 - shard, H)]
    project(n, ws, pk_own, pk_oth, shard, 1 - shard, send)


def ln_send(scal, hid, lat, pk_own, pk_oth, w_own, w_oth):
    L, D = hid.shape
    H = D // 2
    RB = L // 2
    NP = pk_own.shape[1]
    rows = lambda n: pl.BlockSpec((RB, n), lambda r, s: (r, 0))
    w = [
        pl.BlockSpec((H, H), lambda r, s, j=j: (0, 2 * j + 1 - s[0]), pipeline_mode=pl.Buffered(1)) for j in range(3)
    ]
    return call(
        functools.partial(ln_send_kernel, L=L), "ln_send", (2,),
        [rows(D), whole(lat.shape), whole((1, NP)), whole((1, NP))] + w + w,
        [rows(3 * H), rows(D), rows(H), rows(D)],
        (sds((L, 3 * H), BF), sds((L, D), BF), sds((L, H), BF), sds((L, D), BF)),
        [pltpu.VMEM((RB, D), F32), pltpu.VMEM((RB, D), BF), pltpu.VMEM((D, 3 * H), BF)],
        cost(6 * L * D * H, 6e6),
        (scal, hid, lat, pk_own, pk_oth, w_own, w_own, w_own, w_oth, w_oth, w_oth),
    )


def own_kernel(scal, normed, pk_own, pk_oth, qo, ko, vo, qt, kt, vt, keep, ws):
    H = qo.shape[0]
    shard = scal[0]

    @pl.when(pl.program_id(0) == 0)
    def _():
        for j, (o, t) in enumerate(((qo, qt), (ko, kt), (vo, vt))):
            ws[half(shard, H), j * H : (j + 1) * H] = o[...]
            ws[half(1 - shard, H), j * H : (j + 1) * H] = t[...]

    project(normed[...], ws, pk_own, pk_oth, shard, shard, keep)


def own_heads(scal, normed, pk_own, pk_oth, w_own, w_oth):
    L, D = normed.shape
    H = D // 2
    RB = L // 2
    NP = pk_own.shape[1]
    rows = lambda n: pl.BlockSpec((RB, n), lambda r, s: (r, 0))
    w = [pl.BlockSpec((H, H), lambda r, s, j=j: (0, 2 * j + s[0]), pipeline_mode=pl.Buffered(1)) for j in range(3)]
    return call(
        own_kernel, "own_heads", (2,),
        [rows(D), whole((1, NP)), whole((1, NP))] + w + w, rows(3 * H), sds((L, 3 * H), BF),
        [pltpu.VMEM((D, 3 * H), BF)],
        cost(6 * L * D * H, 4e6),
        (scal, normed, pk_own, pk_oth, w_own, w_own, w_own, w_oth, w_oth, w_oth),
    )


def join(dst, own, oth, shard):
    L = own.shape[0]
    dst[half(shard, L), :] = own[...]
    dst[half(1 - shard, L), :] = oth[...]


def attn_fwd_kernel(scal, qa, ka, va, qb, kb_, vb, o_keep, o_send, lse_ref, qs, ks, vs, os_, stat, *, L, RB):
    p_id = pl.program_id(0)
    shard = scal[0]
    pfx = scal[1]
    join(qs, qa, qb, shard)
    join(ks, ka, kb_, shard)
    join(vs, va, vb, shard)
    lane = lax.broadcasted_iota(jnp.int32, (RB, 128), 1)
    c = 0.125 * LOG2E
    HB = L // RB

    for r in range(2 * HB):
        q = qs[r * RB : (r + 1) * RB, :]
        outs = []
        for hh in range(2):
            sel = (lane < 64) if hh == 0 else (lane >= 64)
            qm = jnp.where(sel, q, jnp.zeros_like(q))
            pieces = []
            if r >= HB:
                pieces.append((dot_nt(qm, ks[0:L, :]) * c, vs[0:L, :]))
            for kb in range(HB) if r < HB else range(HB, r + 1):
                s = dot_nt(qm, ks[kb * RB : (kb + 1) * RB, :]) * c
                if kb >= r:
                    col = lax.broadcasted_iota(jnp.int32, (RB, RB), 1) + kb * RB
                    row = lax.broadcasted_iota(jnp.int32, (RB, RB), 0) + r * RB
                    keep = (col <= row) | (col < pfx) if r < HB else (col <= row)
                    s = jnp.where(keep, s, masked_score)
                pieces.append((s, vs[kb * RB : (kb + 1) * RB, :]))
            m = functools.reduce(jnp.maximum, [jnp.max(s, axis=1, keepdims=True) for s, _ in pieces])
            total = jnp.zeros((RB, 1), F32)
            o = jnp.zeros((RB, 128), F32)
            for s, v in pieces:
                p = jnp.exp2(s - m)
                total = total + jnp.sum(p, axis=1, keepdims=True)
                o = o + dot_nn(p.astype(BF), v)
            outs.append(o * (1.0 / total))
            lse = m + jnp.log2(total)
            here = lane == p_id * 2 + hh
            stat[r * RB : (r + 1) * RB, :] = jnp.where(here, lse, stat[r * RB : (r + 1) * RB, :])
        os_[r * RB : (r + 1) * RB, :] = jnp.where(lane < 64, outs[0], outs[1]).astype(BF)

    o_keep[...] = os_[half(shard, L), :]
    o_send[...] = os_[half(1 - shard, L), :]

    @pl.when(p_id == pl.num_programs(0) - 1)
    def _():
        lse_ref[...] = stat[...].T[0:8, :]


def attn_fwd(scal, keep, recv):
    L, W = keep.shape
    H = W // 3
    NP = H // 128
    spec = lambda off: pl.BlockSpec((L, 128), lambda p, s: (0, p + off))
    seq = pltpu.VMEM((2 * L, 128), BF)
    o = sds((L, H), BF)
    return call(
        functools.partial(attn_fwd_kernel, L=L, RB=256), "attn_fwd", (NP,),
        [spec(0), spec(NP), spec(2 * NP)] * 2,
        [spec(0), spec(0), pl.BlockSpec((8, 2 * L), lambda p, s: (0, 0))],
        (o, o, sds((8, 2 * L), F32)),
        [seq, seq, seq, seq, pltpu.VMEM((2 * L, 128), F32)],
        cost(12e9, 4e6, 6e6),
        (scal, keep, keep, keep, recv, recv, recv),
    )


def attn_bwd_kernel(
    scal, qa, ka, va, qb, kb_, vb, ga, gb, aa, ab, lse_ref, d_own, d_oth, qs, ks, vs, gs, as_, dks, dvs, dqt, *, L, KB, p0
):
    shard = scal[0]
    pfx = scal[1]
    join(qs, qa, qb, shard)
    join(ks, ka, kb_, shard)
    join(vs, va, vb, shard)
    join(gs, ga, gb, shard)
    join(as_, aa, ab, shard)
    S = 2 * L
    c = 0.125 * LOG2E
    lane = lax.broadcasted_iota(jnp.int32, (S, 128), 1)
    q = qs[...]
    do = gs[...]
    z = jnp.zeros_like(q)
    qm = [jnp.where(lane < 64, q, z), jnp.where(lane >= 64, q, z)]
    dm = [jnp.where(lane < 64, do, z), jnp.where(lane >= 64, do, z)]
    prod = do.astype(F32) * as_[...].astype(F32)
    hi = prod.astype(BF)
    lo = (prod - hi.astype(F32)).astype(BF)
    head = lax.broadcasted_iota(jnp.int32, (16, 128), 0)
    plane = lax.broadcasted_iota(jnp.int32, (16, 128), 1)
    pick = jnp.where((plane >= head * 64) & (plane < head * 64 + 64), 1.0, 0.0).astype(BF)
    delta = dot_nt(pick, hi) + dot_nt(pick, lo)
    hb = (pl.program_id(0) + p0) * 2
    lse = [lse_ref[pl.ds(hb + hh, 1), :] for hh in range(2)]
    dl = [delta[hh : hh + 1, :] for hh in range(2)]
    dqt[...] = jnp.zeros_like(dqt)

    for kb in range(S // KB):
        rows = slice(kb * KB, (kb + 1) * KB)
        k = ks[rows, :]
        v = vs[rows, :]
        kt = k.T
        dk = None
        dv = None
        spans = [(0, L), (L, S)] if kb * KB < L else [(kb * KB, S)]
        for q0, q1 in spans:
            mask = None
            if q0 <= kb * KB:
                key = lax.broadcasted_iota(jnp.int32, (KB, q1 - q0), 0) + kb * KB
                qry = lax.broadcasted_iota(jnp.int32, (KB, q1 - q0), 1) + q0
                mask = (key <= qry) | (key < pfx) if q1 <= L else key <= qry
            for hh in range(2):
                st = dot_nt(k, qm[hh][q0:q1, :]) * c
                if mask is not None:
                    st = jnp.where(mask, st, masked_score)
                pt = jnp.exp2(st - lse[hh][:, q0:q1])
                dpt = dot_nt(v, dm[hh][q0:q1, :])
                dst = (pt * (dpt - dl[hh][:, q0:q1])).astype(BF)
                a = dot_nn(pt.astype(BF), dm[hh][q0:q1, :])
                b = dot_nn(dst, qm[hh][q0:q1, :])
                dv = a if dv is None else dv + a
                dk = b if dk is None else dk + b
                dqt[hh * 64 : (hh + 1) * 64, q0:q1] += dot_nn(kt[hh * 64 : (hh + 1) * 64, :], dst)
        dks[rows, :] = (dk * 0.125).astype(BF)
        dvs[rows, :] = dv.astype(BF)

    gs[...] = (dqt[...].T * 0.125).astype(BF)
    for j, src in enumerate((gs, dks, dvs)):
        d_own[j] = src[half(shard, L), :]
        d_oth[j] = src[half(1 - shard, L), :]


def attn_bwd(scal, keep, recv, ga_keep, ga_recv, att_keep, att_send, lse, p0, count):
    L, W = keep.shape
    H = W // 3
    NP = H // 128
    spec = lambda off: pl.BlockSpec((L, 128), lambda p, s: (0, p + off))
    seq = pltpu.VMEM((2 * L, 128), BF)
    o = sds((3, L, count * 128), BF)
    ospec = pl.BlockSpec((3, L, 128), lambda p, s: (0, 0, p))
    share = count / NP
    return call(
        functools.partial(attn_bwd_kernel, L=L, KB=256, p0=p0), "attn_bwd", (count,),
        [spec(p0), spec(NP + p0), spec(2 * NP + p0)] * 2 + [spec(p0)] * 4 + [pl.BlockSpec((8, 2 * L), lambda p, s: (0, 0))],
        [ospec, ospec], (o, o),
        [seq] * 7 + [pltpu.VMEM((128, 2 * L), F32)],
        cost(24e9 * share, 8e6 * share, 6e6 * share),
        (scal, keep, keep, keep, recv, recv, recv, ga_keep, ga_recv, att_keep, att_send, lse),
    )


def ffn_kernel(
    scal, ak, ar, xb, dz, pk_own, pk_oth, wp_own, wp_oth, wf_own, wf_oth, wo_own, wo_oth,
    act_keep, act_send, gp, n2_keep, n2_send, out, dmid, gb, ga_keep, ga_send, sfc, sums,
    ns, mid, yacc, gacc, wfs, wos, as_, *, T,
):
    t = pl.program_id(0)
    last = pl.num_programs(0) - 1
    NH = pl.num_programs(0) // 2
    shard = scal[0]
    L, D = xb.shape
    H = D // 2
    FH = wo_own.shape[0] * NH
    o_bp, o_g2, o_b2, o_bf = 4 * H, 5 * H, 6 * H, 7 * H
    o_bo = 11 * H
    RB = L // 4

    @pl.when(t == 0)
    def _():
        g = both(pk_own, pk_oth, shard, o_g2, H)
        b = both(pk_own, pk_oth, shard, o_b2, H)
        bp = both(pk_own, pk_oth, shard, o_bp, H)
        mid[...] = dot_nn(ak[...], wp_own[...]) + dot_nn(ar[...], wp_oth[...])
        for i in range(4):
            rows = slice(i * RB, (i + 1) * RB)
            m = mid[rows, :] + xb[rows, :].astype(F32) + bp
            mid[rows, :] = m
            cen = m - jnp.mean(m, axis=1, keepdims=True)
            var = jnp.mean(cen * cen, axis=1, keepdims=True)
            ns[rows, :] = (cen * lax.rsqrt(var + norm_epsilon) * g + b).astype(BF)
        n2_keep[...] = ns[:, half(shard, H)]
        n2_send[...] = ns[:, half(1 - shard, H)]
        yacc[...] = jnp.zeros_like(yacc)
        gacc[...] = jnp.zeros_like(gacc)

    wfs[half(shard, H), :] = wf_own[...]
    wfs[half(1 - shard, H), :] = wf_oth[...]

    @pl.when(t < NH)
    def _():
        wos[...] = wo_own[...]

    @pl.when(t >= NH)
    def _():
        wos[...] = wo_oth[...]

    at = pl.ds(pl.multiple_of(o_bf + lax.rem(t, NH) * T, 128), T)
    bias = jnp.where(t < NH, pk_own[0:1, at].astype(F32), pk_oth[0:1, at].astype(F32))
    CB = T // 2
    for i in range(2):
        cols = slice(i * CB, (i + 1) * CB)
        u = dot_nn(ns[...], wfs[:, cols]) + bias[:, cols]
        ga = dot_nt(dz[...], wos[cols, :])
        u2 = u * u
        th = jnp.tanh(u * (gelu_root + (gelu_root * gelu_cubic) * u2))
        hp = 0.5 + 0.5 * th
        av = u * hp
        slope = hp + av * ((1.0 - th) * (gelu_root + (3.0 * gelu_root * gelu_cubic) * u2))
        as_[:, cols] = av.astype(BF)
        g = (ga * slope).astype(BF)
        gp[:, cols] = g
        total = jnp.sum(g.astype(F32), axis=0, keepdims=True)
        sfc[:, cols] = jnp.broadcast_to(total, (sfc.shape[0], CB))
    yacc[...] += dot_nn(as_[...], wos[...])
    gacc[...] += dot_nt(gp[...], wfs[...])

    @pl.when(t < NH)
    def _():
        act_keep[...] = as_[...]

    @pl.when(t >= NH)
    def _():
        act_send[...] = as_[...]

    @pl.when(t == last)
    def _():
        g2 = both(pk_own, pk_oth, shard, o_g2, H)
        bo = both(pk_own, pk_oth, shard, o_bo, H)
        sums[...] = jnp.zeros_like(sums)
        for i in range(4):
            rows = slice(i * RB, (i + 1) * RB)
            m = mid[rows, :]
            out[rows, :] = (yacc[rows, :] + m + bo).astype(BF)
            gn = gacc[rows, :]
            cen = m - jnp.mean(m, axis=1, keepdims=True)
            r = lax.rsqrt(jnp.mean(cen * cen, axis=1, keepdims=True) + norm_epsilon)
            n = cen * r
            e = gn * g2
            dzv = dz[rows, :].astype(F32)
            g = dzv + r * (e - jnp.mean(e, axis=1, keepdims=True) - n * jnp.mean(e * n, axis=1, keepdims=True))
            dmid[rows, :] = g
            gbv = g.astype(BF)
            gb[rows, :] = gbv
            sums[0:1, :] += jnp.sum(gbv.astype(F32), axis=0, keepdims=True)
            sums[1:2, :] += jnp.sum(gn * n, axis=0, keepdims=True)
            sums[2:3, :] += jnp.sum(gn, axis=0, keepdims=True)
            sums[3:4, :] += jnp.sum(dzv, axis=0, keepdims=True)
        ga_keep[...] = dot_nt(gb[...], wp_own[...]).astype(BF)
        ga_send[...] = dot_nt(gb[...], wp_oth[...]).astype(BF)


def ffn(scal, ak, ar, xb, dz, pk_own, pk_oth, wp_own, wp_oth, wf_own, wf_oth, wo_own, wo_oth):
    L, D = xb.shape
    H = D // 2
    FH = wo_own.shape[0]
    T = 512
    NH = FH // T
    NP = pk_own.shape[1]
    tile = lambda t, s: jnp.where(t < NH, s[0] * NH + t, (1 - s[0]) * NH + t - NH)
    first = lambda t: jnp.minimum(t, NH - 1)
    second = lambda t: jnp.maximum(t - NH, 0)
    const = lambda *shape: pl.BlockSpec(shape, lambda t, s: (0,) * len(shape))
    wf = pl.BlockSpec((H, T), lambda t, s: (0, tile(t, s)))
    return call(
        functools.partial(ffn_kernel, T=T), "ffn", (2 * NH,),
        [whole((L, H)), whole((L, H)), whole((L, D)), whole((L, D)), whole((1, NP)), whole((1, NP)), whole((H, D)), whole((H, D)),
         wf, wf, pl.BlockSpec((T, D), lambda t, s: (first(t), 0)), pl.BlockSpec((T, D), lambda t, s: (second(t), 0))],
        [pl.BlockSpec((L, T), lambda t, s: (0, first(t))), pl.BlockSpec((L, T), lambda t, s: (0, second(t))),
         pl.BlockSpec((L, T), lambda t, s: (0, tile(t, s))), const(L, H), const(L, H), const(L, D), const(L, D), const(L, D),
         const(L, H), const(L, H), pl.BlockSpec((8, T), lambda t, s: (0, tile(t, s))), const(8, D)],
        (sds((L, FH), BF), sds((L, FH), BF), sds((L, 2 * FH), BF), sds((L, H), BF), sds((L, H), BF), sds((L, D), BF),
         sds((L, D), F32), sds((L, D), BF), sds((L, H), BF), sds((L, H), BF), sds((8, 2 * FH), F32), sds((8, D), F32)),
        [pltpu.VMEM((L, D), BF), pltpu.VMEM((L, D), F32), pltpu.VMEM((L, D), F32), pltpu.VMEM((L, D), F32),
         pltpu.VMEM((D, T), BF), pltpu.VMEM((T, D), BF), pltpu.VMEM((L, T), BF)],
        cost(2 * L * D * (2 * D + 8 * FH), 24e6, 1.5e6),
        (scal, ak, ar, xb, dz, pk_own, pk_oth, wp_own, wp_oth, wf_own, wf_oth, wo_own, wo_oth),
    )


def pair_of(i, s):
    return ((i + 2) & 3) ^ (s[8] >> 1)


def turns(i, outs):
    return (i == 0, i == 1, i >= 2) if len(outs) == 3 else (i < 2, i >= 2)


def put_pair(scal, left, right, *outs):
    H = left.shape[0]
    i = pl.program_id(0)
    flip = scal[8] & 1
    for out, here in zip(outs, turns(i, outs)):

        @pl.when(here)
        def _():
            out[half(flip, H), :] = left
            out[half(1 - flip, H), :] = right


def pair_specs(H, split):
    block = lambda at: pl.BlockSpec((2 * H, H), lambda i, s: (at(i), 0))
    keep = block(lambda i: jnp.maximum(i - 2, 0))
    if split:
        first = block(lambda i: 0)
        return [first, first, keep], (sds((2 * H, H), BF), sds((2 * H, H), BF), sds((4 * H, H), BF))
    return [block(lambda i: jnp.minimum(i, 1)), keep], (sds((4 * H, H), BF), sds((4 * H, H), BF))


def grad_pair_kernel(scal, a_own, a_oth, b_own, b_oth, *outs):
    H = a_own.shape[1]
    val = (dot_tn(a_own[...], b_own[...]) + dot_tn(a_oth[...], b_oth[...])).astype(BF)
    put_pair(scal, val[:, :H], val[:, H:], *outs)


def grad_rows(scal, a_own, a_oth, b_own, b_oth):
    K, M = a_own.shape
    N = b_own.shape[1]
    H = N // 2
    a = pl.BlockSpec((K, H), lambda i, s: (0, pair_of(i, s)))
    specs, shape = pair_specs(H, False)
    return call(
        grad_pair_kernel, "grad_rows", (4,), [a, a, whole((K, N)), whole((K, N))], specs, shape, [],
        cost(4 * K * M * N, 4 * K * (M + N) + 2 * M * N), (scal, a_own, a_oth, b_own, b_oth),
    )


def grad_cols(scal, a_own, a_oth, b_own, b_oth):
    K, M = a_own.shape
    N = b_own.shape[1]
    b = pl.BlockSpec((K, 2 * M), lambda i, s: (0, pair_of(i, s)))
    specs, shape = pair_specs(M, False)
    return call(
        grad_pair_kernel, "grad_cols", (4,), [whole((K, M)), whole((K, M)), b, b], specs, shape, [],
        cost(4 * K * M * N, 4 * K * (M + N) + 2 * M * N), (scal, a_own, a_oth, b_own, b_oth),
    )


def grad_attn_kernel(scal, n_own, n_oth, a_own, a_oth, gb_own, gb_oth, *refs):
    H = n_own.shape[1]
    shard = scal[0]
    outs = refs[-3:]
    n = (len(refs) - 3) // 4
    l_own, l_oth, r_own, r_oth = [refs[n * j : n * j + n] for j in range(4)]
    w = pair_of(pl.program_id(0), scal)
    flip = scal[8] & 1

    def put(rows, value):
        i = pl.program_id(0)
        for out, here in zip(outs, turns(i, outs)):

            @pl.when(here)
            def _():
                out[half(rows, H), :] = value

    def heads(parts):
        return jnp.concatenate([p[0] for p in parts], axis=1)

    @pl.when(w < 3)
    def _():
        mine = dot_tn(n_own[...], heads(l_own)) + dot_tn(n_oth[...], heads(l_oth))
        put(shard ^ flip, mine.astype(BF))
        theirs = dot_tn(n_own[...], heads(r_own)) + dot_tn(n_oth[...], heads(r_oth))
        put(1 - (shard ^ flip), theirs.astype(BF))

    @pl.when(w == 3)
    def _():
        val = (dot_tn(a_own[...], gb_own[...]) + dot_tn(a_oth[...], gb_oth[...])).astype(BF)
        put(flip, val[:, :H])
        put(1 - flip, val[:, H:])


def grad_attn(scal, normed, n_oth, a_own, a_oth, gb_own, gb_oth, *parts):
    K, H = n_oth.shape
    D = 2 * H
    d = [pl.BlockSpec((1, K, p.shape[2]), lambda i, s: (jnp.minimum(pair_of(i, s), 2), 0, 0)) for p in parts]
    n = pl.BlockSpec((K, H), lambda i, s: (0, s[0]), pipeline_mode=pl.Buffered(1))
    w = whole((K, H))
    specs, shape = pair_specs(H, True)
    return call(
        grad_attn_kernel, "grad_attn", (4,), [n, w, w, w, whole((K, D)), whole((K, D))] + d, specs, shape, [],
        cost(32 * K * H * H, 16e6), (scal, normed, n_oth, a_own, a_oth, gb_own, gb_oth, *parts),
    )


def last_kernel(
    scal, d_own, d_oth, xb, dmid, pk_own, pk_oth, w_own, w_oth, sfc, sums,
    gh, glat, s_keep, s_send, gi, es, ds_, vec, *, L,
):
    r_id = pl.program_id(0)
    shard = scal[0]
    RB, D = xb.shape
    H = D // 2
    FF = sfc.shape[1]
    for j in range(3):
        ds_[:, half(2 * j + shard, H)] = d_own[j]
        ds_[:, half(2 * j + 1 - shard, H)] = d_oth[j]
    d = ds_[...]
    es[:, half(shard, H)] = dot_nt(d, w_own[...])
    es[:, half(1 - shard, H)] = dot_nt(d, w_oth[...])
    gn = es[...]
    x = xb[...].astype(F32)
    cen = x - jnp.mean(x, axis=1, keepdims=True)
    r = lax.rsqrt(jnp.mean(cen * cen, axis=1, keepdims=True) + norm_epsilon)
    n = cen * r
    e = gn * both(pk_own, pk_oth, shard, 0, H)
    gi[...] = dmid[...] + r * (e - jnp.mean(e, axis=1, keepdims=True) - n * jnp.mean(e * n, axis=1, keepdims=True))

    @pl.when(r_id == 0)
    def _():
        glat[...] = jnp.zeros_like(glat)
        vec[...] = jnp.zeros_like(vec)

    row0 = shard * L + r_id * RB
    for c in range(6):
        rel = scal[2 + c] - row0

        @pl.when((rel >= 0) & (rel < RB))
        def _():
            glat[c : c + 1, :] = gi[pl.ds(rel, 1), :]
            gi[pl.ds(rel, 1), :] = jnp.zeros((1, D), F32)

    gh[...] = gi[...].astype(BF)
    vec[0:1, 0:D] += jnp.sum(gn * n, axis=0, keepdims=True)
    vec[1:2, 0:D] += jnp.sum(gn, axis=0, keepdims=True)
    vec[2:3, 0:D] += jnp.sum(ds_[:, 0:D].astype(F32), axis=0, keepdims=True)
    vec[2:3, D : 2 * D] += jnp.sum(ds_[:, 2 * D : 3 * D].astype(F32), axis=0, keepdims=True)

    @pl.when(r_id == pl.num_programs(0) - 1)
    def _():
        for side in range(2):
            owner = shard if side == 0 else 1 - shard
            out = s_keep if side == 0 else s_send
            one = half(owner, H)
            wide = vec[2:3, half(owner, D)]
            fc = sfc[0:1, half(owner, FF // 2)]
            flat = jnp.concatenate(
                [vec[0:1, one], vec[1:2, one], wide, sums[0:1, one], sums[1:2, one], sums[2:3, one], fc, sums[3:4, one]], axis=1
            )
            out[...] = jnp.zeros_like(out)
            for k in range(flat.shape[1] // (2 * D)):
                out[k : k + 1, :] = flat[:, k * 2 * D : (k + 1) * 2 * D]


def last_block(scal, parts, xb, dmid, pk_own, pk_oth, w_own, w_oth, sfc, sums):
    L, D = xb.shape
    H = D // 2
    RB = L // 2
    NP = pk_own.shape[1]
    rows = lambda n: pl.BlockSpec((RB, n), lambda r, s: (r, 0))
    const = lambda *shape: pl.BlockSpec(shape, lambda r, s: (0, 0))
    d = [pl.BlockSpec((3, RB, p.shape[2]), lambda r, s: (0, r, 0)) for p in parts]
    return call(
        functools.partial(last_kernel, L=L), "last_block", (2,),
        d + [rows(D), rows(D), whole((1, NP)), whole((1, NP)), whole((H, 3 * D)), whole((H, 3 * D)), whole(sfc.shape), whole(sums.shape)],
        [rows(D), const(8, D), const(8, 2 * D), const(8, 2 * D)],
        (sds((L, D), BF), sds((8, D), F32), sds((8, 2 * D), F32), sds((8, 2 * D), F32)),
        [pltpu.VMEM((RB, D), F32), pltpu.VMEM((RB, D), F32), pltpu.VMEM((RB, 3 * D), BF), pltpu.VMEM((8, 2 * D), F32)],
        cost(6 * L * D * D, 12e6),
        (scal, *parts, xb, dmid, pk_own, pk_oth, w_own, w_oth, sfc, sums),
    )


def final_kernel(scal, *refs, wide):
    pos = refs[:8]
    outs = refs[8:]
    H = pos[0].shape[1]
    w = pl.program_id(0)
    k = w ^ (scal[8] >> 1)
    flip = scal[8] & 1
    for j in range(4):
        for f in range(2):
            for o, here in enumerate((w < wide, w >= wide) if len(outs) == 2 else (True,)):

                @pl.when((k == j) & (flip == f) & here)
                def _():
                    outs[o][:, :H] = pos[2 * j + f][...].astype(F32)
                    outs[o][:, H:] = pos[2 * j + 1 - f][...].astype(F32)


def final(scal, pos, out_specs, out_shape, wide=4):
    H = pos[0].shape[1]
    return call(
        functools.partial(final_kernel, wide=wide), "final", (4,), [whole((H, H))] * 8, out_specs, out_shape, [],
        cost(8 * H * H, 48 * H * H), (scal, *pos),
    )


def swap(x):
    return lax.ppermute(x, "shard", [(0, 1), (1, 0)])


def hop(x, first, second):
    pairs = []
    for rep in range(16):
        pairs.append((2 * rep, 2 * (rep ^ first)))
        pairs.append((2 * rep + 1, 2 * (rep ^ second) + 1))
    return lax.ppermute(x, ("rep", "shard"), pairs)


def gate(x, *deps):
    return lax.optimization_barrier((x, *deps))[0]


def gated(xs, *deps):
    return list(lax.optimization_barrier((*xs, *deps))[: len(xs)])


def total(*xs):
    return functools.reduce(lambda a, b: a + b, [x.astype(F32) for x in xs]).astype(BF)


class Reduce:
    def __init__(self, *parts):
        *sends, self.keep, self.dims = parts
        self.H = self.keep.shape[1]
        self.r1 = [hop(send, *self.dims[0]) for send in sends]

    def rows(self, x, a, b):
        return x[a * self.H : b * self.H]

    def hop2(self, *deps):
        self.r1[-1] = gate(self.r1[-1], *deps)
        n = self.r1[-1].shape[0] // self.H
        send = total(self.rows(self.keep, 2, 4), self.rows(self.r1[-1], n - 2, n))
        self.r2 = hop(send, *self.dims[1])
        return send

    def hop3(self, *deps):
        self.r1[0], self.r2 = gated((self.r1[0], self.r2), *deps)
        send = total(self.rows(self.keep, 1, 2), self.rows(self.r1[0], 1, 2), self.rows(self.r2, 1, 2))
        self.r3 = hop(send, *self.dims[2])
        return send

    def hop4(self, *deps):
        self.x = total(self.rows(self.keep, 0, 1), self.rows(self.r1[0], 0, 1), self.rows(self.r2, 0, 1), gate(self.r3, *deps))
        self.r4 = hop(self.x, 8, 8)
        return self.x

    def hop5(self, *deps):
        p0 = total(self.x, gate(self.r4, *deps))
        self.pos = [p0] + [None] * 7
        for i in range(3):
            self.pos[1 << i] = hop(p0, *self.dims[2 - i])
        return p0

    def take(self, i, *deps):
        self.pos[i] = gate(self.pos[i], *deps)
        if i == 1:
            self.pos[3] = hop(self.pos[1], *self.dims[1])
        self.pos[4 + i] = hop(self.pos[i], *self.dims[0])
        return self.pos[i]


def pair_device(
    hidden, latents, latent_pos, prefix, ln1_gain, ln1_bias, w_qkv, b_qv, w_proj, b_proj,
    ln2_gain, ln2_bias, w_fc, b_fc, w_out, b_out, cotangent,
):
    _, L, D = hidden.shape
    H = D // 2
    shard = lax.axis_index("shard").astype(jnp.int32)
    rep = lax.axis_index("rep").astype(jnp.int32)
    bit0, bit1, bit2 = rep & 1, (rep >> 1) & 1, (rep >> 2) & 1
    high = jnp.where(shard == 0, bit0, bit1)
    low = jnp.where(shard == 0, bit1, bit0)
    code = high * 4 + bit2 * 2 + low
    dims = ((1, 2), (4, 4), (2, 1))
    lead = lax.broadcasted_iota(jnp.int32, (16,), 0)
    scal = jnp.where(lead == 0, shard, jnp.where(lead == 1, prefix[0], jnp.where(lead == 8, code, 0)))
    scal = lax.dynamic_update_slice(scal, latent_pos[0].astype(jnp.int32), (2,))

    pk_own = pack([ln1_gain, ln1_bias, b_qv, b_proj, ln2_gain, ln2_bias, b_fc, b_out])
    pk_oth = swap(pk_own)
    qkv_oth = swap(w_qkv)
    hid = hidden[0]
    dz = cotangent[0]
    lat = latents[0]

    send, normed, nrm_send, xb = ln_send(scal, hid, lat, pk_own, pk_oth, w_qkv, qkv_oth)
    recv = swap(send)
    keep = own_heads(scal, normed, pk_own, pk_oth, w_qkv, qkv_oth)
    proj_oth, fc_oth, out_oth, nrm_recv, dz_oth = [swap(gate(a, recv, keep)) for a in (w_proj, w_fc, w_out, nrm_send, dz)]
    att_keep, att_send, lse = attn_fwd(scal, keep, recv)
    att_recv = swap(att_send)
    dz_oth, nrm_recv, xb = gated((dz_oth, nrm_recv, xb))
    act_keep, act_send, gp, n2_keep, n2_send, block_out, dmid, gb, ga_keep, ga_send, sfc, sums = ffn(
        scal, att_keep, att_recv, xb, dz, pk_own, pk_oth, w_proj, proj_oth, w_fc, fc_oth, w_out, out_oth
    )
    act_recv = swap(act_send)
    ga_recv = swap(ga_send)
    gp_oth = swap(gate(gp, act_recv))
    n2_recv = swap(gate(n2_send, act_recv))
    gb_oth = swap(gate(gb, act_recv))
    s_out, k_out = grad_rows(scal, act_keep, act_recv, dz, dz_oth)
    r_out = Reduce(s_out, k_out, dims)
    s_fc, k_fc = grad_cols(scal, n2_keep, gate(n2_recv, k_out), gp, gp_oth)
    r_fc = Reduce(s_fc, k_fc, dims)
    d_own, d_oth = attn_bwd(scal, keep, recv, ga_keep, gate(ga_recv, k_fc), att_keep, att_send, lse, 0, H // 128)
    e_own, e_oth = swap(d_oth), swap(d_own)
    tok = r_out.hop2(d_own)
    tok = r_fc.hop2(tok)
    a_c, b_c, k_c = grad_attn(scal, normed, nrm_recv, att_keep, att_send, gb, gb_oth, d_own, d_oth, gate(e_own, tok), e_oth)
    r_c = Reduce(a_c, b_c, k_c, dims)
    tok = r_out.hop3(k_c)
    tok = r_fc.hop3(tok)
    gh, glat, s_keep, s_send = last_block(
        scal, (d_own, gate(e_own, tok)), xb, dmid, pk_own, pk_oth, w_qkv, qkv_oth, sfc, sums
    )
    s_recv = swap(s_send)
    glat_oth = swap(glat)
    r_out.hop4(gh)
    small = s_keep + s_recv
    glat = glat + glat_oth
    r_c.hop2()
    r_fc.hop4()
    r_out.hop5()
    for bits in ((1, 2), (2, 1), (4, 4), (8, 8)):
        small = small + hop(small, *bits)
    r_c.hop3()
    r_fc.hop5()
    r_c.hop4()
    r_c.hop5()
    for i in (1, 2, 3):
        r_out.take(i)
    for i in (1, 2, 3):
        r_fc.take(i)
    g_out = final(scal, r_out.pos, pl.BlockSpec((H, D), lambda w, s: (w, 0)), sds((4 * H, D), F32))
    r_c.take(1)
    r_c.take(2)
    r_c.take(3, g_out, small)
    g_fc = final(scal, gated(r_fc.pos, g_out), pl.BlockSpec((H, D), lambda w, s: (0, w)), sds((H, 4 * D), F32))
    g_qkv, g_proj = final(
        scal, gated(r_c.pos, g_fc), [pl.BlockSpec((H, D), lambda w, s: (0, jnp.minimum(w, 2))), pl.BlockSpec((H, D), lambda w, s: (0, 0))],
        (sds((H, 3 * D), F32), sds((H, D), F32)), 3,
    )
    flat = small[:3].reshape(-1)
    cuts = [0]
    for v in (ln1_gain, ln1_bias, b_qv, b_proj, ln2_gain, ln2_bias, b_fc, b_out):
        cuts.append(cuts[-1] + v.shape[0])
    vecs = [flat[cuts[i] : cuts[i + 1]] for i in range(8)]
    return (
        block_out[None], gh[None], glat[None, :6], vecs[0], vecs[1], g_qkv, vecs[2], g_proj, vecs[3],
        vecs[4], vecs[5], g_fc, vecs[6], g_out, vecs[7],
    )


def layer_norm(values, norm_gain, norm_shift):
    average = jnp.mean(values, axis=-1, keepdims=True)
    centered = values - average
    variance = jnp.mean(centered * centered, axis=-1, keepdims=True)
    return centered * lax.rsqrt(variance + norm_epsilon) * norm_gain + norm_shift


def gelu_tanh(values):
    return (
        0.5
        * values
        * (1.0 + jnp.tanh(gelu_root * (values + gelu_cubic * values * values * values)))
    )


def head_scores(query_one, key_one, query_pos, key_pos, prefix_one, score_scale):
    scores = (
        jnp.einsum("qhe,khe->hqk", query_one, key_one, preferred_element_type=jnp.float32)
        * score_scale
    )
    causal = (key_pos[None, :] <= query_pos[:, None])[None]
    in_prefix = (key_pos < prefix_one)[None, None, :]
    return jnp.where(causal | in_prefix, scores, masked_score)


def per_device(
    hidden,
    latents,
    latent_pos,
    prefix,
    ln1_gain,
    ln1_bias,
    w_qkv,
    b_qv,
    w_proj,
    b_proj,
    ln2_gain,
    ln2_bias,
    w_fc,
    b_fc,
    w_out,
    b_out,
    cotangent,
):
    seq_count, local_len, model_width = hidden.shape
    head_dim = model_width // HEADS
    score_scale = head_dim ** (-0.5)
    row_start = lax.axis_index("shard") * local_len
    gathered = (
        lax.all_gather(ln1_gain, "shard", axis=0, tiled=True),
        lax.all_gather(ln1_bias, "shard", axis=0, tiled=True),
        lax.all_gather(w_qkv, "shard", axis=0, tiled=True),
        lax.all_gather(b_qv, "shard", axis=0, tiled=True),
        lax.all_gather(w_proj, "shard", axis=0, tiled=True),
        lax.all_gather(b_proj, "shard", axis=0, tiled=True),
        lax.all_gather(ln2_gain, "shard", axis=0, tiled=True),
        lax.all_gather(ln2_bias, "shard", axis=0, tiled=True),
        lax.all_gather(w_fc, "shard", axis=0, tiled=True),
        lax.all_gather(b_fc, "shard", axis=0, tiled=True),
        lax.all_gather(w_out, "shard", axis=0, tiled=True),
        lax.all_gather(b_out, "shard", axis=0, tiled=True),
    )
    (
        full_ln1_gain,
        full_ln1_bias,
        full_qkv,
        full_b_qv,
        full_proj,
        full_b_proj,
        full_ln2_gain,
        full_ln2_bias,
        full_fc,
        full_b_fc,
        complete_output,
        full_b_out,
    ) = gathered
    row_ids = row_start + jnp.arange(local_len, dtype=jnp.int32)
    latent_matches = row_ids[None, :, None] == latent_pos[:, None, :]
    positioned_rows = jnp.einsum(
        "ety,eyw->etw",
        latent_matches.astype(jnp.bfloat16),
        latents,
        preferred_element_type=jnp.float32,
    )
    replaced = jnp.any(latent_matches, axis=-1)[..., None]
    block_in = jnp.where(replaced, positioned_rows, hidden.astype(jnp.float32)).reshape(
        -1, model_width
    )
    normed, back_norm_one = jax.vjp(
        layer_norm, block_in, full_ln1_gain.astype(jnp.float32), full_ln1_bias.astype(jnp.float32)
    )
    normed_low = normed.astype(jnp.bfloat16)
    bias_full = jnp.concatenate(
        [
            full_b_qv[:model_width].astype(jnp.float32),
            jnp.zeros((model_width,), jnp.float32),
            full_b_qv[model_width:].astype(jnp.float32),
        ]
    )
    projected = (
        jnp.dot(normed_low, full_qkv, preferred_element_type=jnp.float32) + bias_full
    ).astype(jnp.bfloat16)
    query_heads = projected[:, :model_width].reshape(seq_count, local_len, HEADS, head_dim)
    key_local = projected[:, model_width : 2 * model_width].reshape(
        seq_count, local_len, model_width
    )
    value_local = projected[:, 2 * model_width :].reshape(seq_count, local_len, model_width)
    key_full, value_full = (
        lax.all_gather(key_local, "shard", axis=1, tiled=True),
        lax.all_gather(value_local, "shard", axis=1, tiled=True),
    )
    full_len = key_full.shape[1]
    key_heads = key_full.reshape(seq_count, full_len, HEADS, head_dim)
    value_heads = value_full.reshape(seq_count, full_len, HEADS, head_dim)
    key_pos_all = jnp.arange(full_len, dtype=jnp.int32)

    def forward_seq(items):
        query_one, key_one, value_one, prefix_one = items
        scores = head_scores(query_one, key_one, row_ids, key_pos_all, prefix_one, score_scale)
        row_peak = jnp.max(scores, axis=-1, keepdims=True)
        single_logsumexp = row_peak + jnp.log(
            jnp.sum(jnp.exp(scores - row_peak), axis=-1, keepdims=True)
        )
        probs_low = jnp.exp(scores - single_logsumexp).astype(jnp.bfloat16)
        mixed = jnp.einsum("hqk,khe->qhe", probs_low, value_one, preferred_element_type=jnp.float32)
        return (mixed.astype(jnp.bfloat16), single_logsumexp)

    attended_heads, log_total = lax.map(forward_seq, (query_heads, key_heads, value_heads, prefix))
    attended = attended_heads.reshape(-1, model_width)
    middle = (
        block_in
        + jnp.dot(attended, full_proj, preferred_element_type=jnp.float32)
        + full_b_proj.astype(jnp.float32)
    )
    normed_two, back_norm_two = jax.vjp(
        layer_norm, middle, full_ln2_gain.astype(jnp.float32), full_ln2_bias.astype(jnp.float32)
    )
    normed_two_low = normed_two.astype(jnp.bfloat16)
    pre_act = jnp.dot(
        normed_two_low, full_fc, preferred_element_type=jnp.float32
    ) + full_b_fc.astype(jnp.float32)
    activated, back_gelu = jax.vjp(gelu_tanh, pre_act)
    activated_low = activated.astype(jnp.bfloat16)
    block_out = (
        middle
        + jnp.dot(activated_low, complete_output, preferred_element_type=jnp.float32)
        + full_b_out.astype(jnp.float32)
    )
    block_out = block_out.reshape(seq_count, local_len, model_width).astype(jnp.bfloat16)
    back_qkv, back_proj, back_fc, back_out = (
        lax.all_gather(w_qkv, "shard", axis=0, tiled=True),
        lax.all_gather(w_proj, "shard", axis=0, tiled=True),
        lax.all_gather(w_fc, "shard", axis=0, tiled=True),
        lax.all_gather(w_out, "shard", axis=0, tiled=True),
    )
    grad_top = cotangent.reshape(-1, model_width)
    grad_w_out = jnp.einsum(
        "nf,nd->fd", activated_low, grad_top, preferred_element_type=jnp.float32
    )
    grad_b_out = jnp.sum(grad_top.astype(jnp.float32), axis=0)
    grad_act = jnp.einsum("nd,fd->nf", grad_top, back_out, preferred_element_type=jnp.float32)
    (grad_pre,) = back_gelu(grad_act)
    grad_pre_low = grad_pre.astype(jnp.bfloat16)
    grad_w_fc = jnp.einsum(
        "nd,nf->df", normed_two_low, grad_pre_low, preferred_element_type=jnp.float32
    )
    grad_b_fc = jnp.sum(grad_pre_low.astype(jnp.float32), axis=0)
    grad_normed_two = jnp.einsum(
        "nf,df->nd", grad_pre_low, back_fc, preferred_element_type=jnp.float32
    )
    grad_mid_norm, grad_ln2_gain, grad_ln2_bias = back_norm_two(grad_normed_two)
    grad_mid = grad_top.astype(jnp.float32) + grad_mid_norm
    grad_branch_low = grad_mid.astype(jnp.bfloat16)
    grad_w_proj = jnp.einsum(
        "nd,ne->de", attended, grad_branch_low, preferred_element_type=jnp.float32
    )
    grad_b_proj = jnp.sum(grad_branch_low.astype(jnp.float32), axis=0)
    grad_att = jnp.einsum(
        "ne,de->nd", grad_branch_low, back_proj, preferred_element_type=jnp.float32
    )
    grad_att_low = grad_att.astype(jnp.bfloat16).reshape(seq_count, local_len, HEADS, head_dim)

    def backward_sequence(items):
        query_one, key_one, value_one, prefix_one, single_logsumexp, upstream = items
        scores = head_scores(query_one, key_one, row_ids, key_pos_all, prefix_one, score_scale)
        attn_probs = jnp.exp(scores - single_logsumexp)
        grad_value_one = jnp.einsum(
            "hqk,qhe->khe",
            attn_probs.astype(jnp.bfloat16),
            upstream,
            preferred_element_type=jnp.float32,
        )
        grad_probs = jnp.einsum(
            "qhe,khe->hqk", upstream, value_one, preferred_element_type=jnp.float32
        )
        delta_one = jnp.sum(grad_probs * attn_probs, axis=-1, keepdims=True)
        grad_scores = (attn_probs * (grad_probs - delta_one)).astype(jnp.bfloat16)
        grad_query_one = (
            jnp.einsum("hqk,khe->qhe", grad_scores, key_one, preferred_element_type=jnp.float32)
            * score_scale
        )
        grad_key_one = (
            jnp.einsum("hqk,qhe->khe", grad_scores, query_one, preferred_element_type=jnp.float32)
            * score_scale
        )
        return (
            grad_query_one,
            grad_key_one.reshape(full_len, model_width),
            grad_value_one.reshape(full_len, model_width),
        )

    grad_query, grad_key_all, grad_value_all = lax.map(
        backward_sequence, (query_heads, key_heads, value_heads, prefix, log_total, grad_att_low)
    )
    grad_key_own, grad_value_own = (
        lax.psum_scatter(
            grad_key_all.astype(jnp.bfloat16), "shard", scatter_dimension=1, tiled=True
        ).astype(jnp.float32),
        lax.psum_scatter(
            grad_value_all.astype(jnp.bfloat16), "shard", scatter_dimension=1, tiled=True
        ).astype(jnp.float32),
    )
    grad_query_low = grad_query.reshape(-1, model_width).astype(jnp.bfloat16)
    grad_key_low = grad_key_own.reshape(-1, model_width).astype(jnp.bfloat16)
    grad_value_low = grad_value_own.reshape(-1, model_width).astype(jnp.bfloat16)
    grad_projected = jnp.concatenate([grad_query_low, grad_key_low, grad_value_low], axis=1)
    grad_b_qv = jnp.concatenate(
        [
            jnp.sum(grad_query_low.astype(jnp.float32), axis=0),
            jnp.sum(grad_value_low.astype(jnp.float32), axis=0),
        ]
    )
    grad_w_qkv = jnp.einsum(
        "nd,ne->de", normed_low, grad_projected, preferred_element_type=jnp.float32
    )
    grad_normed = jnp.einsum(
        "ne,de->nd", grad_projected, back_qkv, preferred_element_type=jnp.float32
    )
    grad_in_norm, grad_ln1_gain, grad_ln1_bias = back_norm_one(grad_normed)
    block_gradient = (grad_mid + grad_in_norm).reshape(seq_count, local_len, model_width)
    latent_terms = jnp.einsum(
        "inv,inz->ivz",
        latent_matches.astype(jnp.float32),
        block_gradient,
        precision=lax.Precision.HIGHEST,
    )
    grad_latents = lax.psum(latent_terms, "shard")
    grad_hidden = jnp.where(replaced, 0.0, block_gradient).astype(jnp.bfloat16)
    shares = (
        lax.psum_scatter(
            grad_ln1_gain.astype(jnp.bfloat16), "shard", scatter_dimension=0, tiled=True
        ).astype(jnp.float32),
        lax.psum_scatter(
            grad_ln1_bias.astype(jnp.bfloat16), "shard", scatter_dimension=0, tiled=True
        ).astype(jnp.float32),
        lax.psum_scatter(
            grad_w_qkv.astype(jnp.bfloat16), "shard", scatter_dimension=0, tiled=True
        ).astype(jnp.float32),
        lax.psum_scatter(
            grad_b_qv.astype(jnp.bfloat16), "shard", scatter_dimension=0, tiled=True
        ).astype(jnp.float32),
        lax.psum_scatter(
            grad_w_proj.astype(jnp.bfloat16), "shard", scatter_dimension=0, tiled=True
        ).astype(jnp.float32),
        lax.psum_scatter(
            grad_b_proj.astype(jnp.bfloat16), "shard", scatter_dimension=0, tiled=True
        ).astype(jnp.float32),
        lax.psum_scatter(
            grad_ln2_gain.astype(jnp.bfloat16), "shard", scatter_dimension=0, tiled=True
        ).astype(jnp.float32),
        lax.psum_scatter(
            grad_ln2_bias.astype(jnp.bfloat16), "shard", scatter_dimension=0, tiled=True
        ).astype(jnp.float32),
        lax.psum_scatter(
            grad_w_fc.astype(jnp.bfloat16), "shard", scatter_dimension=0, tiled=True
        ).astype(jnp.float32),
        lax.psum_scatter(
            grad_b_fc.astype(jnp.bfloat16), "shard", scatter_dimension=0, tiled=True
        ).astype(jnp.float32),
        lax.psum_scatter(
            grad_w_out.astype(jnp.bfloat16), "shard", scatter_dimension=0, tiled=True
        ).astype(jnp.float32),
        lax.psum_scatter(
            grad_b_out.astype(jnp.bfloat16), "shard", scatter_dimension=0, tiled=True
        ).astype(jnp.float32),
    )
    summed = (
        lax.psum(shares[0].astype(jnp.bfloat16), "rep").astype(jnp.float32),
        lax.psum(shares[1].astype(jnp.bfloat16), "rep").astype(jnp.float32),
        lax.psum(shares[2].astype(jnp.bfloat16), "rep").astype(jnp.float32),
        lax.psum(shares[3].astype(jnp.bfloat16), "rep").astype(jnp.float32),
        lax.psum(shares[4].astype(jnp.bfloat16), "rep").astype(jnp.float32),
        lax.psum(shares[5].astype(jnp.bfloat16), "rep").astype(jnp.float32),
        lax.psum(shares[6].astype(jnp.bfloat16), "rep").astype(jnp.float32),
        lax.psum(shares[7].astype(jnp.bfloat16), "rep").astype(jnp.float32),
        lax.psum(shares[8].astype(jnp.bfloat16), "rep").astype(jnp.float32),
        lax.psum(shares[9].astype(jnp.bfloat16), "rep").astype(jnp.float32),
        lax.psum(shares[10].astype(jnp.bfloat16), "rep").astype(jnp.float32),
        lax.psum(shares[11].astype(jnp.bfloat16), "rep").astype(jnp.float32),
    )
    (
        total_ln1_gain,
        total_ln1_bias,
        total_w_qkv,
        total_b_qv,
        total_w_proj,
        total_b_proj,
        total_ln2_gain,
        total_ln2_bias,
        total_w_fc,
        total_b_fc,
        total_w_out,
        total_b_out,
    ) = summed
    return (
        block_out,
        grad_hidden,
        grad_latents,
        total_ln1_gain,
        total_ln1_bias,
        total_w_qkv,
        total_b_qv,
        total_w_proj,
        total_b_proj,
        total_ln2_gain,
        total_ln2_bias,
        total_w_fc,
        total_b_fc,
        total_w_out,
        total_b_out,
    )


def solution(mesh):
    sizes = dict(mesh.shape)
    paired = sizes["rep"] == 16 and sizes["shard"] == 2
    body = pair_device if paired else per_device
    in_specs = (
        P("rep", "shard", None),
        P("rep", None, None),
        P("rep", None),
        P("rep"),
        P("shard"),
        P("shard"),
        P("shard", None),
        P("shard"),
        P("shard", None),
        P("shard"),
        P("shard"),
        P("shard"),
        P("shard", None),
        P("shard"),
        P("shard", None),
        P("shard"),
        P("rep", "shard", None),
    )
    out_specs = (
        P("rep", "shard", None),
        P("rep", "shard", None),
        P("rep", None, None),
        P("shard"),
        P("shard"),
        P("shard", None),
        P("shard"),
        P("shard", None),
        P("shard"),
        P("shard"),
        P("shard"),
        P("shard", None),
        P("shard"),
        P("shard", None),
        P("shard"),
    )
    return jax.shard_map(
        body, mesh=mesh, in_specs=in_specs, out_specs=out_specs, check_vma=False
    )
```

```python
import functools
import jax
import jax.numpy as jnp
from jax import lax
from jax.experimental import pallas as pl
from jax.experimental.pallas import tpu as pltpu
from jax.sharding import PartitionSpec as P

HEADS = 12
F32 = jnp.float32
BF = jnp.bfloat16

norm_epsilon = 1e-05
gelu_root = 0.7978845608028654
gelu_cubic = 0.044715
masked_score = -1e30
LOG2E = 1.4426950408889634


def dot_nt(a, b):
    return lax.dot_general(a, b, (((1,), (1,)), ((), ())), preferred_element_type=F32)


def dot_nn(a, b):
    return lax.dot_general(a, b, (((1,), (0,)), ((), ())), preferred_element_type=F32)


def dot_tn(a, b):
    return lax.dot_general(a, b, (((0,), (0,)), ((), ())), preferred_element_type=F32)


def params(semantics=None, mb=16):
    return pltpu.CompilerParams(dimension_semantics=semantics, vmem_limit_bytes=mb * 1024 * 1024)


def cost(flops, nbytes, trans=0):
    return pl.CostEstimate(flops=1, bytes_accessed=1, transcendentals=0)


def whole(shape):
    return pl.BlockSpec(shape, lambda *_: (0,) * len(shape), pipeline_mode=pl.Buffered(1))


def both(own, oth, shard, a, n):
    o = own[0:1, a : a + n].astype(F32)
    t = oth[0:1, a : a + n].astype(F32)
    first = jnp.where(shard == 0, o, t)
    second = jnp.where(shard == 0, t, o)
    return jnp.concatenate([first, second], axis=1)


def half(i, n):
    return pl.ds(pl.multiple_of(i * n, n), n)


def call(kernel, name, grid, in_specs, out_specs, out_shape, scratch, est, args, mb=16):
    return pl.pallas_call(
        kernel,
        out_shape=out_shape,
        grid_spec=pltpu.PrefetchScalarGridSpec(
            num_scalar_prefetch=1, grid=grid, in_specs=in_specs, out_specs=out_specs, scratch_shapes=scratch
        ),
        compiler_params=params(("arbitrary",), mb),
        cost_estimate=est,
        name=name,
    )(*args)


sds = jax.ShapeDtypeStruct


def pack(vecs):
    n = sum(v.shape[0] for v in vecs)
    at = 0
    out = []
    for v in vecs:
        out.append(jnp.pad(v, (at, n - at - v.shape[0])))
        at += v.shape[0]
    return functools.reduce(jnp.add, out)[None, :]


def qv_bias(pk_own, pk_oth, shard, which, heads):
    H = pk_own.shape[1] // 12
    a = pk_own[0:1, 2 * H : 4 * H].astype(F32)
    b = pk_oth[0:1, 2 * H : 4 * H].astype(F32)
    src = jnp.where(shard == which, a, b)
    return jnp.where(heads == 0, src[:, :H], src[:, H:])


def project(n, ws, pk_own, pk_oth, shard, heads, out):
    H = ws.shape[0] // 2
    for j in range(3):
        y = dot_nn(n, ws[:, j * H : (j + 1) * H])
        if j != 1:
            y = y + qv_bias(pk_own, pk_oth, shard, j // 2, heads)
        out[:, j * H : (j + 1) * H] = y.astype(BF)


def ln_send_kernel(
    scal, hid, lat, pk_own, pk_oth, qo, ko, vo, qt, kt, vt, send, normed, nrm_send, xb, xs, ns, ws, *, L
):
    r = pl.program_id(0)
    RB, D = hid.shape
    H = D // 2
    shard = scal[0]

    @pl.when(r == 0)
    def _():
        for j, (o, t) in enumerate(((qo, qt), (ko, kt), (vo, vt))):
            ws[half(shard, H), j * H : (j + 1) * H] = o[...]
            ws[half(1 - shard, H), j * H : (j + 1) * H] = t[...]

    xs[...] = hid[...].astype(F32)
    row0 = shard * L + r * RB
    for c in range(6):
        rel = scal[2 + c] - row0

        @pl.when((rel >= 0) & (rel < RB))
        def _():
            xs[pl.ds(rel, 1), :] = lat[c : c + 1, :].astype(F32)

    g = both(pk_own, pk_oth, shard, 0, H)
    b = both(pk_own, pk_oth, shard, H, H)
    x = xs[...]
    xb[...] = x.astype(BF)
    cen = x - jnp.mean(x, axis=1, keepdims=True)
    var = jnp.mean(cen * cen, axis=1, keepdims=True)
    n = (cen * lax.rsqrt(var + norm_epsilon) * g + b).astype(BF)
    ns[...] = n
    normed[...] = n
    nrm_send[...] = ns[:, half(1 - shard, H)]
    project(n, ws, pk_own, pk_oth, shard, 1 - shard, send)


def ln_send(scal, hid, lat, pk_own, pk_oth, w_own, w_oth):
    L, D = hid.shape
    H = D // 2
    RB = L // 2
    NP = pk_own.shape[1]
    rows = lambda n: pl.BlockSpec((RB, n), lambda r, s: (r, 0))
    w = [
        pl.BlockSpec((H, H), lambda r, s, j=j: (0, 2 * j + 1 - s[0]), pipeline_mode=pl.Buffered(1)) for j in range(3)
    ]
    return call(
        functools.partial(ln_send_kernel, L=L), "ln_send", (2,),
        [rows(D), whole(lat.shape), whole((1, NP)), whole((1, NP))] + w + w,
        [rows(3 * H), rows(D), rows(H), rows(D)],
        (sds((L, 3 * H), BF), sds((L, D), BF), sds((L, H), BF), sds((L, D), BF)),
        [pltpu.VMEM((RB, D), F32), pltpu.VMEM((RB, D), BF), pltpu.VMEM((D, 3 * H), BF)],
        cost(6 * L * D * H, 6e6),
        (scal, hid, lat, pk_own, pk_oth, w_own, w_own, w_own, w_oth, w_oth, w_oth),
    )


def own_kernel(scal, normed, pk_own, pk_oth, qo, ko, vo, qt, kt, vt, keep, ws):
    H = qo.shape[0]
    shard = scal[0]

    @pl.when(pl.program_id(0) == 0)
    def _():
        for j, (o, t) in enumerate(((qo, qt), (ko, kt), (vo, vt))):
            ws[half(shard, H), j * H : (j + 1) * H] = o[...]
            ws[half(1 - shard, H), j * H : (j + 1) * H] = t[...]

    project(normed[...], ws, pk_own, pk_oth, shard, shard, keep)


def own_heads(scal, normed, pk_own, pk_oth, w_own, w_oth):
    L, D = normed.shape
    H = D // 2
    RB = L // 2
    NP = pk_own.shape[1]
    rows = lambda n: pl.BlockSpec((RB, n), lambda r, s: (r, 0))
    w = [pl.BlockSpec((H, H), lambda r, s, j=j: (0, 2 * j + s[0]), pipeline_mode=pl.Buffered(1)) for j in range(3)]
    return call(
        own_kernel, "own_heads", (2,),
        [rows(D), whole((1, NP)), whole((1, NP))] + w + w, rows(3 * H), sds((L, 3 * H), BF),
        [pltpu.VMEM((D, 3 * H), BF)],
        cost(6 * L * D * H, 4e6),
        (scal, normed, pk_own, pk_oth, w_own, w_own, w_own, w_oth, w_oth, w_oth),
    )


def join(dst, own, oth, shard):
    L = own.shape[0]
    dst[half(shard, L), :] = own[...]
    dst[half(1 - shard, L), :] = oth[...]


def attn_fwd_kernel(scal, qa, ka, va, qb, kb_, vb, o_keep, o_send, lse_ref, qs, ks, vs, os_, stat, *, L, RB):
    p_id = pl.program_id(0)
    shard = scal[0]
    pfx = scal[1]
    join(qs, qa, qb, shard)
    join(ks, ka, kb_, shard)
    join(vs, va, vb, shard)
    lane = lax.broadcasted_iota(jnp.int32, (RB, 128), 1)
    c = 0.125 * LOG2E
    HB = L // RB

    for r in range(2 * HB):
        q = qs[r * RB : (r + 1) * RB, :]
        outs = []
        for hh in range(2):
            sel = (lane < 64) if hh == 0 else (lane >= 64)
            qm = jnp.where(sel, q, jnp.zeros_like(q))
            pieces = []
            if r >= HB:
                pieces.append((dot_nt(qm, ks[0:L, :]) * c, vs[0:L, :]))
            for kb in range(HB) if r < HB else range(HB, r + 1):
                s = dot_nt(qm, ks[kb * RB : (kb + 1) * RB, :]) * c
                if kb >= r:
                    col = lax.broadcasted_iota(jnp.int32, (RB, RB), 1) + kb * RB
                    row = lax.broadcasted_iota(jnp.int32, (RB, RB), 0) + r * RB
                    keep = (col <= row) | (col < pfx) if r < HB else (col <= row)
                    s = jnp.where(keep, s, masked_score)
                pieces.append((s, vs[kb * RB : (kb + 1) * RB, :]))
            m = functools.reduce(jnp.maximum, [jnp.max(s, axis=1, keepdims=True) for s, _ in pieces])
            total = jnp.zeros((RB, 1), F32)
            o = jnp.zeros((RB, 128), F32)
            for s, v in pieces:
                p = jnp.exp2(s - m)
                total = total + jnp.sum(p, axis=1, keepdims=True)
                o = o + dot_nn(p.astype(BF), v)
            outs.append(o * (1.0 / total))
            lse = m + jnp.log2(total)
            here = lane == p_id * 2 + hh
            stat[r * RB : (r + 1) * RB, :] = jnp.where(here, lse, stat[r * RB : (r + 1) * RB, :])
        os_[r * RB : (r + 1) * RB, :] = jnp.where(lane < 64, outs[0], outs[1]).astype(BF)

    o_keep[...] = os_[half(shard, L), :]
    o_send[...] = os_[half(1 - shard, L), :]

    @pl.when(p_id == pl.num_programs(0) - 1)
    def _():
        lse_ref[...] = stat[...].T[0:8, :]


def attn_fwd(scal, keep, recv):
    L, W = keep.shape
    H = W // 3
    NP = H // 128
    spec = lambda off: pl.BlockSpec((L, 128), lambda p, s: (0, p + off))
    seq = pltpu.VMEM((2 * L, 128), BF)
    o = sds((L, H), BF)
    return call(
        functools.partial(attn_fwd_kernel, L=L, RB=256), "attn_fwd", (NP,),
        [spec(0), spec(NP), spec(2 * NP)] * 2,
        [spec(0), spec(0), pl.BlockSpec((8, 2 * L), lambda p, s: (0, 0))],
        (o, o, sds((8, 2 * L), F32)),
        [seq, seq, seq, seq, pltpu.VMEM((2 * L, 128), F32)],
        cost(12e9, 4e6, 6e6),
        (scal, keep, keep, keep, recv, recv, recv),
    )


def attn_bwd_kernel(
    scal, qa, ka, va, qb, kb_, vb, ga, gb, aa, ab, lse_ref, d_own, d_oth, qs, ks, vs, gs, as_, dks, dvs, dqt, *, L, KB, p0
):
    shard = scal[0]
    pfx = scal[1]
    join(qs, qa, qb, shard)
    join(ks, ka, kb_, shard)
    join(vs, va, vb, shard)
    join(gs, ga, gb, shard)
    join(as_, aa, ab, shard)
    S = 2 * L
    c = 0.125 * LOG2E
    lane = lax.broadcasted_iota(jnp.int32, (S, 128), 1)
    q = qs[...]
    do = gs[...]
    z = jnp.zeros_like(q)
    qm = [jnp.where(lane < 64, q, z), jnp.where(lane >= 64, q, z)]
    dm = [jnp.where(lane < 64, do, z), jnp.where(lane >= 64, do, z)]
    prod = do.astype(F32) * as_[...].astype(F32)
    hi = prod.astype(BF)
    lo = (prod - hi.astype(F32)).astype(BF)
    head = lax.broadcasted_iota(jnp.int32, (16, 128), 0)
    plane = lax.broadcasted_iota(jnp.int32, (16, 128), 1)
    pick = jnp.where((plane >= head * 64) & (plane < head * 64 + 64), 1.0, 0.0).astype(BF)
    delta = dot_nt(pick, hi) + dot_nt(pick, lo)
    hb = (pl.program_id(0) + p0) * 2
    lse = [lse_ref[pl.ds(hb + hh, 1), :] for hh in range(2)]
    dl = [delta[hh : hh + 1, :] for hh in range(2)]
    dqt[...] = jnp.zeros_like(dqt)

    for kb in range(S // KB):
        rows = slice(kb * KB, (kb + 1) * KB)
        k = ks[rows, :]
        v = vs[rows, :]
        kt = k.T
        dk = None
        dv = None
        spans = [(0, L), (L, S)] if kb * KB < L else [(kb * KB, S)]
        for q0, q1 in spans:
            mask = None
            if q0 <= kb * KB:
                key = lax.broadcasted_iota(jnp.int32, (KB, q1 - q0), 0) + kb * KB
                qry = lax.broadcasted_iota(jnp.int32, (KB, q1 - q0), 1) + q0
                mask = (key <= qry) | (key < pfx) if q1 <= L else key <= qry
            for hh in range(2):
                st = dot_nt(k, qm[hh][q0:q1, :]) * c
                if mask is not None:
                    st = jnp.where(mask, st, masked_score)
                pt = jnp.exp2(st - lse[hh][:, q0:q1])
                dpt = dot_nt(v, dm[hh][q0:q1, :])
                dst = (pt * (dpt - dl[hh][:, q0:q1])).astype(BF)
                a = dot_nn(pt.astype(BF), dm[hh][q0:q1, :])
                b = dot_nn(dst, qm[hh][q0:q1, :])
                dv = a if dv is None else dv + a
                dk = b if dk is None else dk + b
                dqt[hh * 64 : (hh + 1) * 64, q0:q1] += dot_nn(kt[hh * 64 : (hh + 1) * 64, :], dst)
        dks[rows, :] = (dk * 0.125).astype(BF)
        dvs[rows, :] = dv.astype(BF)

    gs[...] = (dqt[...].T * 0.125).astype(BF)
    for j, src in enumerate((gs, dks, dvs)):
        d_own[j] = src[half(shard, L), :]
        d_oth[j] = src[half(1 - shard, L), :]


def attn_bwd(scal, keep, recv, ga_keep, ga_recv, att_keep, att_send, lse, p0, count):
    L, W = keep.shape
    H = W // 3
    NP = H // 128
    spec = lambda off: pl.BlockSpec((L, 128), lambda p, s: (0, p + off))
    seq = pltpu.VMEM((2 * L, 128), BF)
    o = sds((3, L, count * 128), BF)
    ospec = pl.BlockSpec((3, L, 128), lambda p, s: (0, 0, p))
    share = count / NP
    return call(
        functools.partial(attn_bwd_kernel, L=L, KB=256, p0=p0), "attn_bwd", (count,),
        [spec(p0), spec(NP + p0), spec(2 * NP + p0)] * 2 + [spec(p0)] * 4 + [pl.BlockSpec((8, 2 * L), lambda p, s: (0, 0))],
        [ospec, ospec], (o, o),
        [seq] * 7 + [pltpu.VMEM((128, 2 * L), F32)],
        cost(24e9 * share, 8e6 * share, 6e6 * share),
        (scal, keep, keep, keep, recv, recv, recv, ga_keep, ga_recv, att_keep, att_send, lse),
    )


def ffn_kernel(
    scal, ak, ar, xb, dz, pk_own, pk_oth, wp_own, wp_oth, wf_own, wf_oth, wo_own, wo_oth,
    act_keep, act_send, gp, n2_keep, n2_send, out, dmid, gb, ga_keep, ga_send, sfc, sums,
    ns, mid, yacc, gacc, wfs, wos, as_, *, T,
):
    t = pl.program_id(0)
    last = pl.num_programs(0) - 1
    NH = pl.num_programs(0) // 2
    shard = scal[0]
    L, D = xb.shape
    H = D // 2
    FH = wo_own.shape[0] * NH
    o_bp, o_g2, o_b2, o_bf = 4 * H, 5 * H, 6 * H, 7 * H
    o_bo = 11 * H
    RB = L // 4

    @pl.when(t == 0)
    def _():
        g = both(pk_own, pk_oth, shard, o_g2, H)
        b = both(pk_own, pk_oth, shard, o_b2, H)
        bp = both(pk_own, pk_oth, shard, o_bp, H)
        mid[...] = dot_nn(ak[...], wp_own[...]) + dot_nn(ar[...], wp_oth[...])
        for i in range(4):
            rows = slice(i * RB, (i + 1) * RB)
            m = mid[rows, :] + xb[rows, :].astype(F32) + bp
            mid[rows, :] = m
            cen = m - jnp.mean(m, axis=1, keepdims=True)
            var = jnp.mean(cen * cen, axis=1, keepdims=True)
            ns[rows, :] = (cen * lax.rsqrt(var + norm_epsilon) * g + b).astype(BF)
        n2_keep[...] = ns[:, half(shard, H)]
        n2_send[...] = ns[:, half(1 - shard, H)]
        yacc[...] = jnp.zeros_like(yacc)
        gacc[...] = jnp.zeros_like(gacc)

    wfs[half(shard, H), :] = wf_own[...]
    wfs[half(1 - shard, H), :] = wf_oth[...]

    @pl.when(t < NH)
    def _():
        wos[...] = wo_own[...]

    @pl.when(t >= NH)
    def _():
        wos[...] = wo_oth[...]

    at = pl.ds(pl.multiple_of(o_bf + lax.rem(t, NH) * T, 128), T)
    bias = jnp.where(t < NH, pk_own[0:1, at].astype(F32), pk_oth[0:1, at].astype(F32))
    CB = T // 2
    for i in range(2):
        cols = slice(i * CB, (i + 1) * CB)
        u = dot_nn(ns[...], wfs[:, cols]) + bias[:, cols]
        ga = dot_nt(dz[...], wos[cols, :])
        u2 = u * u
        th = jnp.tanh(u * (gelu_root + (gelu_root * gelu_cubic) * u2))
        hp = 0.5 + 0.5 * th
        av = u * hp
        slope = hp + av * ((1.0 - th) * (gelu_root + (3.0 * gelu_root * gelu_cubic) * u2))
        as_[:, cols] = av.astype(BF)
        g = (ga * slope).astype(BF)
        gp[:, cols] = g
        total = jnp.sum(g.astype(F32), axis=0, keepdims=True)
        sfc[:, cols] = jnp.broadcast_to(total, (sfc.shape[0], CB))
    yacc[...] += dot_nn(as_[...], wos[...])
    gacc[...] += dot_nt(gp[...], wfs[...])

    @pl.when(t < NH)
    def _():
        act_keep[...] = as_[...]

    @pl.when(t >= NH)
    def _():
        act_send[...] = as_[...]

    @pl.when(t == last)
    def _():
        g2 = both(pk_own, pk_oth, shard, o_g2, H)
        bo = both(pk_own, pk_oth, shard, o_bo, H)
        sums[...] = jnp.zeros_like(sums)
        for i in range(4):
            rows = slice(i * RB, (i + 1) * RB)
            m = mid[rows, :]
            out[rows, :] = (yacc[rows, :] + m + bo).astype(BF)
            gn = gacc[rows, :]
            cen = m - jnp.mean(m, axis=1, keepdims=True)
            r = lax.rsqrt(jnp.mean(cen * cen, axis=1, keepdims=True) + norm_epsilon)
            n = cen * r
            e = gn * g2
            dzv = dz[rows, :].astype(F32)
            g = dzv + r * (e - jnp.mean(e, axis=1, keepdims=True) - n * jnp.mean(e * n, axis=1, keepdims=True))
            dmid[rows, :] = g
            gbv = g.astype(BF)
            gb[rows, :] = gbv
            sums[0:1, :] += jnp.sum(gbv.astype(F32), axis=0, keepdims=True)
            sums[1:2, :] += jnp.sum(gn * n, axis=0, keepdims=True)
            sums[2:3, :] += jnp.sum(gn, axis=0, keepdims=True)
            sums[3:4, :] += jnp.sum(dzv, axis=0, keepdims=True)
        ga_keep[...] = dot_nt(gb[...], wp_own[...]).astype(BF)
        ga_send[...] = dot_nt(gb[...], wp_oth[...]).astype(BF)


def ffn(scal, ak, ar, xb, dz, pk_own, pk_oth, wp_own, wp_oth, wf_own, wf_oth, wo_own, wo_oth):
    L, D = xb.shape
    H = D // 2
    FH = wo_own.shape[0]
    T = 512
    NH = FH // T
    NP = pk_own.shape[1]
    tile = lambda t, s: jnp.where(t < NH, s[0] * NH + t, (1 - s[0]) * NH + t - NH)
    first = lambda t: jnp.minimum(t, NH - 1)
    second = lambda t: jnp.maximum(t - NH, 0)
    const = lambda *shape: pl.BlockSpec(shape, lambda t, s: (0,) * len(shape))
    wf = pl.BlockSpec((H, T), lambda t, s: (0, tile(t, s)))
    return call(
        functools.partial(ffn_kernel, T=T), "ffn", (2 * NH,),
        [whole((L, H)), whole((L, H)), whole((L, D)), whole((L, D)), whole((1, NP)), whole((1, NP)), whole((H, D)), whole((H, D)),
         wf, wf, pl.BlockSpec((T, D), lambda t, s: (first(t), 0)), pl.BlockSpec((T, D), lambda t, s: (second(t), 0))],
        [pl.BlockSpec((L, T), lambda t, s: (0, first(t))), pl.BlockSpec((L, T), lambda t, s: (0, second(t))),
         pl.BlockSpec((L, T), lambda t, s: (0, tile(t, s))), const(L, H), const(L, H), const(L, D), const(L, D), const(L, D),
         const(L, H), const(L, H), pl.BlockSpec((8, T), lambda t, s: (0, tile(t, s))), const(8, D)],
        (sds((L, FH), BF), sds((L, FH), BF), sds((L, 2 * FH), BF), sds((L, H), BF), sds((L, H), BF), sds((L, D), BF),
         sds((L, D), F32), sds((L, D), BF), sds((L, H), BF), sds((L, H), BF), sds((8, 2 * FH), F32), sds((8, D), F32)),
        [pltpu.VMEM((L, D), BF), pltpu.VMEM((L, D), F32), pltpu.VMEM((L, D), F32), pltpu.VMEM((L, D), F32),
         pltpu.VMEM((D, T), BF), pltpu.VMEM((T, D), BF), pltpu.VMEM((L, T), BF)],
        cost(2 * L * D * (2 * D + 8 * FH), 24e6, 1.5e6),
        (scal, ak, ar, xb, dz, pk_own, pk_oth, wp_own, wp_oth, wf_own, wf_oth, wo_own, wo_oth),
    )


def pair_of(i, s):
    return ((i + 2) & 3) ^ (s[8] >> 1)


def turns(i, outs):
    return (i == 0, i == 1, i >= 2) if len(outs) == 3 else (i < 2, i >= 2)


def put_pair(scal, left, right, *outs):
    H = left.shape[0]
    i = pl.program_id(0)
    flip = scal[8] & 1
    for out, here in zip(outs, turns(i, outs)):

        @pl.when(here)
        def _():
            out[half(flip, H), :] = left
            out[half(1 - flip, H), :] = right


def pair_specs(H, split):
    block = lambda at: pl.BlockSpec((2 * H, H), lambda i, s: (at(i), 0))
    keep = block(lambda i: jnp.maximum(i - 2, 0))
    if split:
        first = block(lambda i: 0)
        return [first, first, keep], (sds((2 * H, H), BF), sds((2 * H, H), BF), sds((4 * H, H), BF))
    return [block(lambda i: jnp.minimum(i, 1)), keep], (sds((4 * H, H), BF), sds((4 * H, H), BF))


def grad_pair_kernel(scal, a_own, a_oth, b_own, b_oth, *outs):
    H = a_own.shape[1]
    val = (dot_tn(a_own[...], b_own[...]) + dot_tn(a_oth[...], b_oth[...])).astype(BF)
    put_pair(scal, val[:, :H], val[:, H:], *outs)


def grad_rows(scal, a_own, a_oth, b_own, b_oth):
    K, M = a_own.shape
    N = b_own.shape[1]
    H = N // 2
    a = pl.BlockSpec((K, H), lambda i, s: (0, pair_of(i, s)))
    specs, shape = pair_specs(H, False)
    return call(
        grad_pair_kernel, "grad_rows", (4,), [a, a, whole((K, N)), whole((K, N))], specs, shape, [],
        cost(4 * K * M * N, 4 * K * (M + N) + 2 * M * N), (scal, a_own, a_oth, b_own, b_oth),
    )


def grad_cols(scal, a_own, a_oth, b_own, b_oth):
    K, M = a_own.shape
    N = b_own.shape[1]
    b = pl.BlockSpec((K, 2 * M), lambda i, s: (0, pair_of(i, s)))
    specs, shape = pair_specs(M, False)
    return call(
        grad_pair_kernel, "grad_cols", (4,), [whole((K, M)), whole((K, M)), b, b], specs, shape, [],
        cost(4 * K * M * N, 4 * K * (M + N) + 2 * M * N), (scal, a_own, a_oth, b_own, b_oth),
    )


def grad_attn_kernel(scal, n_own, n_oth, a_own, a_oth, gb_own, gb_oth, *refs):
    H = n_own.shape[1]
    shard = scal[0]
    outs = refs[-3:]
    n = (len(refs) - 3) // 4
    l_own, l_oth, r_own, r_oth = [refs[n * j : n * j + n] for j in range(4)]
    w = pair_of(pl.program_id(0), scal)
    flip = scal[8] & 1

    def put(rows, value):
        i = pl.program_id(0)
        for out, here in zip(outs, turns(i, outs)):

            @pl.when(here)
            def _():
                out[half(rows, H), :] = value

    def heads(parts):
        return jnp.concatenate([p[0] for p in parts], axis=1)

    @pl.when(w < 3)
    def _():
        mine = dot_tn(n_own[...], heads(l_own)) + dot_tn(n_oth[...], heads(l_oth))
        put(shard ^ flip, mine.astype(BF))
        theirs = dot_tn(n_own[...], heads(r_own)) + dot_tn(n_oth[...], heads(r_oth))
        put(1 - (shard ^ flip), theirs.astype(BF))

    @pl.when(w == 3)
    def _():
        val = (dot_tn(a_own[...], gb_own[...]) + dot_tn(a_oth[...], gb_oth[...])).astype(BF)
        put(flip, val[:, :H])
        put(1 - flip, val[:, H:])


def grad_attn(scal, normed, n_oth, a_own, a_oth, gb_own, gb_oth, *parts):
    K, H = n_oth.shape
    D = 2 * H
    d = [pl.BlockSpec((1, K, p.shape[2]), lambda i, s: (jnp.minimum(pair_of(i, s), 2), 0, 0)) for p in parts]
    n = pl.BlockSpec((K, H), lambda i, s: (0, s[0]), pipeline_mode=pl.Buffered(1))
    w = whole((K, H))
    specs, shape = pair_specs(H, True)
    return call(
        grad_attn_kernel, "grad_attn", (4,), [n, w, w, w, whole((K, D)), whole((K, D))] + d, specs, shape, [],
        cost(32 * K * H * H, 16e6), (scal, normed, n_oth, a_own, a_oth, gb_own, gb_oth, *parts),
    )


def last_kernel(
    scal, d_own, d_oth, xb, dmid, pk_own, pk_oth, w_own, w_oth, sfc, sums,
    gh, glat, s_keep, s_send, gi, es, ds_, vec, *, L,
):
    r_id = pl.program_id(0)
    shard = scal[0]
    RB, D = xb.shape
    H = D // 2
    FF = sfc.shape[1]
    for j in range(3):
        ds_[:, half(2 * j + shard, H)] = d_own[j]
        ds_[:, half(2 * j + 1 - shard, H)] = d_oth[j]
    d = ds_[...]
    es[:, half(shard, H)] = dot_nt(d, w_own[...])
    es[:, half(1 - shard, H)] = dot_nt(d, w_oth[...])
    gn = es[...]
    x = xb[...].astype(F32)
    cen = x - jnp.mean(x, axis=1, keepdims=True)
    r = lax.rsqrt(jnp.mean(cen * cen, axis=1, keepdims=True) + norm_epsilon)
    n = cen * r
    e = gn * both(pk_own, pk_oth, shard, 0, H)
    gi[...] = dmid[...] + r * (e - jnp.mean(e, axis=1, keepdims=True) - n * jnp.mean(e * n, axis=1, keepdims=True))

    @pl.when(r_id == 0)
    def _():
        glat[...] = jnp.zeros_like(glat)
        vec[...] = jnp.zeros_like(vec)

    row0 = shard * L + r_id * RB
    for c in range(6):
        rel = scal[2 + c] - row0

        @pl.when((rel >= 0) & (rel < RB))
        def _():
            glat[c : c + 1, :] = gi[pl.ds(rel, 1), :]
            gi[pl.ds(rel, 1), :] = jnp.zeros((1, D), F32)

    gh[...] = gi[...].astype(BF)
    vec[0:1, 0:D] += jnp.sum(gn * n, axis=0, keepdims=True)
    vec[1:2, 0:D] += jnp.sum(gn, axis=0, keepdims=True)
    vec[2:3, 0:D] += jnp.sum(ds_[:, 0:D].astype(F32), axis=0, keepdims=True)
    vec[2:3, D : 2 * D] += jnp.sum(ds_[:, 2 * D : 3 * D].astype(F32), axis=0, keepdims=True)

    @pl.when(r_id == pl.num_programs(0) - 1)
    def _():
        for side in range(2):
            owner = shard if side == 0 else 1 - shard
            out = s_keep if side == 0 else s_send
            one = half(owner, H)
            wide = vec[2:3, half(owner, D)]
            fc = sfc[0:1, half(owner, FF // 2)]
            flat = jnp.concatenate(
                [vec[0:1, one], vec[1:2, one], wide, sums[0:1, one], sums[1:2, one], sums[2:3, one], fc, sums[3:4, one]], axis=1
            )
            out[...] = jnp.zeros_like(out)
            for k in range(flat.shape[1] // (2 * D)):
                out[k : k + 1, :] = flat[:, k * 2 * D : (k + 1) * 2 * D]


def last_block(scal, parts, xb, dmid, pk_own, pk_oth, w_own, w_oth, sfc, sums):
    L, D = xb.shape
    H = D // 2
    RB = L // 2
    NP = pk_own.shape[1]
    rows = lambda n: pl.BlockSpec((RB, n), lambda r, s: (r, 0))
    const = lambda *shape: pl.BlockSpec(shape, lambda r, s: (0, 0))
    d = [pl.BlockSpec((3, RB, p.shape[2]), lambda r, s: (0, r, 0)) for p in parts]
    return call(
        functools.partial(last_kernel, L=L), "last_block", (2,),
        d + [rows(D), rows(D), whole((1, NP)), whole((1, NP)), whole((H, 3 * D)), whole((H, 3 * D)), whole(sfc.shape), whole(sums.shape)],
        [rows(D), const(8, D), const(8, 2 * D), const(8, 2 * D)],
        (sds((L, D), BF), sds((8, D), F32), sds((8, 2 * D), F32), sds((8, 2 * D), F32)),
        [pltpu.VMEM((RB, D), F32), pltpu.VMEM((RB, D), F32), pltpu.VMEM((RB, 3 * D), BF), pltpu.VMEM((8, 2 * D), F32)],
        cost(6 * L * D * D, 12e6),
        (scal, *parts, xb, dmid, pk_own, pk_oth, w_own, w_oth, sfc, sums),
    )


def final_kernel(scal, *refs, wide):
    pos = refs[:8]
    outs = refs[8:]
    H = pos[0].shape[1]
    w = pl.program_id(0)
    k = w ^ (scal[8] >> 1)
    flip = scal[8] & 1
    for j in range(4):
        for f in range(2):
            for o, here in enumerate((w < wide, w >= wide) if len(outs) == 2 else (True,)):

                @pl.when((k == j) & (flip == f) & here)
                def _():
                    outs[o][:, :H] = pos[2 * j + f][...].astype(F32)
                    outs[o][:, H:] = pos[2 * j + 1 - f][...].astype(F32)


def final(scal, pos, out_specs, out_shape, wide=4):
    H = pos[0].shape[1]
    return call(
        functools.partial(final_kernel, wide=wide), "final", (4,), [whole((H, H))] * 8, out_specs, out_shape, [],
        cost(8 * H * H, 48 * H * H), (scal, *pos),
    )


def unpack_kernel(a, b, *outs):
    W = a.shape[1]
    at = 0
    for out in outs:
        n = out.shape[0]
        done = 0
        while done < n:
            row, col = divmod(at + done, W)
            w = min(n - done, W - col)
            out[done : done + w] = (a[row : row + 1, col : col + w] + b[row : row + 1, col : col + w]).reshape(w)
            done += w
        at += n


def unpack(a, b, sizes):
    return pl.pallas_call(
        unpack_kernel,
        out_shape=[sds((n,), F32) for n in sizes],
        compiler_params=params(),
        cost_estimate=cost(1, 1),
        name="unpack",
    )(a, b)


def swap(x):
    return lax.ppermute(x, "shard", [(0, 1), (1, 0)])


def hop(x, first, second):
    pairs = []
    for rep in range(16):
        pairs.append((2 * rep, 2 * (rep ^ first)))
        pairs.append((2 * rep + 1, 2 * (rep ^ second) + 1))
    return lax.ppermute(x, ("rep", "shard"), pairs)


def gate(x, *deps):
    return lax.optimization_barrier((x, *deps))[0]


def gated(xs, *deps):
    return list(lax.optimization_barrier((*xs, *deps))[: len(xs)])


def total(*xs):
    return functools.reduce(lambda a, b: a + b, [x.astype(F32) for x in xs]).astype(BF)


class Reduce:
    def __init__(self, *parts):
        *sends, self.keep, self.dims = parts
        self.H = self.keep.shape[1]
        self.r1 = [hop(send, *self.dims[0]) for send in sends]

    def rows(self, x, a, b):
        return x[a * self.H : b * self.H]

    def hop2(self, *deps):
        self.r1[-1] = gate(self.r1[-1], *deps)
        n = self.r1[-1].shape[0] // self.H
        send = total(self.rows(self.keep, 2, 4), self.rows(self.r1[-1], n - 2, n))
        self.r2 = hop(send, *self.dims[1])
        return send

    def hop3(self, *deps):
        self.r1[0], self.r2 = gated((self.r1[0], self.r2), *deps)
        send = total(self.rows(self.keep, 1, 2), self.rows(self.r1[0], 1, 2), self.rows(self.r2, 1, 2))
        self.r3 = hop(send, *self.dims[2])
        return send

    def hop4(self, *deps):
        self.x = total(self.rows(self.keep, 0, 1), self.rows(self.r1[0], 0, 1), self.rows(self.r2, 0, 1), gate(self.r3, *deps))
        self.r4 = hop(self.x, 8, 8)
        return self.x

    def hop5(self, *deps):
        p0 = total(self.x, gate(self.r4, *deps))
        self.pos = [p0] + [None] * 7
        for i in range(3):
            self.pos[1 << i] = hop(p0, *self.dims[2 - i])
        return p0

    def take(self, i, *deps):
        if i >= 2:
            deps += (self.pos[2 + i],)
        self.pos[i] = gate(self.pos[i], *deps)
        if i == 1:
            self.pos[3] = hop(self.pos[1], *self.dims[1])
        self.pos[4 + i] = hop(self.pos[i], *self.dims[0])
        return self.pos[i]


def pair_device(
    hidden, latents, latent_pos, prefix, ln1_gain, ln1_bias, w_qkv, b_qv, w_proj, b_proj,
    ln2_gain, ln2_bias, w_fc, b_fc, w_out, b_out, cotangent,
):
    _, L, D = hidden.shape
    H = D // 2
    shard = lax.axis_index("shard").astype(jnp.int32)
    rep = lax.axis_index("rep").astype(jnp.int32)
    bit0, bit1, bit2 = rep & 1, (rep >> 1) & 1, (rep >> 2) & 1
    high = jnp.where(shard == 0, bit0, bit1)
    low = jnp.where(shard == 0, bit1, bit0)
    code = high * 4 + low * 2 + bit2
    dims = ((1, 2), (2, 1), (4, 4))
    lead = lax.broadcasted_iota(jnp.int32, (16,), 0)
    scal = jnp.where(lead == 0, shard, jnp.where(lead == 1, prefix[0], jnp.where(lead == 8, code, 0)))
    scal = lax.dynamic_update_slice(scal, latent_pos[0].astype(jnp.int32), (2,))

    pk_own = pack([ln1_gain, ln1_bias, b_qv, b_proj, ln2_gain, ln2_bias, b_fc, b_out])
    pk_oth = swap(pk_own)
    qkv_oth = swap(w_qkv)
    hid = hidden[0]
    dz = cotangent[0]
    lat = latents[0]

    send, normed, nrm_send, xb = ln_send(scal, hid, lat, pk_own, pk_oth, w_qkv, qkv_oth)
    recv = swap(send)
    keep = own_heads(scal, normed, pk_own, pk_oth, w_qkv, qkv_oth)
    proj_oth, fc_oth, out_oth, nrm_recv, dz_oth = [swap(gate(a, recv, keep)) for a in (w_proj, w_fc, w_out, nrm_send, dz)]
    att_keep, att_send, lse = attn_fwd(scal, keep, recv)
    att_recv = swap(att_send)
    dz_oth, nrm_recv, xb = gated((dz_oth, nrm_recv, xb))
    act_keep, act_send, gp, n2_keep, n2_send, block_out, dmid, gb, ga_keep, ga_send, sfc, sums = ffn(
        scal, att_keep, att_recv, xb, dz, pk_own, pk_oth, w_proj, proj_oth, w_fc, fc_oth, w_out, out_oth
    )
    act_recv = swap(act_send)
    ga_recv = swap(ga_send)
    gp_oth = swap(gate(gp, act_recv))
    n2_recv = swap(gate(n2_send, act_recv))
    gb_oth = swap(gate(gb, act_recv))
    s_out, k_out = grad_rows(scal, act_keep, act_recv, dz, dz_oth)
    r_out = Reduce(s_out, k_out, dims)
    s_fc, k_fc = grad_cols(scal, n2_keep, gate(n2_recv, k_out), gp, gp_oth)
    r_fc = Reduce(s_fc, k_fc, dims)
    d_own, d_oth = attn_bwd(scal, keep, recv, ga_keep, gate(ga_recv, k_fc), att_keep, att_send, lse, 0, H // 128)
    e_own, e_oth = swap(d_oth), swap(d_own)
    tok = r_out.hop2(d_own)
    tok = r_fc.hop2(tok)
    a_c, b_c, k_c = grad_attn(scal, normed, nrm_recv, att_keep, att_send, gb, gb_oth, d_own, d_oth, gate(e_own, tok), e_oth)
    r_c = Reduce(a_c, b_c, k_c, dims)
    tok = r_out.hop3(k_c)
    tok = r_out.hop4(tok)
    tok = r_fc.hop3(tok)
    gh, glat, s_keep, s_send = last_block(
        scal, (d_own, gate(e_own, tok)), xb, dmid, pk_own, pk_oth, w_qkv, qkv_oth, sfc, sums
    )
    s_recv = swap(s_send)
    glat_oth = swap(glat)
    tok = r_c.hop2(gh)
    tok = r_fc.hop4(tok)
    tok = r_c.hop3(tok)
    tok = r_out.hop5(tok)
    tok = r_c.hop4(tok)
    tok = r_fc.hop5(tok)
    small = s_keep + gate(s_recv, tok)
    glat = glat + gate(glat_oth, tok)
    for bits in ((1, 2), (2, 1), (4, 4)):
        small = small + hop(small, *bits)
    m = hop(small, 8, 8)
    r_c.hop5(tok)
    for i in (1, 2, 3):
        r_out.take(i)
    r_fc.take(1, r_out.pos[4], r_out.pos[5])
    r_fc.take(2, r_out.pos[6])
    r_fc.take(3, r_out.pos[7])
    r_c.take(1, r_fc.pos[4], r_fc.pos[5])
    g_out = final(scal, r_out.pos, pl.BlockSpec((H, D), lambda w, s: (w, 0)), sds((4 * H, D), F32))
    r_c.take(2, r_fc.pos[6], g_out)
    tok = r_c.take(3, r_fc.pos[7])
    g_fc = final(scal, gated(r_fc.pos, tok), pl.BlockSpec((H, D), lambda w, s: (0, w)), sds((H, 4 * D), F32))
    g_qkv, g_proj = final(
        scal, gated(r_c.pos, g_fc), [pl.BlockSpec((H, D), lambda w, s: (0, jnp.minimum(w, 2))), pl.BlockSpec((H, D), lambda w, s: (0, 0))],
        (sds((H, 3 * D), F32), sds((H, D), F32)), 3,
    )
    sizes = [v.shape[0] for v in (ln1_gain, ln1_bias, b_qv, b_proj, ln2_gain, ln2_bias, b_fc, b_out)]
    vecs = unpack(small, gate(m, tok), sizes)
    return (
        block_out[None], gh[None], glat[None, :6], vecs[0], vecs[1], g_qkv, vecs[2], g_proj, vecs[3],
        vecs[4], vecs[5], g_fc, vecs[6], g_out, vecs[7],
    )


def layer_norm(values, norm_gain, norm_shift):
    average = jnp.mean(values, axis=-1, keepdims=True)
    centered = values - average
    variance = jnp.mean(centered * centered, axis=-1, keepdims=True)
    return centered * lax.rsqrt(variance + norm_epsilon) * norm_gain + norm_shift


def gelu_tanh(values):
    return (
        0.5
        * values
        * (1.0 + jnp.tanh(gelu_root * (values + gelu_cubic * values * values * values)))
    )


def head_scores(query_one, key_one, query_pos, key_pos, prefix_one, score_scale):
    scores = (
        jnp.einsum("qhe,khe->hqk", query_one, key_one, preferred_element_type=jnp.float32)
        * score_scale
    )
    causal = (key_pos[None, :] <= query_pos[:, None])[None]
    in_prefix = (key_pos < prefix_one)[None, None, :]
    return jnp.where(causal | in_prefix, scores, masked_score)


def per_device(
    hidden,
    latents,
    latent_pos,
    prefix,
    ln1_gain,
    ln1_bias,
    w_qkv,
    b_qv,
    w_proj,
    b_proj,
    ln2_gain,
    ln2_bias,
    w_fc,
    b_fc,
    w_out,
    b_out,
    cotangent,
):
    seq_count, local_len, model_width = hidden.shape
    head_dim = model_width // HEADS
    score_scale = head_dim ** (-0.5)
    row_start = lax.axis_index("shard") * local_len
    gathered = (
        lax.all_gather(ln1_gain, "shard", axis=0, tiled=True),
        lax.all_gather(ln1_bias, "shard", axis=0, tiled=True),
        lax.all_gather(w_qkv, "shard", axis=0, tiled=True),
        lax.all_gather(b_qv, "shard", axis=0, tiled=True),
        lax.all_gather(w_proj, "shard", axis=0, tiled=True),
        lax.all_gather(b_proj, "shard", axis=0, tiled=True),
        lax.all_gather(ln2_gain, "shard", axis=0, tiled=True),
        lax.all_gather(ln2_bias, "shard", axis=0, tiled=True),
        lax.all_gather(w_fc, "shard", axis=0, tiled=True),
        lax.all_gather(b_fc, "shard", axis=0, tiled=True),
        lax.all_gather(w_out, "shard", axis=0, tiled=True),
        lax.all_gather(b_out, "shard", axis=0, tiled=True),
    )
    (
        full_ln1_gain,
        full_ln1_bias,
        full_qkv,
        full_b_qv,
        full_proj,
        full_b_proj,
        full_ln2_gain,
        full_ln2_bias,
        full_fc,
        full_b_fc,
        complete_output,
        full_b_out,
    ) = gathered
    row_ids = row_start + jnp.arange(local_len, dtype=jnp.int32)
    latent_matches = row_ids[None, :, None] == latent_pos[:, None, :]
    positioned_rows = jnp.einsum(
        "ety,eyw->etw",
        latent_matches.astype(jnp.bfloat16),
        latents,
        preferred_element_type=jnp.float32,
    )
    replaced = jnp.any(latent_matches, axis=-1)[..., None]
    block_in = jnp.where(replaced, positioned_rows, hidden.astype(jnp.float32)).reshape(
        -1, model_width
    )
    normed, back_norm_one = jax.vjp(
        layer_norm, block_in, full_ln1_gain.astype(jnp.float32), full_ln1_bias.astype(jnp.float32)
    )
    normed_low = normed.astype(jnp.bfloat16)
    bias_full = jnp.concatenate(
        [
            full_b_qv[:model_width].astype(jnp.float32),
            jnp.zeros((model_width,), jnp.float32),
            full_b_qv[model_width:].astype(jnp.float32),
        ]
    )
    projected = (
        jnp.dot(normed_low, full_qkv, preferred_element_type=jnp.float32) + bias_full
    ).astype(jnp.bfloat16)
    query_heads = projected[:, :model_width].reshape(seq_count, local_len, HEADS, head_dim)
    key_local = projected[:, model_width : 2 * model_width].reshape(
        seq_count, local_len, model_width
    )
    value_local = projected[:, 2 * model_width :].reshape(seq_count, local_len, model_width)
    key_full, value_full = (
        lax.all_gather(key_local, "shard", axis=1, tiled=True),
        lax.all_gather(value_local, "shard", axis=1, tiled=True),
    )
    full_len = key_full.shape[1]
    key_heads = key_full.reshape(seq_count, full_len, HEADS, head_dim)
    value_heads = value_full.reshape(seq_count, full_len, HEADS, head_dim)
    key_pos_all = jnp.arange(full_len, dtype=jnp.int32)

    def forward_seq(items):
        query_one, key_one, value_one, prefix_one = items
        scores = head_scores(query_one, key_one, row_ids, key_pos_all, prefix_one, score_scale)
        row_peak = jnp.max(scores, axis=-1, keepdims=True)
        single_logsumexp = row_peak + jnp.log(
            jnp.sum(jnp.exp(scores - row_peak), axis=-1, keepdims=True)
        )
        probs_low = jnp.exp(scores - single_logsumexp).astype(jnp.bfloat16)
        mixed = jnp.einsum("hqk,khe->qhe", probs_low, value_one, preferred_element_type=jnp.float32)
        return (mixed.astype(jnp.bfloat16), single_logsumexp)

    attended_heads, log_total = lax.map(forward_seq, (query_heads, key_heads, value_heads, prefix))
    attended = attended_heads.reshape(-1, model_width)
    middle = (
        block_in
        + jnp.dot(attended, full_proj, preferred_element_type=jnp.float32)
        + full_b_proj.astype(jnp.float32)
    )
    normed_two, back_norm_two = jax.vjp(
        layer_norm, middle, full_ln2_gain.astype(jnp.float32), full_ln2_bias.astype(jnp.float32)
    )
    normed_two_low = normed_two.astype(jnp.bfloat16)
    pre_act = jnp.dot(
        normed_two_low, full_fc, preferred_element_type=jnp.float32
    ) + full_b_fc.astype(jnp.float32)
    activated, back_gelu = jax.vjp(gelu_tanh, pre_act)
    activated_low = activated.astype(jnp.bfloat16)
    block_out = (
        middle
        + jnp.dot(activated_low, complete_output, preferred_element_type=jnp.float32)
        + full_b_out.astype(jnp.float32)
    )
    block_out = block_out.reshape(seq_count, local_len, model_width).astype(jnp.bfloat16)
    back_qkv, back_proj, back_fc, back_out = (
        lax.all_gather(w_qkv, "shard", axis=0, tiled=True),
        lax.all_gather(w_proj, "shard", axis=0, tiled=True),
        lax.all_gather(w_fc, "shard", axis=0, tiled=True),
        lax.all_gather(w_out, "shard", axis=0, tiled=True),
    )
    grad_top = cotangent.reshape(-1, model_width)
    grad_w_out = jnp.einsum(
        "nf,nd->fd", activated_low, grad_top, preferred_element_type=jnp.float32
    )
    grad_b_out = jnp.sum(grad_top.astype(jnp.float32), axis=0)
    grad_act = jnp.einsum("nd,fd->nf", grad_top, back_out, preferred_element_type=jnp.float32)
    (grad_pre,) = back_gelu(grad_act)
    grad_pre_low = grad_pre.astype(jnp.bfloat16)
    grad_w_fc = jnp.einsum(
        "nd,nf->df", normed_two_low, grad_pre_low, preferred_element_type=jnp.float32
    )
    grad_b_fc = jnp.sum(grad_pre_low.astype(jnp.float32), axis=0)
    grad_normed_two = jnp.einsum(
        "nf,df->nd", grad_pre_low, back_fc, preferred_element_type=jnp.float32
    )
    grad_mid_norm, grad_ln2_gain, grad_ln2_bias = back_norm_two(grad_normed_two)
    grad_mid = grad_top.astype(jnp.float32) + grad_mid_norm
    grad_branch_low = grad_mid.astype(jnp.bfloat16)
    grad_w_proj = jnp.einsum(
        "nd,ne->de", attended, grad_branch_low, preferred_element_type=jnp.float32
    )
    grad_b_proj = jnp.sum(grad_branch_low.astype(jnp.float32), axis=0)
    grad_att = jnp.einsum(
        "ne,de->nd", grad_branch_low, back_proj, preferred_element_type=jnp.float32
    )
    grad_att_low = grad_att.astype(jnp.bfloat16).reshape(seq_count, local_len, HEADS, head_dim)

    def backward_sequence(items):
        query_one, key_one, value_one, prefix_one, single_logsumexp, upstream = items
        scores = head_scores(query_one, key_one, row_ids, key_pos_all, prefix_one, score_scale)
        attn_probs = jnp.exp(scores - single_logsumexp)
        grad_value_one = jnp.einsum(
            "hqk,qhe->khe",
            attn_probs.astype(jnp.bfloat16),
            upstream,
            preferred_element_type=jnp.float32,
        )
        grad_probs = jnp.einsum(
            "qhe,khe->hqk", upstream, value_one, preferred_element_type=jnp.float32
        )
        delta_one = jnp.sum(grad_probs * attn_probs, axis=-1, keepdims=True)
        grad_scores = (attn_probs * (grad_probs - delta_one)).astype(jnp.bfloat16)
        grad_query_one = (
            jnp.einsum("hqk,khe->qhe", grad_scores, key_one, preferred_element_type=jnp.float32)
            * score_scale
        )
        grad_key_one = (
            jnp.einsum("hqk,qhe->khe", grad_scores, query_one, preferred_element_type=jnp.float32)
            * score_scale
        )
        return (
            grad_query_one,
            grad_key_one.reshape(full_len, model_width),
            grad_value_one.reshape(full_len, model_width),
        )

    grad_query, grad_key_all, grad_value_all = lax.map(
        backward_sequence, (query_heads, key_heads, value_heads, prefix, log_total, grad_att_low)
    )
    grad_key_own, grad_value_own = (
        lax.psum_scatter(
            grad_key_all.astype(jnp.bfloat16), "shard", scatter_dimension=1, tiled=True
        ).astype(jnp.float32),
        lax.psum_scatter(
            grad_value_all.astype(jnp.bfloat16), "shard", scatter_dimension=1, tiled=True
        ).astype(jnp.float32),
    )
    grad_query_low = grad_query.reshape(-1, model_width).astype(jnp.bfloat16)
    grad_key_low = grad_key_own.reshape(-1, model_width).astype(jnp.bfloat16)
    grad_value_low = grad_value_own.reshape(-1, model_width).astype(jnp.bfloat16)
    grad_projected = jnp.concatenate([grad_query_low, grad_key_low, grad_value_low], axis=1)
    grad_b_qv = jnp.concatenate(
        [
            jnp.sum(grad_query_low.astype(jnp.float32), axis=0),
            jnp.sum(grad_value_low.astype(jnp.float32), axis=0),
        ]
    )
    grad_w_qkv = jnp.einsum(
        "nd,ne->de", normed_low, grad_projected, preferred_element_type=jnp.float32
    )
    grad_normed = jnp.einsum(
        "ne,de->nd", grad_projected, back_qkv, preferred_element_type=jnp.float32
    )
    grad_in_norm, grad_ln1_gain, grad_ln1_bias = back_norm_one(grad_normed)
    block_gradient = (grad_mid + grad_in_norm).reshape(seq_count, local_len, model_width)
    latent_terms = jnp.einsum(
        "inv,inz->ivz",
        latent_matches.astype(jnp.float32),
        block_gradient,
        precision=lax.Precision.HIGHEST,
    )
    grad_latents = lax.psum(latent_terms, "shard")
    grad_hidden = jnp.where(replaced, 0.0, block_gradient).astype(jnp.bfloat16)
    shares = (
        lax.psum_scatter(
            grad_ln1_gain.astype(jnp.bfloat16), "shard", scatter_dimension=0, tiled=True
        ).astype(jnp.float32),
        lax.psum_scatter(
            grad_ln1_bias.astype(jnp.bfloat16), "shard", scatter_dimension=0, tiled=True
        ).astype(jnp.float32),
        lax.psum_scatter(
            grad_w_qkv.astype(jnp.bfloat16), "shard", scatter_dimension=0, tiled=True
        ).astype(jnp.float32),
        lax.psum_scatter(
            grad_b_qv.astype(jnp.bfloat16), "shard", scatter_dimension=0, tiled=True
        ).astype(jnp.float32),
        lax.psum_scatter(
            grad_w_proj.astype(jnp.bfloat16), "shard", scatter_dimension=0, tiled=True
        ).astype(jnp.float32),
        lax.psum_scatter(
            grad_b_proj.astype(jnp.bfloat16), "shard", scatter_dimension=0, tiled=True
        ).astype(jnp.float32),
        lax.psum_scatter(
            grad_ln2_gain.astype(jnp.bfloat16), "shard", scatter_dimension=0, tiled=True
        ).astype(jnp.float32),
        lax.psum_scatter(
            grad_ln2_bias.astype(jnp.bfloat16), "shard", scatter_dimension=0, tiled=True
        ).astype(jnp.float32),
        lax.psum_scatter(
            grad_w_fc.astype(jnp.bfloat16), "shard", scatter_dimension=0, tiled=True
        ).astype(jnp.float32),
        lax.psum_scatter(
            grad_b_fc.astype(jnp.bfloat16), "shard", scatter_dimension=0, tiled=True
        ).astype(jnp.float32),
        lax.psum_scatter(
            grad_w_out.astype(jnp.bfloat16), "shard", scatter_dimension=0, tiled=True
        ).astype(jnp.float32),
        lax.psum_scatter(
            grad_b_out.astype(jnp.bfloat16), "shard", scatter_dimension=0, tiled=True
        ).astype(jnp.float32),
    )
    summed = (
        lax.psum(shares[0].astype(jnp.bfloat16), "rep").astype(jnp.float32),
        lax.psum(shares[1].astype(jnp.bfloat16), "rep").astype(jnp.float32),
        lax.psum(shares[2].astype(jnp.bfloat16), "rep").astype(jnp.float32),
        lax.psum(shares[3].astype(jnp.bfloat16), "rep").astype(jnp.float32),
        lax.psum(shares[4].astype(jnp.bfloat16), "rep").astype(jnp.float32),
        lax.psum(shares[5].astype(jnp.bfloat16), "rep").astype(jnp.float32),
        lax.psum(shares[6].astype(jnp.bfloat16), "rep").astype(jnp.float32),
        lax.psum(shares[7].astype(jnp.bfloat16), "rep").astype(jnp.float32),
        lax.psum(shares[8].astype(jnp.bfloat16), "rep").astype(jnp.float32),
        lax.psum(shares[9].astype(jnp.bfloat16), "rep").astype(jnp.float32),
        lax.psum(shares[10].astype(jnp.bfloat16), "rep").astype(jnp.float32),
        lax.psum(shares[11].astype(jnp.bfloat16), "rep").astype(jnp.float32),
    )
    (
        total_ln1_gain,
        total_ln1_bias,
        total_w_qkv,
        total_b_qv,
        total_w_proj,
        total_b_proj,
        total_ln2_gain,
        total_ln2_bias,
        total_w_fc,
        total_b_fc,
        total_w_out,
        total_b_out,
    ) = summed
    return (
        block_out,
        grad_hidden,
        grad_latents,
        total_ln1_gain,
        total_ln1_bias,
        total_w_qkv,
        total_b_qv,
        total_w_proj,
        total_b_proj,
        total_ln2_gain,
        total_ln2_bias,
        total_w_fc,
        total_b_fc,
        total_w_out,
        total_b_out,
    )


def solution(mesh):
    sizes = dict(mesh.shape)
    paired = sizes["rep"] == 16 and sizes["shard"] == 2
    body = pair_device if paired else per_device
    in_specs = (
        P("rep", "shard", None),
        P("rep", None, None),
        P("rep", None),
        P("rep"),
        P("shard"),
        P("shard"),
        P("shard", None),
        P("shard"),
        P("shard", None),
        P("shard"),
        P("shard"),
        P("shard"),
        P("shard", None),
        P("shard"),
        P("shard", None),
        P("shard"),
        P("rep", "shard", None),
    )
    out_specs = (
        P("rep", "shard", None),
        P("rep", "shard", None),
        P("rep", None, None),
        P("shard"),
        P("shard"),
        P("shard", None),
        P("shard"),
        P("shard", None),
        P("shard"),
        P("shard"),
        P("shard"),
        P("shard", None),
        P("shard"),
        P("shard", None),
        P("shard"),
    )
    return jax.shard_map(
        body, mesh=mesh, in_specs=in_specs, out_specs=out_specs, check_vma=False
    )
```

```python
import functools
import jax
import jax.numpy as jnp
from jax import lax
from jax.experimental import pallas as pl
from jax.experimental.pallas import tpu as pltpu
from jax.sharding import PartitionSpec as P

HEADS = 12
F32 = jnp.float32
BF = jnp.bfloat16

norm_epsilon = 1e-05
gelu_root = 0.7978845608028654
gelu_cubic = 0.044715
masked_score = -1e30
LOG2E = 1.4426950408889634


def dot_nt(a, b):
    return lax.dot_general(a, b, (((1,), (1,)), ((), ())), preferred_element_type=F32)


def dot_nn(a, b):
    return lax.dot_general(a, b, (((1,), (0,)), ((), ())), preferred_element_type=F32)


def dot_tn(a, b):
    return lax.dot_general(a, b, (((0,), (0,)), ((), ())), preferred_element_type=F32)


def params(semantics=None, mb=16):
    return pltpu.CompilerParams(dimension_semantics=semantics, vmem_limit_bytes=mb * 1024 * 1024)


def cost(flops, nbytes, trans=0):
    return pl.CostEstimate(flops=1, bytes_accessed=1, transcendentals=0)


def whole(shape):
    return pl.BlockSpec(shape, lambda *_: (0,) * len(shape), pipeline_mode=pl.Buffered(1))


def both(own, oth, shard, a, n):
    o = own[0:1, a : a + n].astype(F32)
    t = oth[0:1, a : a + n].astype(F32)
    first = jnp.where(shard == 0, o, t)
    second = jnp.where(shard == 0, t, o)
    return jnp.concatenate([first, second], axis=1)


def half(i, n):
    return pl.ds(pl.multiple_of(i * n, n), n)


def call(kernel, name, grid, in_specs, out_specs, out_shape, scratch, est, args, mb=16):
    return pl.pallas_call(
        kernel,
        out_shape=out_shape,
        grid_spec=pltpu.PrefetchScalarGridSpec(
            num_scalar_prefetch=1, grid=grid, in_specs=in_specs, out_specs=out_specs, scratch_shapes=scratch
        ),
        compiler_params=params(("arbitrary",), mb),
        cost_estimate=est,
        name=name,
    )(*args)


sds = jax.ShapeDtypeStruct


def pack(vecs):
    n = sum(v.shape[0] for v in vecs)
    at = 0
    out = []
    for v in vecs:
        out.append(jnp.pad(v, (at, n - at - v.shape[0])))
        at += v.shape[0]
    return functools.reduce(jnp.add, out)[None, :]


def qv_bias(pk_own, pk_oth, shard, which, heads):
    H = pk_own.shape[1] // 12
    a = pk_own[0:1, 2 * H : 4 * H].astype(F32)
    b = pk_oth[0:1, 2 * H : 4 * H].astype(F32)
    src = jnp.where(shard == which, a, b)
    return jnp.where(heads == 0, src[:, :H], src[:, H:])


def project(n, ws, pk_own, pk_oth, shard, heads, out):
    H = ws.shape[0] // 2
    for j in range(3):
        y = dot_nn(n, ws[:, j * H : (j + 1) * H])
        if j != 1:
            y = y + qv_bias(pk_own, pk_oth, shard, j // 2, heads)
        out[:, j * H : (j + 1) * H] = y.astype(BF)


def ln_send_kernel(
    scal, hid, lat, pk_own, pk_oth, qo, ko, vo, qt, kt, vt, send, normed, nrm_send, xb, xs, ns, ws, *, L
):
    r = pl.program_id(0)
    RB, D = hid.shape
    H = D // 2
    shard = scal[0]

    @pl.when(r == 0)
    def _():
        for j, (o, t) in enumerate(((qo, qt), (ko, kt), (vo, vt))):
            ws[half(shard, H), j * H : (j + 1) * H] = o[...]
            ws[half(1 - shard, H), j * H : (j + 1) * H] = t[...]

    xs[...] = hid[...].astype(F32)
    row0 = shard * L + r * RB
    for c in range(6):
        rel = scal[2 + c] - row0

        @pl.when((rel >= 0) & (rel < RB))
        def _():
            xs[pl.ds(rel, 1), :] = lat[c : c + 1, :].astype(F32)

    g = both(pk_own, pk_oth, shard, 0, H)
    b = both(pk_own, pk_oth, shard, H, H)
    x = xs[...]
    xb[...] = x.astype(BF)
    cen = x - jnp.mean(x, axis=1, keepdims=True)
    var = jnp.mean(cen * cen, axis=1, keepdims=True)
    n = (cen * lax.rsqrt(var + norm_epsilon) * g + b).astype(BF)
    ns[...] = n
    normed[...] = n
    nrm_send[...] = ns[:, half(1 - shard, H)]
    project(n, ws, pk_own, pk_oth, shard, 1 - shard, send)


def ln_send(scal, hid, lat, pk_own, pk_oth, w_own, w_oth):
    L, D = hid.shape
    H = D // 2
    RB = L // 2
    NP = pk_own.shape[1]
    rows = lambda n: pl.BlockSpec((RB, n), lambda r, s: (r, 0))
    w = [
        pl.BlockSpec((H, H), lambda r, s, j=j: (0, 2 * j + 1 - s[0]), pipeline_mode=pl.Buffered(1)) for j in range(3)
    ]
    return call(
        functools.partial(ln_send_kernel, L=L), "ln_send", (2,),
        [rows(D), whole(lat.shape), whole((1, NP)), whole((1, NP))] + w + w,
        [rows(3 * H), rows(D), rows(H), rows(D)],
        (sds((L, 3 * H), BF), sds((L, D), BF), sds((L, H), BF), sds((L, D), BF)),
        [pltpu.VMEM((RB, D), F32), pltpu.VMEM((RB, D), BF), pltpu.VMEM((D, 3 * H), BF)],
        cost(6 * L * D * H, 6e6),
        (scal, hid, lat, pk_own, pk_oth, w_own, w_own, w_own, w_oth, w_oth, w_oth),
    )


def own_kernel(scal, normed, pk_own, pk_oth, qo, ko, vo, qt, kt, vt, keep, ws):
    H = qo.shape[0]
    shard = scal[0]

    @pl.when(pl.program_id(0) == 0)
    def _():
        for j, (o, t) in enumerate(((qo, qt), (ko, kt), (vo, vt))):
            ws[half(shard, H), j * H : (j + 1) * H] = o[...]
            ws[half(1 - shard, H), j * H : (j + 1) * H] = t[...]

    project(normed[...], ws, pk_own, pk_oth, shard, shard, keep)


def own_heads(scal, normed, pk_own, pk_oth, w_own, w_oth):
    L, D = normed.shape
    H = D // 2
    RB = L // 2
    NP = pk_own.shape[1]
    rows = lambda n: pl.BlockSpec((RB, n), lambda r, s: (r, 0))
    w = [pl.BlockSpec((H, H), lambda r, s, j=j: (0, 2 * j + s[0]), pipeline_mode=pl.Buffered(1)) for j in range(3)]
    return call(
        own_kernel, "own_heads", (2,),
        [rows(D), whole((1, NP)), whole((1, NP))] + w + w, rows(3 * H), sds((L, 3 * H), BF),
        [pltpu.VMEM((D, 3 * H), BF)],
        cost(6 * L * D * H, 4e6),
        (scal, normed, pk_own, pk_oth, w_own, w_own, w_own, w_oth, w_oth, w_oth),
    )


def join(dst, own, oth, shard):
    L = own.shape[0]
    dst[half(shard, L), :] = own[...]
    dst[half(1 - shard, L), :] = oth[...]


def attn_fwd_kernel(scal, qa, ka, va, qb, kb_, vb, o_keep, o_send, lse_ref, qs, ks, vs, os_, stat, *, L, RB):
    p_id = pl.program_id(0)
    shard = scal[0]
    pfx = scal[1]
    join(qs, qa, qb, shard)
    join(ks, ka, kb_, shard)
    join(vs, va, vb, shard)
    lane = lax.broadcasted_iota(jnp.int32, (RB, 128), 1)
    c = 0.125 * LOG2E
    HB = L // RB

    for r in range(2 * HB):
        q = qs[r * RB : (r + 1) * RB, :]
        outs = []
        for hh in range(2):
            sel = (lane < 64) if hh == 0 else (lane >= 64)
            qm = jnp.where(sel, q, jnp.zeros_like(q))
            pieces = []
            if r >= HB:
                pieces.append((dot_nt(qm, ks[0:L, :]) * c, vs[0:L, :]))
            for kb in range(HB) if r < HB else range(HB, r + 1):
                s = dot_nt(qm, ks[kb * RB : (kb + 1) * RB, :]) * c
                if kb >= r:
                    col = lax.broadcasted_iota(jnp.int32, (RB, RB), 1) + kb * RB
                    row = lax.broadcasted_iota(jnp.int32, (RB, RB), 0) + r * RB
                    keep = (col <= row) | (col < pfx) if r < HB else (col <= row)
                    s = jnp.where(keep, s, masked_score)
                pieces.append((s, vs[kb * RB : (kb + 1) * RB, :]))
            m = functools.reduce(jnp.maximum, [jnp.max(s, axis=1, keepdims=True) for s, _ in pieces])
            total = jnp.zeros((RB, 1), F32)
            o = jnp.zeros((RB, 128), F32)
            for s, v in pieces:
                p = jnp.exp2(s - m)
                total = total + jnp.sum(p, axis=1, keepdims=True)
                o = o + dot_nn(p.astype(BF), v)
            outs.append(o * (1.0 / total))
            lse = m + jnp.log2(total)
            here = lane == p_id * 2 + hh
            stat[r * RB : (r + 1) * RB, :] = jnp.where(here, lse, stat[r * RB : (r + 1) * RB, :])
        os_[r * RB : (r + 1) * RB, :] = jnp.where(lane < 64, outs[0], outs[1]).astype(BF)

    o_keep[...] = os_[half(shard, L), :]
    o_send[...] = os_[half(1 - shard, L), :]

    @pl.when(p_id == pl.num_programs(0) - 1)
    def _():
        lse_ref[...] = stat[...].T[0:8, :]


def attn_fwd(scal, keep, recv):
    L, W = keep.shape
    H = W // 3
    NP = H // 128
    spec = lambda off: pl.BlockSpec((L, 128), lambda p, s: (0, p + off))
    seq = pltpu.VMEM((2 * L, 128), BF)
    o = sds((L, H), BF)
    return call(
        functools.partial(attn_fwd_kernel, L=L, RB=256), "attn_fwd", (NP,),
        [spec(0), spec(NP), spec(2 * NP)] * 2,
        [spec(0), spec(0), pl.BlockSpec((8, 2 * L), lambda p, s: (0, 0))],
        (o, o, sds((8, 2 * L), F32)),
        [seq, seq, seq, seq, pltpu.VMEM((2 * L, 128), F32)],
        cost(12e9, 4e6, 6e6),
        (scal, keep, keep, keep, recv, recv, recv),
    )


def attn_bwd_kernel(
    scal, qa, ka, va, qb, kb_, vb, ga, gb, aa, ab, lse_ref, d_own, d_oth, qs, ks, vs, gs, as_, dks, dvs, dqt, *, L, KB, p0
):
    shard = scal[0]
    pfx = scal[1]
    join(qs, qa, qb, shard)
    join(ks, ka, kb_, shard)
    join(vs, va, vb, shard)
    join(gs, ga, gb, shard)
    join(as_, aa, ab, shard)
    S = 2 * L
    c = 0.125 * LOG2E
    lane = lax.broadcasted_iota(jnp.int32, (S, 128), 1)
    q = qs[...]
    do = gs[...]
    z = jnp.zeros_like(q)
    qm = [jnp.where(lane < 64, q, z), jnp.where(lane >= 64, q, z)]
    dm = [jnp.where(lane < 64, do, z), jnp.where(lane >= 64, do, z)]
    prod = do.astype(F32) * as_[...].astype(F32)
    hi = prod.astype(BF)
    lo = (prod - hi.astype(F32)).astype(BF)
    head = lax.broadcasted_iota(jnp.int32, (16, 128), 0)
    plane = lax.broadcasted_iota(jnp.int32, (16, 128), 1)
    pick = jnp.where((plane >= head * 64) & (plane < head * 64 + 64), 1.0, 0.0).astype(BF)
    delta = dot_nt(pick, hi) + dot_nt(pick, lo)
    hb = (pl.program_id(0) + p0) * 2
    lse = [lse_ref[pl.ds(hb + hh, 1), :] for hh in range(2)]
    dl = [delta[hh : hh + 1, :] for hh in range(2)]
    dqt[...] = jnp.zeros_like(dqt)

    for kb in range(S // KB):
        rows = slice(kb * KB, (kb + 1) * KB)
        k = ks[rows, :]
        v = vs[rows, :]
        kt = k.T
        dk = None
        dv = None
        spans = [(0, L), (L, S)] if kb * KB < L else [(kb * KB, S)]
        for q0, q1 in spans:
            mask = None
            if q0 <= kb * KB:
                key = lax.broadcasted_iota(jnp.int32, (KB, q1 - q0), 0) + kb * KB
                qry = lax.broadcasted_iota(jnp.int32, (KB, q1 - q0), 1) + q0
                mask = (key <= qry) | (key < pfx) if q1 <= L else key <= qry
            for hh in range(2):
                st = dot_nt(k, qm[hh][q0:q1, :]) * c
                if mask is not None:
                    st = jnp.where(mask, st, masked_score)
                pt = jnp.exp2(st - lse[hh][:, q0:q1])
                dpt = dot_nt(v, dm[hh][q0:q1, :])
                dst = (pt * (dpt - dl[hh][:, q0:q1])).astype(BF)
                a = dot_nn(pt.astype(BF), dm[hh][q0:q1, :])
                b = dot_nn(dst, qm[hh][q0:q1, :])
                dv = a if dv is None else dv + a
                dk = b if dk is None else dk + b
                dqt[hh * 64 : (hh + 1) * 64, q0:q1] += dot_nn(kt[hh * 64 : (hh + 1) * 64, :], dst)
        dks[rows, :] = (dk * 0.125).astype(BF)
        dvs[rows, :] = dv.astype(BF)

    gs[...] = (dqt[...].T * 0.125).astype(BF)
    for j, src in enumerate((gs, dks, dvs)):
        d_own[j] = src[half(shard, L), :]
        d_oth[j] = src[half(1 - shard, L), :]


def attn_bwd(scal, keep, recv, ga_keep, ga_recv, att_keep, att_send, lse, p0, count):
    L, W = keep.shape
    H = W // 3
    NP = H // 128
    spec = lambda off: pl.BlockSpec((L, 128), lambda p, s: (0, p + off))
    seq = pltpu.VMEM((2 * L, 128), BF)
    o = sds((3, L, count * 128), BF)
    ospec = pl.BlockSpec((3, L, 128), lambda p, s: (0, 0, p))
    share = count / NP
    return call(
        functools.partial(attn_bwd_kernel, L=L, KB=256, p0=p0), "attn_bwd", (count,),
        [spec(p0), spec(NP + p0), spec(2 * NP + p0)] * 2 + [spec(p0)] * 4 + [pl.BlockSpec((8, 2 * L), lambda p, s: (0, 0))],
        [ospec, ospec], (o, o),
        [seq] * 7 + [pltpu.VMEM((128, 2 * L), F32)],
        cost(24e9 * share, 8e6 * share, 6e6 * share),
        (scal, keep, keep, keep, recv, recv, recv, ga_keep, ga_recv, att_keep, att_send, lse),
    )


def ffn_kernel(
    scal, ak, ar, xb, dz, pk_own, pk_oth, wp_own, wp_oth, wf_own, wf_oth, wo_own, wo_oth,
    act_keep, act_send, gp, n2_keep, n2_send, out, dmid, gb, ga_keep, ga_send, sfc, sums,
    ns, mid, yacc, gacc, wfs, wos, as_, *, T,
):
    t = pl.program_id(0)
    last = pl.num_programs(0) - 1
    NH = pl.num_programs(0) // 2
    shard = scal[0]
    L, D = xb.shape
    H = D // 2
    FH = wo_own.shape[0] * NH
    o_bp, o_g2, o_b2, o_bf = 4 * H, 5 * H, 6 * H, 7 * H
    o_bo = 11 * H
    RB = L // 4

    @pl.when(t == 0)
    def _():
        g = both(pk_own, pk_oth, shard, o_g2, H)
        b = both(pk_own, pk_oth, shard, o_b2, H)
        bp = both(pk_own, pk_oth, shard, o_bp, H)
        mid[...] = dot_nn(ak[...], wp_own[...]) + dot_nn(ar[...], wp_oth[...])
        for i in range(4):
            rows = slice(i * RB, (i + 1) * RB)
            m = mid[rows, :] + xb[rows, :].astype(F32) + bp
            mid[rows, :] = m
            cen = m - jnp.mean(m, axis=1, keepdims=True)
            var = jnp.mean(cen * cen, axis=1, keepdims=True)
            ns[rows, :] = (cen * lax.rsqrt(var + norm_epsilon) * g + b).astype(BF)
        n2_keep[...] = ns[:, half(shard, H)]
        n2_send[...] = ns[:, half(1 - shard, H)]
        yacc[...] = jnp.zeros_like(yacc)
        gacc[...] = jnp.zeros_like(gacc)

    wfs[half(shard, H), :] = wf_own[...]
    wfs[half(1 - shard, H), :] = wf_oth[...]

    @pl.when(t < NH)
    def _():
        wos[...] = wo_own[...]

    @pl.when(t >= NH)
    def _():
        wos[...] = wo_oth[...]

    at = pl.ds(pl.multiple_of(o_bf + lax.rem(t, NH) * T, 128), T)
    bias = jnp.where(t < NH, pk_own[0:1, at].astype(F32), pk_oth[0:1, at].astype(F32))
    CB = T // 2
    for i in range(2):
        cols = slice(i * CB, (i + 1) * CB)
        u = dot_nn(ns[...], wfs[:, cols]) + bias[:, cols]
        ga = dot_nt(dz[...], wos[cols, :])
        u2 = u * u
        th = jnp.tanh(u * (gelu_root + (gelu_root * gelu_cubic) * u2))
        hp = 0.5 + 0.5 * th
        av = u * hp
        slope = hp + av * ((1.0 - th) * (gelu_root + (3.0 * gelu_root * gelu_cubic) * u2))
        as_[:, cols] = av.astype(BF)
        g = (ga * slope).astype(BF)
        gp[:, cols] = g
        total = jnp.sum(g.astype(F32), axis=0, keepdims=True)
        sfc[:, cols] = jnp.broadcast_to(total, (sfc.shape[0], CB))
    yacc[...] += dot_nn(as_[...], wos[...])
    gacc[...] += dot_nt(gp[...], wfs[...])

    @pl.when(t < NH)
    def _():
        act_keep[...] = as_[...]

    @pl.when(t >= NH)
    def _():
        act_send[...] = as_[...]

    @pl.when(t == last)
    def _():
        g2 = both(pk_own, pk_oth, shard, o_g2, H)
        bo = both(pk_own, pk_oth, shard, o_bo, H)
        sums[...] = jnp.zeros_like(sums)
        for i in range(4):
            rows = slice(i * RB, (i + 1) * RB)
            m = mid[rows, :]
            out[rows, :] = (yacc[rows, :] + m + bo).astype(BF)
            gn = gacc[rows, :]
            cen = m - jnp.mean(m, axis=1, keepdims=True)
            r = lax.rsqrt(jnp.mean(cen * cen, axis=1, keepdims=True) + norm_epsilon)
            n = cen * r
            e = gn * g2
            dzv = dz[rows, :].astype(F32)
            g = dzv + r * (e - jnp.mean(e, axis=1, keepdims=True) - n * jnp.mean(e * n, axis=1, keepdims=True))
            dmid[rows, :] = g
            gbv = g.astype(BF)
            gb[rows, :] = gbv
            sums[0:1, :] += jnp.sum(gbv.astype(F32), axis=0, keepdims=True)
            sums[1:2, :] += jnp.sum(gn * n, axis=0, keepdims=True)
            sums[2:3, :] += jnp.sum(gn, axis=0, keepdims=True)
            sums[3:4, :] += jnp.sum(dzv, axis=0, keepdims=True)
        ga_keep[...] = dot_nt(gb[...], wp_own[...]).astype(BF)
        ga_send[...] = dot_nt(gb[...], wp_oth[...]).astype(BF)


def ffn(scal, ak, ar, xb, dz, pk_own, pk_oth, wp_own, wp_oth, wf_own, wf_oth, wo_own, wo_oth):
    L, D = xb.shape
    H = D // 2
    FH = wo_own.shape[0]
    T = 512
    NH = FH // T
    NP = pk_own.shape[1]
    tile = lambda t, s: jnp.where(t < NH, s[0] * NH + t, (1 - s[0]) * NH + t - NH)
    first = lambda t: jnp.minimum(t, NH - 1)
    second = lambda t: jnp.maximum(t - NH, 0)
    const = lambda *shape: pl.BlockSpec(shape, lambda t, s: (0,) * len(shape))
    wf = pl.BlockSpec((H, T), lambda t, s: (0, tile(t, s)))
    return call(
        functools.partial(ffn_kernel, T=T), "ffn", (2 * NH,),
        [whole((L, H)), whole((L, H)), whole((L, D)), whole((L, D)), whole((1, NP)), whole((1, NP)), whole((H, D)), whole((H, D)),
         wf, wf, pl.BlockSpec((T, D), lambda t, s: (first(t), 0)), pl.BlockSpec((T, D), lambda t, s: (second(t), 0))],
        [pl.BlockSpec((L, T), lambda t, s: (0, first(t))), pl.BlockSpec((L, T), lambda t, s: (0, second(t))),
         pl.BlockSpec((L, T), lambda t, s: (0, tile(t, s))), const(L, H), const(L, H), const(L, D), const(L, D), const(L, D),
         const(L, H), const(L, H), pl.BlockSpec((8, T), lambda t, s: (0, tile(t, s))), const(8, D)],
        (sds((L, FH), BF), sds((L, FH), BF), sds((L, 2 * FH), BF), sds((L, H), BF), sds((L, H), BF), sds((L, D), BF),
         sds((L, D), F32), sds((L, D), BF), sds((L, H), BF), sds((L, H), BF), sds((8, 2 * FH), F32), sds((8, D), F32)),
        [pltpu.VMEM((L, D), BF), pltpu.VMEM((L, D), F32), pltpu.VMEM((L, D), F32), pltpu.VMEM((L, D), F32),
         pltpu.VMEM((D, T), BF), pltpu.VMEM((T, D), BF), pltpu.VMEM((L, T), BF)],
        cost(2 * L * D * (2 * D + 8 * FH), 24e6, 1.5e6),
        (scal, ak, ar, xb, dz, pk_own, pk_oth, wp_own, wp_oth, wf_own, wf_oth, wo_own, wo_oth),
    )


def pair_of(i, s):
    return ((i + 2) & 3) ^ (s[8] >> 1)


def turns(i, outs):
    return (i == 0, i == 1, i >= 2) if len(outs) == 3 else (i < 2, i >= 2)


def put_pair(scal, left, right, *outs):
    H = left.shape[0]
    i = pl.program_id(0)
    flip = scal[8] & 1
    for out, here in zip(outs, turns(i, outs)):

        @pl.when(here)
        def _():
            out[half(flip, H), :] = left
            out[half(1 - flip, H), :] = right


def pair_specs(H, split):
    block = lambda at: pl.BlockSpec((2 * H, H), lambda i, s: (at(i), 0))
    keep = block(lambda i: jnp.maximum(i - 2, 0))
    if split:
        first = block(lambda i: 0)
        return [first, first, keep], (sds((2 * H, H), BF), sds((2 * H, H), BF), sds((4 * H, H), BF))
    return [block(lambda i: jnp.minimum(i, 1)), keep], (sds((4 * H, H), BF), sds((4 * H, H), BF))


def grad_pair_kernel(scal, a_own, a_oth, b_own, b_oth, *outs):
    H = a_own.shape[1]
    val = (dot_tn(a_own[...], b_own[...]) + dot_tn(a_oth[...], b_oth[...])).astype(BF)
    put_pair(scal, val[:, :H], val[:, H:], *outs)


def grad_rows(scal, a_own, a_oth, b_own, b_oth):
    K, M = a_own.shape
    N = b_own.shape[1]
    H = N // 2
    a = pl.BlockSpec((K, H), lambda i, s: (0, pair_of(i, s)))
    specs, shape = pair_specs(H, False)
    return call(
        grad_pair_kernel, "grad_rows", (4,), [a, a, whole((K, N)), whole((K, N))], specs, shape, [],
        cost(4 * K * M * N, 4 * K * (M + N) + 2 * M * N), (scal, a_own, a_oth, b_own, b_oth),
    )


def grad_cols(scal, a_own, a_oth, b_own, b_oth):
    K, M = a_own.shape
    N = b_own.shape[1]
    b = pl.BlockSpec((K, 2 * M), lambda i, s: (0, pair_of(i, s)))
    specs, shape = pair_specs(M, False)
    return call(
        grad_pair_kernel, "grad_cols", (4,), [whole((K, M)), whole((K, M)), b, b], specs, shape, [],
        cost(4 * K * M * N, 4 * K * (M + N) + 2 * M * N), (scal, a_own, a_oth, b_own, b_oth),
    )


def grad_attn_kernel(scal, n_own, n_oth, a_own, a_oth, gb_own, gb_oth, *refs):
    H = n_own.shape[1]
    shard = scal[0]
    outs = refs[-3:]
    n = (len(refs) - 3) // 4
    l_own, l_oth, r_own, r_oth = [refs[n * j : n * j + n] for j in range(4)]
    w = pair_of(pl.program_id(0), scal)
    flip = scal[8] & 1

    def put(rows, value):
        i = pl.program_id(0)
        for out, here in zip(outs, turns(i, outs)):

            @pl.when(here)
            def _():
                out[half(rows, H), :] = value

    def heads(parts):
        return jnp.concatenate([p[0] for p in parts], axis=1)

    @pl.when(w < 3)
    def _():
        mine = dot_tn(n_own[...], heads(l_own)) + dot_tn(n_oth[...], heads(l_oth))
        put(shard ^ flip, mine.astype(BF))
        theirs = dot_tn(n_own[...], heads(r_own)) + dot_tn(n_oth[...], heads(r_oth))
        put(1 - (shard ^ flip), theirs.astype(BF))

    @pl.when(w == 3)
    def _():
        val = (dot_tn(a_own[...], gb_own[...]) + dot_tn(a_oth[...], gb_oth[...])).astype(BF)
        put(flip, val[:, :H])
        put(1 - flip, val[:, H:])


def grad_attn(scal, normed, n_oth, a_own, a_oth, gb_own, gb_oth, *parts):
    K, H = n_oth.shape
    D = 2 * H
    d = [pl.BlockSpec((1, K, p.shape[2]), lambda i, s: (jnp.minimum(pair_of(i, s), 2), 0, 0)) for p in parts]
    n = pl.BlockSpec((K, H), lambda i, s: (0, s[0]), pipeline_mode=pl.Buffered(1))
    w = whole((K, H))
    specs, shape = pair_specs(H, True)
    return call(
        grad_attn_kernel, "grad_attn", (4,), [n, w, w, w, whole((K, D)), whole((K, D))] + d, specs, shape, [],
        cost(32 * K * H * H, 16e6), (scal, normed, n_oth, a_own, a_oth, gb_own, gb_oth, *parts),
    )


def last_kernel(
    scal, d_own, d_oth, xb, dmid, pk_own, pk_oth, w_own, w_oth, sfc, sums,
    gh, glat, s_keep, s_send, gi, es, ds_, vec, *, L,
):
    r_id = pl.program_id(0)
    shard = scal[0]
    RB, D = xb.shape
    H = D // 2
    FF = sfc.shape[1]
    for j in range(3):
        ds_[:, half(2 * j + shard, H)] = d_own[j]
        ds_[:, half(2 * j + 1 - shard, H)] = d_oth[j]
    d = ds_[...]
    es[:, half(shard, H)] = dot_nt(d, w_own[...])
    es[:, half(1 - shard, H)] = dot_nt(d, w_oth[...])
    gn = es[...]
    x = xb[...].astype(F32)
    cen = x - jnp.mean(x, axis=1, keepdims=True)
    r = lax.rsqrt(jnp.mean(cen * cen, axis=1, keepdims=True) + norm_epsilon)
    n = cen * r
    e = gn * both(pk_own, pk_oth, shard, 0, H)
    gi[...] = dmid[...] + r * (e - jnp.mean(e, axis=1, keepdims=True) - n * jnp.mean(e * n, axis=1, keepdims=True))

    @pl.when(r_id == 0)
    def _():
        glat[...] = jnp.zeros_like(glat)
        vec[...] = jnp.zeros_like(vec)

    row0 = shard * L + r_id * RB
    for c in range(6):
        rel = scal[2 + c] - row0

        @pl.when((rel >= 0) & (rel < RB))
        def _():
            glat[c : c + 1, :] = gi[pl.ds(rel, 1), :]
            gi[pl.ds(rel, 1), :] = jnp.zeros((1, D), F32)

    gh[...] = gi[...].astype(BF)
    vec[0:1, 0:D] += jnp.sum(gn * n, axis=0, keepdims=True)
    vec[1:2, 0:D] += jnp.sum(gn, axis=0, keepdims=True)
    vec[2:3, 0:D] += jnp.sum(ds_[:, 0:D].astype(F32), axis=0, keepdims=True)
    vec[2:3, D : 2 * D] += jnp.sum(ds_[:, 2 * D : 3 * D].astype(F32), axis=0, keepdims=True)

    @pl.when(r_id == pl.num_programs(0) - 1)
    def _():
        for side in range(2):
            owner = shard if side == 0 else 1 - shard
            out = s_keep if side == 0 else s_send
            one = half(owner, H)
            wide = vec[2:3, half(owner, D)]
            fc = sfc[0:1, half(owner, FF // 2)]
            flat = jnp.concatenate(
                [vec[0:1, one], vec[1:2, one], wide, sums[0:1, one], sums[1:2, one], sums[2:3, one], fc, sums[3:4, one]], axis=1
            )
            out[...] = jnp.zeros_like(out)
            for k in range(flat.shape[1] // (2 * D)):
                out[k : k + 1, :] = flat[:, k * 2 * D : (k + 1) * 2 * D]


def last_block(scal, parts, xb, dmid, pk_own, pk_oth, w_own, w_oth, sfc, sums):
    L, D = xb.shape
    H = D // 2
    RB = L // 2
    NP = pk_own.shape[1]
    rows = lambda n: pl.BlockSpec((RB, n), lambda r, s: (r, 0))
    const = lambda *shape: pl.BlockSpec(shape, lambda r, s: (0, 0))
    d = [pl.BlockSpec((3, RB, p.shape[2]), lambda r, s: (0, r, 0)) for p in parts]
    return call(
        functools.partial(last_kernel, L=L), "last_block", (2,),
        d + [rows(D), rows(D), whole((1, NP)), whole((1, NP)), whole((H, 3 * D)), whole((H, 3 * D)), whole(sfc.shape), whole(sums.shape)],
        [rows(D), const(8, D), const(8, 2 * D), const(8, 2 * D)],
        (sds((L, D), BF), sds((8, D), F32), sds((8, 2 * D), F32), sds((8, 2 * D), F32)),
        [pltpu.VMEM((RB, D), F32), pltpu.VMEM((RB, D), F32), pltpu.VMEM((RB, 3 * D), BF), pltpu.VMEM((8, 2 * D), F32)],
        cost(6 * L * D * D, 12e6),
        (scal, *parts, xb, dmid, pk_own, pk_oth, w_own, w_oth, sfc, sums),
    )


def final_kernel(scal, *refs, wide):
    pos = refs[:8]
    outs = refs[8:]
    H = pos[0].shape[1]
    w = pl.program_id(0)
    k = w ^ (scal[8] >> 1)
    flip = scal[8] & 1
    for j in range(4):
        for f in range(2):
            for o, here in enumerate((w < wide, w >= wide) if len(outs) == 2 else (True,)):

                @pl.when((k == j) & (flip == f) & here)
                def _():
                    outs[o][:, :H] = pos[2 * j + f][...].astype(F32)
                    outs[o][:, H:] = pos[2 * j + 1 - f][...].astype(F32)


def final(scal, pos, out_specs, out_shape, wide=4):
    H = pos[0].shape[1]
    return call(
        functools.partial(final_kernel, wide=wide), "final", (4,), [whole((H, H))] * 8, out_specs, out_shape, [],
        cost(8 * H * H, 48 * H * H), (scal, *pos),
    )


def unpack_kernel(a, b, *outs):
    W = a.shape[1]
    at = 0
    for out in outs:
        n = out.shape[0]
        done = 0
        while done < n:
            row, col = divmod(at + done, W)
            w = min(n - done, W - col)
            out[done : done + w] = (a[row : row + 1, col : col + w] + b[row : row + 1, col : col + w]).reshape(w)
            done += w
        at += n


def unpack(a, b, sizes):
    return pl.pallas_call(
        unpack_kernel,
        out_shape=[sds((n,), F32) for n in sizes],
        compiler_params=params(),
        cost_estimate=cost(1, 1),
        name="unpack",
    )(a, b)


def swap(x):
    return lax.ppermute(x, "shard", [(0, 1), (1, 0)])


def hop(x, first, second):
    pairs = []
    for rep in range(16):
        pairs.append((2 * rep, 2 * (rep ^ first)))
        pairs.append((2 * rep + 1, 2 * (rep ^ second) + 1))
    return lax.ppermute(x, ("rep", "shard"), pairs)


def gate(x, *deps):
    return lax.optimization_barrier((x, *deps))[0]


def gated(xs, *deps):
    return list(lax.optimization_barrier((*xs, *deps))[: len(xs)])


def total(*xs):
    return functools.reduce(lambda a, b: a + b, [x.astype(F32) for x in xs]).astype(BF)


class Reduce:
    def __init__(self, *parts):
        *sends, self.keep, self.dims = parts
        self.H = self.keep.shape[1]
        self.r1 = [hop(send, *self.dims[0]) for send in sends]

    def rows(self, x, a, b):
        return x[a * self.H : b * self.H]

    def hop2(self, *deps):
        self.r1[-1] = gate(self.r1[-1], *deps)
        n = self.r1[-1].shape[0] // self.H
        send = total(self.rows(self.keep, 2, 4), self.rows(self.r1[-1], n - 2, n))
        self.r2 = hop(send, *self.dims[1])
        return send

    def hop3(self, *deps):
        self.r1[0], self.r2 = gated((self.r1[0], self.r2), *deps)
        send = total(self.rows(self.keep, 1, 2), self.rows(self.r1[0], 1, 2), self.rows(self.r2, 1, 2))
        self.r3 = hop(send, *self.dims[2])
        return send

    def hop4(self, *deps):
        self.x = total(self.rows(self.keep, 0, 1), self.rows(self.r1[0], 0, 1), self.rows(self.r2, 0, 1), gate(self.r3, *deps))
        self.r4 = hop(self.x, 8, 8)
        return self.x

    def hop5(self, *deps):
        p0 = total(self.x, gate(self.r4, *deps))
        self.pos = [p0] + [None] * 7
        for i in range(3):
            self.pos[1 << i] = hop(p0, *self.dims[2 - i])
        return p0

    def take(self, i, *deps):
        if i >= 2:
            deps += (self.pos[2 + i],)
        self.pos[i] = gate(self.pos[i], *deps)
        if i == 1:
            self.pos[3] = hop(self.pos[1], *self.dims[1])
        self.pos[4 + i] = hop(self.pos[i], *self.dims[0])
        return self.pos[i]


def pair_device(
    hidden, latents, latent_pos, prefix, ln1_gain, ln1_bias, w_qkv, b_qv, w_proj, b_proj,
    ln2_gain, ln2_bias, w_fc, b_fc, w_out, b_out, cotangent,
):
    _, L, D = hidden.shape
    H = D // 2
    shard = lax.axis_index("shard").astype(jnp.int32)
    rep = lax.axis_index("rep").astype(jnp.int32)
    bit0, bit1, bit2 = rep & 1, (rep >> 1) & 1, (rep >> 2) & 1
    high = jnp.where(shard == 0, bit0, bit1)
    low = jnp.where(shard == 0, bit1, bit0)
    code = high * 4 + low * 2 + bit2
    dims = ((1, 2), (2, 1), (4, 4))
    lead = lax.broadcasted_iota(jnp.int32, (16,), 0)
    scal = jnp.where(lead == 0, shard, jnp.where(lead == 1, prefix[0], jnp.where(lead == 8, code, 0)))
    scal = lax.dynamic_update_slice(scal, latent_pos[0].astype(jnp.int32), (2,))

    pk_own = pack([ln1_gain, ln1_bias, b_qv, b_proj, ln2_gain, ln2_bias, b_fc, b_out])
    pk_oth = swap(pk_own)
    qkv_oth = swap(w_qkv)
    hid = hidden[0]
    dz = cotangent[0]
    lat = latents[0]

    send, normed, nrm_send, xb = ln_send(scal, hid, lat, pk_own, pk_oth, w_qkv, qkv_oth)
    recv = swap(send)
    keep = own_heads(scal, normed, pk_own, pk_oth, w_qkv, qkv_oth)
    proj_oth, fc_oth, out_oth, nrm_recv, dz_oth = [swap(gate(a, recv, keep)) for a in (w_proj, w_fc, w_out, nrm_send, dz)]
    att_keep, att_send, lse = attn_fwd(scal, keep, recv)
    att_recv = swap(att_send)
    dz_oth, nrm_recv, xb = gated((dz_oth, nrm_recv, xb))
    act_keep, act_send, gp, n2_keep, n2_send, block_out, dmid, gb, ga_keep, ga_send, sfc, sums = ffn(
        scal, att_keep, att_recv, xb, dz, pk_own, pk_oth, w_proj, proj_oth, w_fc, fc_oth, w_out, out_oth
    )
    act_recv = swap(act_send)
    ga_recv = swap(ga_send)
    gp_oth = swap(gate(gp, act_recv))
    n2_recv = swap(gate(n2_send, act_recv))
    gb_oth = swap(gate(gb, act_recv))
    s_out, k_out = grad_rows(scal, act_keep, act_recv, dz, dz_oth)
    r_out = Reduce(s_out, k_out, dims)
    s_fc, k_fc = grad_cols(scal, n2_keep, gate(n2_recv, k_out), gp, gp_oth)
    r_fc = Reduce(s_fc, k_fc, dims)
    d_own, d_oth = attn_bwd(scal, keep, recv, ga_keep, gate(ga_recv, k_fc), att_keep, att_send, lse, 0, H // 128)
    e_own, e_oth = swap(d_oth), swap(d_own)
    tok = r_out.hop2(d_own)
    tok = r_fc.hop2(tok)
    a_c, b_c, k_c = grad_attn(scal, normed, nrm_recv, att_keep, att_send, gb, gb_oth, d_own, d_oth, gate(e_own, tok), e_oth)
    r_c = Reduce(a_c, b_c, k_c, dims)
    tok = r_out.hop3(k_c)
    tok = r_out.hop4(tok)
    tok = r_fc.hop3(tok)
    gh, glat, s_keep, s_send = last_block(
        scal, (d_own, gate(e_own, tok)), xb, dmid, pk_own, pk_oth, w_qkv, qkv_oth, sfc, sums
    )
    s_recv = swap(s_send)
    glat_oth = swap(glat)
    tok = r_c.hop2(gh)
    tok = r_fc.hop4(tok)
    tok = r_c.hop3(tok)
    tok = r_out.hop5(tok)
    tok = r_c.hop4(tok)
    tok = r_fc.hop5(tok)
    small = s_keep + gate(s_recv, tok)
    glat = glat + gate(glat_oth, tok)
    for bits in ((1, 2), (2, 1)):
        small = small + hop(small, *bits)
    early = small
    small = small + hop(small, 4, 4)
    m = hop(small, 8, 8)
    r_c.hop5(tok)
    for i in (1, 2, 3):
        r_out.take(i)
    r_fc.take(1, r_out.pos[4], r_out.pos[5])
    r_fc.take(2, r_out.pos[6])
    r_fc.take(3, r_out.pos[7])
    r_c.take(1, r_fc.pos[4], r_fc.pos[5])
    g_out = final(scal, r_out.pos, pl.BlockSpec((H, D), lambda w, s: (w, 0)), sds((4 * H, D), F32))
    r_c.take(2, r_fc.pos[6], g_out, early)
    tok = r_c.take(3, r_fc.pos[7])
    g_fc = final(scal, gated(r_fc.pos, tok), pl.BlockSpec((H, D), lambda w, s: (0, w)), sds((H, 4 * D), F32))
    g_qkv, g_proj = final(
        scal, gated(r_c.pos, g_fc), [pl.BlockSpec((H, D), lambda w, s: (0, jnp.minimum(w, 2))), pl.BlockSpec((H, D), lambda w, s: (0, 0))],
        (sds((H, 3 * D), F32), sds((H, D), F32)), 3,
    )
    sizes = [v.shape[0] for v in (ln1_gain, ln1_bias, b_qv, b_proj, ln2_gain, ln2_bias, b_fc, b_out)]
    vecs = unpack(small, gate(m, tok), sizes)
    return (
        block_out[None], gh[None], glat[None, :6], vecs[0], vecs[1], g_qkv, vecs[2], g_proj, vecs[3],
        vecs[4], vecs[5], g_fc, vecs[6], g_out, vecs[7],
    )


def layer_norm(values, norm_gain, norm_shift):
    average = jnp.mean(values, axis=-1, keepdims=True)
    centered = values - average
    variance = jnp.mean(centered * centered, axis=-1, keepdims=True)
    return centered * lax.rsqrt(variance + norm_epsilon) * norm_gain + norm_shift


def gelu_tanh(values):
    return (
        0.5
        * values
        * (1.0 + jnp.tanh(gelu_root * (values + gelu_cubic * values * values * values)))
    )


def head_scores(query_one, key_one, query_pos, key_pos, prefix_one, score_scale):
    scores = (
        jnp.einsum("qhe,khe->hqk", query_one, key_one, preferred_element_type=jnp.float32)
        * score_scale
    )
    causal = (key_pos[None, :] <= query_pos[:, None])[None]
    in_prefix = (key_pos < prefix_one)[None, None, :]
    return jnp.where(causal | in_prefix, scores, masked_score)


def per_device(
    hidden,
    latents,
    latent_pos,
    prefix,
    ln1_gain,
    ln1_bias,
    w_qkv,
    b_qv,
    w_proj,
    b_proj,
    ln2_gain,
    ln2_bias,
    w_fc,
    b_fc,
    w_out,
    b_out,
    cotangent,
):
    seq_count, local_len, model_width = hidden.shape
    head_dim = model_width // HEADS
    score_scale = head_dim ** (-0.5)
    row_start = lax.axis_index("shard") * local_len
    gathered = (
        lax.all_gather(ln1_gain, "shard", axis=0, tiled=True),
        lax.all_gather(ln1_bias, "shard", axis=0, tiled=True),
        lax.all_gather(w_qkv, "shard", axis=0, tiled=True),
        lax.all_gather(b_qv, "shard", axis=0, tiled=True),
        lax.all_gather(w_proj, "shard", axis=0, tiled=True),
        lax.all_gather(b_proj, "shard", axis=0, tiled=True),
        lax.all_gather(ln2_gain, "shard", axis=0, tiled=True),
        lax.all_gather(ln2_bias, "shard", axis=0, tiled=True),
        lax.all_gather(w_fc, "shard", axis=0, tiled=True),
        lax.all_gather(b_fc, "shard", axis=0, tiled=True),
        lax.all_gather(w_out, "shard", axis=0, tiled=True),
        lax.all_gather(b_out, "shard", axis=0, tiled=True),
    )
    (
        full_ln1_gain,
        full_ln1_bias,
        full_qkv,
        full_b_qv,
        full_proj,
        full_b_proj,
        full_ln2_gain,
        full_ln2_bias,
        full_fc,
        full_b_fc,
        complete_output,
        full_b_out,
    ) = gathered
    row_ids = row_start + jnp.arange(local_len, dtype=jnp.int32)
    latent_matches = row_ids[None, :, None] == latent_pos[:, None, :]
    positioned_rows = jnp.einsum(
        "ety,eyw->etw",
        latent_matches.astype(jnp.bfloat16),
        latents,
        preferred_element_type=jnp.float32,
    )
    replaced = jnp.any(latent_matches, axis=-1)[..., None]
    block_in = jnp.where(replaced, positioned_rows, hidden.astype(jnp.float32)).reshape(
        -1, model_width
    )
    normed, back_norm_one = jax.vjp(
        layer_norm, block_in, full_ln1_gain.astype(jnp.float32), full_ln1_bias.astype(jnp.float32)
    )
    normed_low = normed.astype(jnp.bfloat16)
    bias_full = jnp.concatenate(
        [
            full_b_qv[:model_width].astype(jnp.float32),
            jnp.zeros((model_width,), jnp.float32),
            full_b_qv[model_width:].astype(jnp.float32),
        ]
    )
    projected = (
        jnp.dot(normed_low, full_qkv, preferred_element_type=jnp.float32) + bias_full
    ).astype(jnp.bfloat16)
    query_heads = projected[:, :model_width].reshape(seq_count, local_len, HEADS, head_dim)
    key_local = projected[:, model_width : 2 * model_width].reshape(
        seq_count, local_len, model_width
    )
    value_local = projected[:, 2 * model_width :].reshape(seq_count, local_len, model_width)
    key_full, value_full = (
        lax.all_gather(key_local, "shard", axis=1, tiled=True),
        lax.all_gather(value_local, "shard", axis=1, tiled=True),
    )
    full_len = key_full.shape[1]
    key_heads = key_full.reshape(seq_count, full_len, HEADS, head_dim)
    value_heads = value_full.reshape(seq_count, full_len, HEADS, head_dim)
    key_pos_all = jnp.arange(full_len, dtype=jnp.int32)

    def forward_seq(items):
        query_one, key_one, value_one, prefix_one = items
        scores = head_scores(query_one, key_one, row_ids, key_pos_all, prefix_one, score_scale)
        row_peak = jnp.max(scores, axis=-1, keepdims=True)
        single_logsumexp = row_peak + jnp.log(
            jnp.sum(jnp.exp(scores - row_peak), axis=-1, keepdims=True)
        )
        probs_low = jnp.exp(scores - single_logsumexp).astype(jnp.bfloat16)
        mixed = jnp.einsum("hqk,khe->qhe", probs_low, value_one, preferred_element_type=jnp.float32)
        return (mixed.astype(jnp.bfloat16), single_logsumexp)

    attended_heads, log_total = lax.map(forward_seq, (query_heads, key_heads, value_heads, prefix))
    attended = attended_heads.reshape(-1, model_width)
    middle = (
        block_in
        + jnp.dot(attended, full_proj, preferred_element_type=jnp.float32)
        + full_b_proj.astype(jnp.float32)
    )
    normed_two, back_norm_two = jax.vjp(
        layer_norm, middle, full_ln2_gain.astype(jnp.float32), full_ln2_bias.astype(jnp.float32)
    )
    normed_two_low = normed_two.astype(jnp.bfloat16)
    pre_act = jnp.dot(
        normed_two_low, full_fc, preferred_element_type=jnp.float32
    ) + full_b_fc.astype(jnp.float32)
    activated, back_gelu = jax.vjp(gelu_tanh, pre_act)
    activated_low = activated.astype(jnp.bfloat16)
    block_out = (
        middle
        + jnp.dot(activated_low, complete_output, preferred_element_type=jnp.float32)
        + full_b_out.astype(jnp.float32)
    )
    block_out = block_out.reshape(seq_count, local_len, model_width).astype(jnp.bfloat16)
    back_qkv, back_proj, back_fc, back_out = (
        lax.all_gather(w_qkv, "shard", axis=0, tiled=True),
        lax.all_gather(w_proj, "shard", axis=0, tiled=True),
        lax.all_gather(w_fc, "shard", axis=0, tiled=True),
        lax.all_gather(w_out, "shard", axis=0, tiled=True),
    )
    grad_top = cotangent.reshape(-1, model_width)
    grad_w_out = jnp.einsum(
        "nf,nd->fd", activated_low, grad_top, preferred_element_type=jnp.float32
    )
    grad_b_out = jnp.sum(grad_top.astype(jnp.float32), axis=0)
    grad_act = jnp.einsum("nd,fd->nf", grad_top, back_out, preferred_element_type=jnp.float32)
    (grad_pre,) = back_gelu(grad_act)
    grad_pre_low = grad_pre.astype(jnp.bfloat16)
    grad_w_fc = jnp.einsum(
        "nd,nf->df", normed_two_low, grad_pre_low, preferred_element_type=jnp.float32
    )
    grad_b_fc = jnp.sum(grad_pre_low.astype(jnp.float32), axis=0)
    grad_normed_two = jnp.einsum(
        "nf,df->nd", grad_pre_low, back_fc, preferred_element_type=jnp.float32
    )
    grad_mid_norm, grad_ln2_gain, grad_ln2_bias = back_norm_two(grad_normed_two)
    grad_mid = grad_top.astype(jnp.float32) + grad_mid_norm
    grad_branch_low = grad_mid.astype(jnp.bfloat16)
    grad_w_proj = jnp.einsum(
        "nd,ne->de", attended, grad_branch_low, preferred_element_type=jnp.float32
    )
    grad_b_proj = jnp.sum(grad_branch_low.astype(jnp.float32), axis=0)
    grad_att = jnp.einsum(
        "ne,de->nd", grad_branch_low, back_proj, preferred_element_type=jnp.float32
    )
    grad_att_low = grad_att.astype(jnp.bfloat16).reshape(seq_count, local_len, HEADS, head_dim)

    def backward_sequence(items):
        query_one, key_one, value_one, prefix_one, single_logsumexp, upstream = items
        scores = head_scores(query_one, key_one, row_ids, key_pos_all, prefix_one, score_scale)
        attn_probs = jnp.exp(scores - single_logsumexp)
        grad_value_one = jnp.einsum(
            "hqk,qhe->khe",
            attn_probs.astype(jnp.bfloat16),
            upstream,
            preferred_element_type=jnp.float32,
        )
        grad_probs = jnp.einsum(
            "qhe,khe->hqk", upstream, value_one, preferred_element_type=jnp.float32
        )
        delta_one = jnp.sum(grad_probs * attn_probs, axis=-1, keepdims=True)
        grad_scores = (attn_probs * (grad_probs - delta_one)).astype(jnp.bfloat16)
        grad_query_one = (
            jnp.einsum("hqk,khe->qhe", grad_scores, key_one, preferred_element_type=jnp.float32)
            * score_scale
        )
        grad_key_one = (
            jnp.einsum("hqk,qhe->khe", grad_scores, query_one, preferred_element_type=jnp.float32)
            * score_scale
        )
        return (
            grad_query_one,
            grad_key_one.reshape(full_len, model_width),
            grad_value_one.reshape(full_len, model_width),
        )

    grad_query, grad_key_all, grad_value_all = lax.map(
        backward_sequence, (query_heads, key_heads, value_heads, prefix, log_total, grad_att_low)
    )
    grad_key_own, grad_value_own = (
        lax.psum_scatter(
            grad_key_all.astype(jnp.bfloat16), "shard", scatter_dimension=1, tiled=True
        ).astype(jnp.float32),
        lax.psum_scatter(
            grad_value_all.astype(jnp.bfloat16), "shard", scatter_dimension=1, tiled=True
        ).astype(jnp.float32),
    )
    grad_query_low = grad_query.reshape(-1, model_width).astype(jnp.bfloat16)
    grad_key_low = grad_key_own.reshape(-1, model_width).astype(jnp.bfloat16)
    grad_value_low = grad_value_own.reshape(-1, model_width).astype(jnp.bfloat16)
    grad_projected = jnp.concatenate([grad_query_low, grad_key_low, grad_value_low], axis=1)
    grad_b_qv = jnp.concatenate(
        [
            jnp.sum(grad_query_low.astype(jnp.float32), axis=0),
            jnp.sum(grad_value_low.astype(jnp.float32), axis=0),
        ]
    )
    grad_w_qkv = jnp.einsum(
        "nd,ne->de", normed_low, grad_projected, preferred_element_type=jnp.float32
    )
    grad_normed = jnp.einsum(
        "ne,de->nd", grad_projected, back_qkv, preferred_element_type=jnp.float32
    )
    grad_in_norm, grad_ln1_gain, grad_ln1_bias = back_norm_one(grad_normed)
    block_gradient = (grad_mid + grad_in_norm).reshape(seq_count, local_len, model_width)
    latent_terms = jnp.einsum(
        "inv,inz->ivz",
        latent_matches.astype(jnp.float32),
        block_gradient,
        precision=lax.Precision.HIGHEST,
    )
    grad_latents = lax.psum(latent_terms, "shard")
    grad_hidden = jnp.where(replaced, 0.0, block_gradient).astype(jnp.bfloat16)
    shares = (
        lax.psum_scatter(
            grad_ln1_gain.astype(jnp.bfloat16), "shard", scatter_dimension=0, tiled=True
        ).astype(jnp.float32),
        lax.psum_scatter(
            grad_ln1_bias.astype(jnp.bfloat16), "shard", scatter_dimension=0, tiled=True
        ).astype(jnp.float32),
        lax.psum_scatter(
            grad_w_qkv.astype(jnp.bfloat16), "shard", scatter_dimension=0, tiled=True
        ).astype(jnp.float32),
        lax.psum_scatter(
            grad_b_qv.astype(jnp.bfloat16), "shard", scatter_dimension=0, tiled=True
        ).astype(jnp.float32),
        lax.psum_scatter(
            grad_w_proj.astype(jnp.bfloat16), "shard", scatter_dimension=0, tiled=True
        ).astype(jnp.float32),
        lax.psum_scatter(
            grad_b_proj.astype(jnp.bfloat16), "shard", scatter_dimension=0, tiled=True
        ).astype(jnp.float32),
        lax.psum_scatter(
            grad_ln2_gain.astype(jnp.bfloat16), "shard", scatter_dimension=0, tiled=True
        ).astype(jnp.float32),
        lax.psum_scatter(
            grad_ln2_bias.astype(jnp.bfloat16), "shard", scatter_dimension=0, tiled=True
        ).astype(jnp.float32),
        lax.psum_scatter(
            grad_w_fc.astype(jnp.bfloat16), "shard", scatter_dimension=0, tiled=True
        ).astype(jnp.float32),
        lax.psum_scatter(
            grad_b_fc.astype(jnp.bfloat16), "shard", scatter_dimension=0, tiled=True
        ).astype(jnp.float32),
        lax.psum_scatter(
            grad_w_out.astype(jnp.bfloat16), "shard", scatter_dimension=0, tiled=True
        ).astype(jnp.float32),
        lax.psum_scatter(
            grad_b_out.astype(jnp.bfloat16), "shard", scatter_dimension=0, tiled=True
        ).astype(jnp.float32),
    )
    summed = (
        lax.psum(shares[0].astype(jnp.bfloat16), "rep").astype(jnp.float32),
        lax.psum(shares[1].astype(jnp.bfloat16), "rep").astype(jnp.float32),
        lax.psum(shares[2].astype(jnp.bfloat16), "rep").astype(jnp.float32),
        lax.psum(shares[3].astype(jnp.bfloat16), "rep").astype(jnp.float32),
        lax.psum(shares[4].astype(jnp.bfloat16), "rep").astype(jnp.float32),
        lax.psum(shares[5].astype(jnp.bfloat16), "rep").astype(jnp.float32),
        lax.psum(shares[6].astype(jnp.bfloat16), "rep").astype(jnp.float32),
        lax.psum(shares[7].astype(jnp.bfloat16), "rep").astype(jnp.float32),
        lax.psum(shares[8].astype(jnp.bfloat16), "rep").astype(jnp.float32),
        lax.psum(shares[9].astype(jnp.bfloat16), "rep").astype(jnp.float32),
        lax.psum(shares[10].astype(jnp.bfloat16), "rep").astype(jnp.float32),
        lax.psum(shares[11].astype(jnp.bfloat16), "rep").astype(jnp.float32),
    )
    (
        total_ln1_gain,
        total_ln1_bias,
        total_w_qkv,
        total_b_qv,
        total_w_proj,
        total_b_proj,
        total_ln2_gain,
        total_ln2_bias,
        total_w_fc,
        total_b_fc,
        total_w_out,
        total_b_out,
    ) = summed
    return (
        block_out,
        grad_hidden,
        grad_latents,
        total_ln1_gain,
        total_ln1_bias,
        total_w_qkv,
        total_b_qv,
        total_w_proj,
        total_b_proj,
        total_ln2_gain,
        total_ln2_bias,
        total_w_fc,
        total_b_fc,
        total_w_out,
        total_b_out,
    )


def solution(mesh):
    sizes = dict(mesh.shape)
    paired = sizes["rep"] == 16 and sizes["shard"] == 2
    body = pair_device if paired else per_device
    in_specs = (
        P("rep", "shard", None),
        P("rep", None, None),
        P("rep", None),
        P("rep"),
        P("shard"),
        P("shard"),
        P("shard", None),
        P("shard"),
        P("shard", None),
        P("shard"),
        P("shard"),
        P("shard"),
        P("shard", None),
        P("shard"),
        P("shard", None),
        P("shard"),
        P("rep", "shard", None),
    )
    out_specs = (
        P("rep", "shard", None),
        P("rep", "shard", None),
        P("rep", None, None),
        P("shard"),
        P("shard"),
        P("shard", None),
        P("shard"),
        P("shard", None),
        P("shard"),
        P("shard"),
        P("shard"),
        P("shard", None),
        P("shard"),
        P("shard", None),
        P("shard"),
    )
    return jax.shard_map(
        body, mesh=mesh, in_specs=in_specs, out_specs=out_specs, check_vma=False
    )
```
